128 devices in a mesh: space: 32 (over y, x, core), tx: 4 (over z).
Axes of the slice: x: 4, y: 4, z: 4, core: 2. Of those that a mesh axis runs over, the one named last changes fastest.
Arguments:
- conductivity: float32 [64, 128, 256], P('space'), may hold values from 0.25 to 2
- chargeability: float32 [64, 128, 256], P('space'), may hold values from 0.05 to 0.6
- relaxation: float32 [64, 128, 256], P('space'), may hold values from 0.5 to 8
- start_potential: float32 [8, 64, 128, 256], P('tx', 'space'), may hold values from 0 to 2
- start_memory: float32 [4, 8, 64, 128, 256], P(None, 'tx', 'space'), may hold values from -6 to 6
- source_cells: int32 [2, 8], P(None, 'tx'), may hold values from 0 to 2097151
- dipole_cells: int32 [2, 4096], replicated, may hold values from 0 to 2097151
- live_counts: int32 [32], replicated, may hold values from 32 to 128, as said below
- observed: float32 [3, 8, 4096], P(None, 'tx', 'space'), may hold values from -4 to 4
Outputs:
- voltages: float32 [3, 8, 4096], P(None, 'tx', 'space')
- misfit: float32 [], replicated
- grad_chargeability: float32 [64, 128, 256], P('space', 'tx')
- grad_relaxation: float32 [64, 128, 256], P('space', 'tx')
The draws below stay inside these ranges and needn't reach their ends.
Inputs may be any that keep to these rules, and one draw needn't show every extreme that they name: `source_cells`: flat cell indices of the grid. `dipole_cells`: flat cell indices of the grid. `live_counts`: some slab has all 128 slots live.
All inputs are finite; a program needn't handle non-finite values.
Results may differ from the reference program's by a relative error of at most 0.00002.
Values sent between devices are 32-bit elements; how exact they have to be, the bound alone decides.
A program may use at most 192 MiB of HBM per device.

```python
import math
import jax
import jax.numpy as jnp
from jax import lax

NY = 128
NZ = 256
REC_DEV = 128
NSTEPS = 3
JACOBI = 8
NMEM = 4
NX = 64
NTX = 8
NDIP = 4096
NTILE = 32


def draw_live_counts(key, part):
    first_key, second_key = jax.random.split(key)
    base = jax.random.randint(first_key, (NTILE,), REC_DEV // 4, REC_DEV + 1)
    chosen = jax.random.randint(second_key, (), 0, NTILE)
    return jnp.where(jnp.arange(NTILE) == chosen, REC_DEV, base).astype(jnp.int32)


def touch_ends(values, rng, least, top_value):
    longest = values.shape.index(max(values.shape))
    spots = []
    for shift in (0, 1):
        where = [jax.random.randint(jax.random.fold_in(rng, axis), (), 0, length) for axis, length in enumerate(values.shape)]
        where[longest] = (where[longest] + shift) % values.shape[longest]
        spots.append(tuple(where))
    return values.at[spots[0]].set(least).at[spots[1]].set(top_value)


def level_of(own_key, shape, shards, low, high):
    loudness = 1.0
    for dim, shards_of in shards:
        draws = jax.random.uniform(jax.random.fold_in(jax.random.fold_in(own_key, 6), dim), (shards_of,), jnp.float32, low / len(shards), high / len(shards))
        loudness = loudness * jnp.repeat(jnp.exp(draws), shape[dim] // shards_of).reshape((-1,) + (1,) * (len(shape) - 1 - dim))
    return loudness


def gaussian(key, dims, spread, most, cuts=(), kind=jnp.bfloat16):
    gain = level_of(key, dims, cuts, -0.22, 0.18) if cuts else 1.0
    values = jax.random.normal(key, dims, jnp.float32) * spread * gain
    return jnp.minimum(jnp.maximum(values, -most), most).astype(kind)


def setup_inputs(seed: int = 0) -> dict:
    splits = jax.random.split(jax.random.key(seed), 10)
    conductivity = jnp.clip(0.25 + 1.75 * jax.random.uniform(splits[0], (NX, NY, NZ), jnp.float32) ** level_of(splits[0], (NX, NY, NZ), ((0, 32),), -0.2, 0.2), 0.25, 2.0)
    chargeability = jnp.clip(0.05 + 0.55 * jax.random.uniform(splits[1], (NX, NY, NZ), jnp.float32) ** level_of(splits[1], (NX, NY, NZ), ((0, 32),), -0.2, 0.2), 0.05, 0.6)
    relaxation = jnp.clip(jnp.exp(math.log(8.0) - 2.7725887 * jax.random.uniform(splits[2], (NX, NY, NZ), jnp.float32) ** level_of(splits[2], (NX, NY, NZ), ((0, 32),), -0.2, 0.2)), 0.5, 8.0)
    start_potential = jnp.clip(2.0 * jax.random.uniform(splits[3], (NTX, NX, NY, NZ), jnp.float32) ** level_of(splits[3], (NTX, NX, NY, NZ), ((0, 4), (1, 32)), -0.2, 0.2), 0.0, 2.0)
    start_memory = gaussian(splits[4], (NMEM, NTX, NX, NY, NZ), 1.0, 6.0, ((1, 4), (2, 32)), jnp.float32)
    source_cells = touch_ends(jax.random.randint(splits[5], (2, NTX), 0, NX * NY * NZ), jax.random.fold_in(splits[5], 1), 0, (NX * NY * NZ) - 1).astype(jnp.int32)
    dipole_cells = touch_ends(jax.random.randint(splits[6], (2, NDIP), 0, NX * NY * NZ), jax.random.fold_in(splits[6], 1), 0, (NX * NY * NZ) - 1).astype(jnp.int32)
    live_counts = draw_live_counts(jax.random.fold_in(splits[9], 71), 0)
    observed = gaussian(splits[8], (NSTEPS, NTX, NDIP), 0.3, 4.0, ((1, 4), (2, 32)), jnp.float32)
    return {"conductivity": conductivity, "chargeability": chargeability, "relaxation": relaxation, "start_potential": start_potential, "start_memory": start_memory, "source_cells": source_cells, "dipole_cells": dipole_cells, "live_counts": live_counts, "observed": observed}


mode_weights = (0.4, 0.3, 0.2, 0.1)
mode_ratios = (0.25, 1.0, 4.0, 16.0)
strength = 4.0

def neighbours(field):
    padded = jnp.pad(field, 1)
    total = padded[2:, 1:-1, 1:-1] + padded[:-2, 1:-1, 1:-1]
    total = total + padded[1:-1, 2:, 1:-1] + padded[1:-1, :-2, 1:-1]
    return total + padded[1:-1, 1:-1, 2:] + padded[1:-1, 1:-1, :-2]

def forward_one(conductivity, chargeability, relaxation, potential, memory, pair, dipole_cells, live):
    inverse = 1.0 / (6.0 + conductivity)
    source = jnp.zeros((NX * NY * NZ,), jnp.float32).at[pair[0]].add(strength).at[pair[1]].add(-strength)
    source = source.reshape((NX, NY, NZ))
    decays = [jnp.exp(-1.0 / (relaxation * ratio)) for ratio in mode_ratios]
    couple = [chargeability * mode_weights[level] * (1.0 - decays[level]) for level in range(4)]
    fields = [memory[level] for level in range(4)]
    result = []
    for step in range(NSTEPS):
        stored = fields[0] + fields[1] + fields[2] + fields[3]
        if step == 0:
            rhs = source + conductivity * stored
        else:
            rhs = conductivity * stored
        for sweep in range(JACOBI):
            potential = (rhs + neighbours(potential)) * inverse
        fields = [decays[level] * fields[level] + couple[level] * potential for level in range(4)]
        flat = potential.reshape(-1)
        result.append(live * (flat[dipole_cells[0]] - flat[dipole_cells[1]]))
    return jnp.stack(result)

def reference(conductivity, chargeability, relaxation, start_potential, start_memory, source_cells, dipole_cells, live_counts, observed):
    dipole_ids = jnp.arange(NDIP, dtype=jnp.int32)
    live = (dipole_ids % REC_DEV < live_counts[dipole_ids // REC_DEV]).astype(jnp.float32)

    def forward_of(index):
        return forward_one(conductivity, chargeability, relaxation, start_potential[index], start_memory[:, index], source_cells[:, index], dipole_cells, live)
    volts = jnp.transpose(lax.map(forward_of, jnp.arange(NTX, dtype=jnp.int32)), (1, 0, 2))
    resid = live * (volts - observed)
    misfit = jnp.sqrt(1.0 + jnp.sum(resid * resid))

    def gradient_step(carry, index):

        def volts_of(charge_field, relax_field):
            return forward_one(conductivity, charge_field, relax_field, start_potential[index], start_memory[:, index], source_cells[:, index], dipole_cells, live)
        unused, pull = jax.vjp(volts_of, chargeability, relaxation)
        grad_c, grad_t = pull(resid[:, index] / misfit)
        return ((carry[0] + grad_c, carry[1] + grad_t), None)
    zero_field = jnp.zeros((NX, NY, NZ), jnp.float32)
    (grad_c, grad_t), unused = lax.scan(gradient_step, (zero_field, zero_field), jnp.arange(NTX, dtype=jnp.int32))
    return (volts, misfit, grad_c, grad_t)
```

```python
import functools

import jax
import jax.numpy as jnp
from jax import lax
from jax.experimental import pallas as pl
from jax.experimental.pallas import tpu as pltpu
from jax.sharding import PartitionSpec as P

MESH = pl.DeviceIdType.MESH
F32 = jnp.float32
BF16 = jnp.bfloat16
NSTEPS = 3
JACOBI = 8
WEIGHTS = (0.4, 0.3, 0.2, 0.1)
RATIOS = (0.25, 1.0, 4.0, 16.0)
STRENGTH = 4.0

GY, GX = 4, 4
SLOTS = 2 * GX
BX, BY, LANES = 16, 32, 128
TOP = 8
NDIP = 4096
CHUNK = 512
ROWS = BX * BY
U0, R0, R1, R2, T1, T2 = range(6)
COND, CHG, RLX = range(3)


def remote(src, dst, send, recv, device):
    return pltpu.make_async_remote_copy(
        src_ref=src, dst_ref=dst, send_sem=send, recv_sem=recv, device_id=device, device_id_type=MESH
    )


def kernel(
    cond, chg, rlx, start, mem, src_cells, dip, counts, obs,
    volts_out, misfit_out, gc_out, gt_out,
    stage, sstage, blk, sblk, v, ysend, yrecv,
    inv, rhs, f1, f2, ka0, ka1, kb0, kb1, un, adj, back,
    ut, acc, part, prx, pry, res, obs_all, live, vswap, sq, sqc, sqz,
    grad, rc, red, rx, rz,
    fsend, frecv, ssend, srecv, hsend, hrecv, osend, orecv, psend, precv, qsend, qrecv, gsend, grecv,
):
    space = lax.axis_index("space")
    tx = lax.axis_index("tx")
    gy = space // SLOTS
    slot = lax.rem(space, SLOTS)
    gx = slot // 2
    core = lax.rem(slot, 2)
    base = gy * SLOTS
    partner = base + gx * 2 + 1 - core

    def peer_slot(p):
        return lax.rem(slot + p, SLOTS)

    def pieces(body):
        def at(i, carry):
            row, layer = i // 2, lax.rem(i, 2)
            for half in range(2):
                body(row, layer, half, (layer, pl.ds(pl.multiple_of(row * BY, BY), BY), pl.ds(half * LANES, LANES)))
            return carry

        lax.fori_loop(0, 2 * GX, at, 0)

    def first_fields(row, layer, half, where):
        c = cond[where]
        sstage[COND, row, half, layer] = c
        ids = (2 * space + layer) * (128 * 256) + row * (BY * 256) + half * LANES
        ids = ids + lax.broadcasted_iota(jnp.int32, (BY, LANES), 0) * 256
        ids = ids + lax.broadcasted_iota(jnp.int32, (BY, LANES), 1)
        for t in range(2):
            stage[U0, t, row, half, layer] = start[(t,) + where]
            total = mem[(0, t) + where] + mem[(1, t) + where] + mem[(2, t) + where] + mem[(3, t) + where]
            source = jnp.where(ids == src_cells[0, t], STRENGTH, 0.0) - jnp.where(ids == src_cells[1, t], STRENGTH, 0.0)
            stage[R0, t, row, half, layer] = source + c * total

    def later_fields(row, layer, half, where):
        c = cond[where]
        relax = rlx[where]
        sstage[CHG, row, half, layer] = chg[where]
        sstage[RLX, row, half, layer] = relax
        rate = 1.0 / relax
        decays = [jnp.exp(-rate / ratio) for ratio in RATIOS]
        for t in range(2):
            first, second, slope, slope_d = (jnp.zeros((BY, LANES), F32) for _ in range(4))
            for k in range(4):
                scaled = decays[k] * mem[(k, t) + where]
                first = first + scaled
                second = second + decays[k] * scaled
                tilt = scaled * (1.0 / RATIOS[k])
                slope = slope + tilt
                slope_d = slope_d + decays[k] * tilt
            stage[R1, t, row, half, layer] = c * first
            stage[R2, t, row, half, layer] = c * second
            stage[T1, t, row, half, layer] = c * rate * rate * slope
            stage[T2, t, row, half, layer] = 2.0 * c * rate * rate * slope_d

    def field_copy(f, p):
        to = peer_slot(p)
        return remote(
            stage.at[f, lax.rem(to, 2), to // 2], blk.at[f, :, pl.ds(2 * slot, 2)],
            fsend.at[f, to], frecv.at[f, slot], {"space": base + to},
        )

    def static_copy(f, p):
        to = peer_slot(p)
        return remote(
            sstage.at[f, to // 2], sblk.at[f, :, pl.ds(2 * slot, 2)],
            ssend.at[f, to], srecv.at[f, slot], {"space": base + to},
        )

    def over_peers(body):
        def at(p, carry):
            body(p)
            return carry

        lax.fori_loop(1, SLOTS, at, 0)

    def send_field(f):
        over_peers(lambda p: field_copy(f, p).start())
        blk[f, :, pl.ds(2 * slot, 2)] = stage[f, core, gx]

    def send_static(f):
        over_peers(lambda p: static_copy(f, p).start())
        sblk[f, :, pl.ds(2 * slot, 2)] = sstage[f, gx]

    def take_field(f):
        def one(p):
            of = peer_slot(p)
            here = blk.at[f, :, pl.ds(2 * of, 2)]
            remote(here, here, fsend.at[f, of], frecv.at[f, of], {"space": base + of}).wait_recv()

        over_peers(one)

    def take_static(f):
        def one(p):
            of = peer_slot(p)
            here = sblk.at[f, :, pl.ds(2 * of, 2)]
            remote(here, here, ssend.at[f, of], srecv.at[f, of], {"space": base + of}).wait_recv()

        over_peers(one)

    pieces(first_fields)
    send_field(U0)
    send_static(COND)
    send_field(R0)
    pieces(later_fields)
    send_static(CHG)
    send_static(RLX)
    for f in (R1, R2, T1, T2):
        send_field(f)

    def obs_copy(p):
        to = peer_slot(p)
        return remote(
            vswap.at[pl.ds(3 * lax.rem(to, 2), 3)], obs_all.at[:, :, pl.ds(pl.multiple_of(space * LANES, LANES), LANES)],
            osend.at[to], orecv.at[slot], {"space": base + to},
        )

    for t in range(2):
        for n in range(NSTEPS):
            vswap[3 * t + n] = obs[n, t : t + 1, :]
    over_peers(lambda p: obs_copy(p).start())
    obs_all[:, :, pl.ds(pl.multiple_of(space * LANES, LANES), LANES)] = vswap[pl.ds(3 * core, 3)]

    def obs_wait(p):
        of = peer_slot(p)
        here = obs_all.at[:, :, pl.ds(pl.multiple_of((base + of) * LANES, LANES), LANES)]
        remote(here, here, osend.at[of], orecv.at[of], {"space": base + of}).wait_recv()

    def column_copy(p):
        to = lax.rem(gy + p, GY)
        here = obs_all.at[:, :, pl.ds(pl.multiple_of(base * LANES, SLOTS * LANES), SLOTS * LANES)]
        return remote(here, here, qsend.at[to], qrecv.at[gy], {"space": to * SLOTS + slot})

    def column_wait(p):
        of = lax.rem(gy + p, GY)
        here = obs_all.at[:, :, pl.ds(pl.multiple_of(of * SLOTS * LANES, SLOTS * LANES), SLOTS * LANES)]
        remote(here, here, qsend.at[of], qrecv.at[of], {"space": of * SLOTS + slot}).wait_recv()

    def over_four(body):
        def at(p, carry):
            body(p)
            return carry

        lax.fori_loop(1, 4, at, 0)

    lane_ids = lax.broadcasted_iota(jnp.int32, (1, LANES), 1)

    def live_at(j, carry):
        live[:, pl.ds(pl.multiple_of(j * LANES, LANES), LANES)] = jnp.where(lane_ids < counts[j], 1.0, 0.0)
        return carry

    lax.fori_loop(0, GY * SLOTS, live_at, 0)

    core_rows = pl.ds(TOP, BY)

    def edge_layer(x):
        v[:, :, x, core_rows] = jnp.zeros((2, 2, BY, LANES), F32)

    def edge_rows(side):
        yrecv[:, side] = jnp.zeros((2, 2, BX, LANES), F32)

    pl.when(gy == 0)(lambda: edge_layer(0))
    pl.when(gy == GY - 1)(lambda: edge_layer(BX + 1))
    pl.when(gx == 0)(lambda: edge_rows(0))
    pl.when(gx == GX - 1)(lambda: edge_rows(1))

    def halo(at):
        up = {"space": space - SLOTS}
        down = {"space": space + SLOTS}
        left = {"space": space - 2}
        right = {"space": space + 2}
        return (
            (gy > 0, gy < GY - 1,
             remote(v.at[at, :, 1, core_rows], v.at[at, :, BX + 1, core_rows], hsend.at[at, 0], hrecv.at[at, 0], up)),
            (gy < GY - 1, gy > 0,
             remote(v.at[at, :, BX, core_rows], v.at[at, :, 0, core_rows], hsend.at[at, 1], hrecv.at[at, 1], down)),
            (gx > 0, gx < GX - 1,
             remote(ysend.at[at, 0], yrecv.at[at, 1], hsend.at[at, 2], hrecv.at[at, 2], left)),
            (gx < GX - 1, gx > 0,
             remote(ysend.at[at, 1], yrecv.at[at, 0], hsend.at[at, 3], hrecv.at[at, 3], right)),
        )

    def exchange(at):
        copies = halo(at)
        for sends, _, copy in copies:
            pl.when(sends)(copy.start)
        for sends, takes, copy in copies:
            pl.when(takes)(copy.wait_recv)
            pl.when(sends)(copy.wait_send)

    def put(at, half, x, value):
        v[at, half, x + 1, TOP : TOP + BY, :] = value
        ysend[at, 0, half, pl.ds(x, 1), :] = value[0:1]
        ysend[at, 1, half, pl.ds(x, 1), :] = value[BY - 1 : BY]

    lane = lax.broadcasted_iota(jnp.int32, (BY, LANES), 1)

    def over_x(body, unroll=1):
        def at(x, carry):
            body(x)
            return carry

        lax.fori_loop(0, BX, at, 0, unroll=unroll)

    def neighbour_sums(at, x):
        c0 = v[at, 0, x + 1, TOP : TOP + BY, :]
        c1 = v[at, 1, x + 1, TOP : TOP + BY, :]
        next0, next1 = pltpu.roll(c0, LANES - 1, 1), pltpu.roll(c1, LANES - 1, 1)
        last0, last1 = pltpu.roll(c0, 1, 1), pltpu.roll(c1, 1, 1)
        z0 = jnp.where(lane == LANES - 1, next1, next0) + jnp.where(lane == 0, 0.0, last0)
        z1 = jnp.where(lane == LANES - 1, 0.0, next1) + jnp.where(lane == 0, last0, last1)
        sums = []
        for half, z in ((0, z0), (1, z1)):
            total = v[at, half, x + 2, TOP : TOP + BY, :] + v[at, half, x, TOP : TOP + BY, :]
            total = total + v[at, half, x + 1, TOP + 1 : TOP + BY + 1, :] + v[at, half, x + 1, TOP - 1 : TOP + BY - 1, :]
            sums.append(total + z)
        return sums

    def spread_rows(at):
        def body(x):
            for half in range(2):
                v[at, half, x + 1, TOP - 1 : TOP, :] = yrecv[at, 0, half, pl.ds(x, 1), :]
                v[at, half, x + 1, TOP + BY : TOP + BY + 1, :] = yrecv[at, 1, half, pl.ds(x, 1), :]

        over_x(body, unroll=4)

    def locate(sign, k):
        cells = dip[sign : sign + 1, pl.ds(pl.multiple_of(k * CHUNK, CHUNK), CHUNK)]
        x, y, z = cells >> 15, (cells >> 8) & 127, cells & 255
        own = ((x >> 4) == gy) & ((y >> 5) == gx)
        row = jnp.where(own, (x & 15) * BY + (y & 31), -1)
        hot = lax.broadcasted_iota(jnp.int32, (ROWS, CHUNK), 0) == row
        return jnp.where(hot, 1.0, 0.0).astype(BF16), lax.broadcasted_iota(jnp.int32, (2 * LANES, CHUNK), 0) == z

    def gather(n):
        for half in range(2):
            rows = un[n, half].reshape(ROWS, LANES).T
            high = rows.astype(BF16)
            ut[half * LANES : (half + 1) * LANES, :] = high
            ut[(2 + half) * LANES : (3 + half) * LANES, :] = (rows - high.astype(F32)).astype(BF16)

        def at(k, carry):
            found = []
            for sign in range(2):
                hot, depth = locate(sign, k)
                both = jnp.dot(ut[...], hot, preferred_element_type=F32)
                value = both[: 2 * LANES] + both[2 * LANES :]
                found.append(jnp.sum(jnp.where(depth, value, 0.0), axis=0, keepdims=True))
            part[n, :, pl.ds(pl.multiple_of(k * CHUNK, CHUNK), CHUNK)] = found[0] - found[1]
            return carry

        lax.fori_loop(0, NDIP // CHUNK, at, 0)

    def scatter(n):
        acc[...] = jnp.zeros_like(acc)

        def at(k, carry):
            value = res[n, :, pl.ds(pl.multiple_of(k * CHUNK, CHUNK), CHUNK)]
            for sign in range(2):
                hot, depth = locate(sign, k)
                placed = jnp.where(depth, value if sign == 0 else -value, 0.0)
                high = placed.astype(BF16)
                low = (placed - high.astype(F32)).astype(BF16)
                acc[...] += lax.dot_general(
                    hot, jnp.concatenate([high, low], axis=0), (((1,), (1,)), ((), ())), preferred_element_type=F32
                )
            return carry

        lax.fori_loop(0, NDIP // CHUNK, at, 0)

    def injected(half, x):
        rows = pl.ds(pl.multiple_of(x * BY, BY), BY)
        return (
            acc[rows, half * LANES : (half + 1) * LANES] + acc[rows, (2 + half) * LANES : (3 + half) * LANES]
        )

    take_field(U0)

    def begin(x):
        for half in range(2):
            put(0, half, x, blk[U0, half, x])

    over_x(begin)
    take_static(COND)
    take_field(R0)

    def step_zero(x):
        for half in range(2):
            inv[half, x] = 1.0 / (6.0 + sblk[COND, half, x])
            rhs[half, x] = blk[R0, half, x]

    over_x(step_zero)

    def forward_sweep(s, carry):
        at = lax.rem(s, 2)
        exchange(at)
        spread_rows(at)

        def body(x):
            sums = neighbour_sums(at, x)
            for half in range(2):
                put(1 - at, half, x, (rhs[half, x] + sums[half]) * inv[half, x])

        over_x(body, unroll=2)
        return carry

    def keep(n):
        def body(x):
            for half in range(2):
                un[n, half, x] = v[0, half, x + 1, TOP : TOP + BY, :]

        over_x(body)

    def statics(x):
        for half in range(2):
            c, g = sblk[COND, half, x], sblk[CHG, half, x]
            rate = 1.0 / sblk[RLX, half, x]
            a0, a1, e1, b0, b1 = (jnp.zeros((BY, LANES), F32) for _ in range(5))
            for k in range(4):
                decay = jnp.exp(-rate / RATIOS[k])
                fresh = WEIGHTS[k] * (1.0 - decay)
                a0 = a0 + fresh
                a1 = a1 + fresh * decay
                tilt = decay * (WEIGHTS[k] / RATIOS[k])
                b0 = b0 + tilt
                b1 = b1 + tilt * (1.0 - 2.0 * decay)
            f1[half, x] = c * g * a0
            f2[half, x] = c * g * a1
            ka0[half, x] = c * a0
            ka1[half, x] = c * a1
            kb0[half, x] = c * g * rate * rate * b0
            kb1[half, x] = c * g * rate * rate * b1

    for n in range(NSTEPS):
        lax.fori_loop(0, JACOBI, forward_sweep, 0)
        keep(n)
        if n == 0:
            take_static(CHG)
            take_static(RLX)
            over_x(statics)
            take_field(R1)

            def step_one(x):
                for half in range(2):
                    rhs[half, x] = blk[R1, half, x] + f1[half, x] * un[0, half, x]

            over_x(step_one)
            over_peers(obs_wait)
            over_four(lambda p: column_copy(p).start())
        if n == 1:
            take_field(R2)

            def step_two(x):
                for half in range(2):
                    rhs[half, x] = (
                        blk[R2, half, x] + f2[half, x] * un[0, half, x] + f1[half, x] * un[1, half, x]
                    )

            over_x(step_two)
            over_four(column_wait)
        gather(n)

    def row_copy(p):
        to = lax.rem(gx + p, GX)
        return remote(part, prx.at[gx], psend.at[0, to], precv.at[0, gx], {"space": base + 2 * to + core})

    def row_wait(p):
        of = lax.rem(gx + p, GX)
        remote(part, prx.at[of], psend.at[0, of], precv.at[0, of], {"space": base + 2 * of + core}).wait_recv()

    over_four(lambda p: row_copy(p).start())
    prx[gx] = part[...]
    over_four(row_wait)
    res[...] = (prx[0] + prx[1]) + (prx[2] + prx[3])

    def col_copy(p):
        to = lax.rem(gy + p, GY)
        return remote(res, pry.at[gy], psend.at[1, to], precv.at[1, gy], {"space": to * SLOTS + slot})

    def col_wait(p):
        of = lax.rem(gy + p, GY)
        remote(res, pry.at[of], psend.at[1, of], precv.at[1, of], {"space": of * SLOTS + slot}).wait_recv()

    over_four(lambda p: col_copy(p).start())
    pry[gy] = res[...]
    over_four(col_wait)
    over_four(lambda p: col_copy(p).wait_send())
    squares = jnp.zeros((1, NDIP), F32)
    for n in range(NSTEPS):
        volts = live[...] * ((pry[0, n] + pry[1, n]) + (pry[2, n] + pry[3, n]))
        part_resid = live[...] * (volts - obs_all[n])
        pry[0, n] = volts
        res[n] = part_resid
        squares = squares + part_resid * part_resid

    own = pl.ds(pl.multiple_of(space * LANES, LANES), LANES)
    other = pl.ds(pl.multiple_of(partner * LANES, LANES), LANES)
    swap = remote(pry.at[0, :, :, other], vswap.at[pl.ds(6, 3)], qsend.at[4], qrecv.at[4], {"space": partner})
    swap.start()
    lanes = squares[:, 0:LANES]
    for j in range(1, NDIP // LANES):
        lanes = lanes + squares[:, j * LANES : (j + 1) * LANES]
    sq[...] = lanes
    pair = remote(sq, sqc, qsend.at[5], qrecv.at[5], {"space": partner})
    pair.start()
    for n in range(NSTEPS):
        volts_out[n, pl.ds(core, 1), :] = pry[0, n, :, own]
    swap.wait()
    for n in range(NSTEPS):
        volts_out[n, pl.ds(1 - core, 1), :] = vswap[6 + n]
    pair.wait()
    sqz[tx] = sq[...] + sqc[...]

    def sq_copy(p):
        to = lax.rem(tx + p, 4)
        return remote(sqz.at[tx], sqz.at[tx], gsend.at[3, to], grecv.at[3, tx], {"tx": to})

    def sq_wait(p):
        of = lax.rem(tx + p, 4)
        remote(sqz.at[of], sqz.at[of], gsend.at[3, of], grecv.at[3, of], {"tx": of}).wait_recv()

    over_four(lambda p: sq_copy(p).start())

    def begin_adjoint(n):
        def body(x):
            for half in range(2):
                field = injected(half, x)
                if n == 1:
                    field = field + back[half, x] + f1[half, x] * adj[2, half, x]
                scaled = field * inv[half, x]
                adj[n, half, x] = scaled
                put(0, half, x, scaled)

        over_x(body)

    def adjoint_sweep(n, s, carry):
        at = lax.rem(s, 2)
        exchange(at)
        spread_rows(at)

        def body(x):
            sums = neighbour_sums(at, x)
            for half in range(2):
                scaled = sums[half] * inv[half, x]
                adj[n, half, x] += scaled
                put(1 - at, half, x, scaled)

        over_x(body, unroll=2)
        return carry

    scatter(2)
    begin_adjoint(2)
    lax.fori_loop(0, JACOBI - 1, functools.partial(adjoint_sweep, 2), 0)
    exchange((JACOBI - 1) % 2)
    spread_rows((JACOBI - 1) % 2)

    def last_back(x):
        sums = neighbour_sums((JACOBI - 1) % 2, x)
        for half in range(2):
            back[half, x] = sums[half]

    over_x(last_back)
    scatter(1)
    begin_adjoint(1)
    lax.fori_loop(0, JACOBI - 1, functools.partial(adjoint_sweep, 1), 0)

    over_four(sq_wait)
    total = (sqz[0] + sqz[1]) + (sqz[2] + sqz[3])
    misfit = jnp.sqrt(1.0 + jnp.sum(total, axis=1, keepdims=True))
    misfit_out[...] = misfit
    take_field(T1)
    take_field(T2)

    def gradients(i, carry):
        x = i
        row, rest = x // 4, lax.rem(x, 4)
        side, layer = rest // 2, lax.rem(rest, 2)
        for half in range(2):
            s1, s2 = adj[1, half, x], adj[2, half, x]
            u0, u1 = un[0, half, x], un[1, half, x]
            same = s2 * u1 + s1 * u0
            cross = s2 * u0
            grad[0, row, side, half, layer] = ka0[half, x] * same + ka1[half, x] * cross
            grad[1, row, side, half, layer] = (
                s1 * blk[T1, half, x] + s2 * blk[T2, half, x] - kb0[half, x] * same + kb1[half, x] * cross
            )
        return carry

    lax.fori_loop(0, BX, gradients, 0)
    across = remote(grad.at[:, :, 1 - core], rc, gsend.at[2, 0], grecv.at[2, 0], {"space": partner})
    across.start()
    across.wait()

    def sum_cores(i, carry):
        f, row = i // 4, lax.rem(i, 4)
        red[f, row] = grad[f, row, core] + rc[f, row]
        return carry

    lax.fori_loop(0, 8, sum_cores, 0)

    def back_copy(p):
        to = lax.rem(gx + p, GX)
        return remote(red.at[:, to], rx.at[:, gx], gsend.at[0, to], grecv.at[0, gx], {"space": base + 2 * to + core})

    def back_wait(p):
        of = lax.rem(gx + p, GX)
        remote(red.at[:, of], rx.at[:, of], gsend.at[0, of], grecv.at[0, of], {"space": base + 2 * of + core}).wait_recv()

    over_four(lambda p: back_copy(p).start())
    for f in range(2):
        rx[f, gx] = red[f, gx]
    over_four(back_wait)

    def tx_copy(p):
        to = lax.rem(tx + p, 4)
        return remote(rx.at[:, to], rz.at[:, tx], gsend.at[1, to], grecv.at[1, tx], {"tx": to})

    def tx_wait(p):
        of = lax.rem(tx + p, 4)
        remote(rx.at[:, of], rz.at[:, of], gsend.at[1, of], grecv.at[1, of], {"tx": of}).wait_recv()

    over_four(lambda p: tx_copy(p).start())
    for f in range(2):
        rz[f, tx] = rx[f, tx]
    over_four(tx_wait)
    scale = 1.0 / misfit
    for f, out in ((0, gc_out), (1, gt_out)):
        for half in range(2):
            value = (rz[f, 0, half] + rz[f, 1, half]) + (rz[f, 2, half] + rz[f, 3, half])
            out[:, :, half * LANES : (half + 1) * LANES] = value * scale.reshape(1, 1, 1)

    for f in range(6):
        over_peers(lambda p: field_copy(f, p).wait_send())
    for f in range(3):
        over_peers(lambda p: static_copy(f, p).wait_send())
    over_peers(lambda p: obs_copy(p).wait_send())
    over_four(lambda p: column_copy(p).wait_send())
    over_four(lambda p: row_copy(p).wait_send())
    over_four(lambda p: sq_copy(p).wait_send())
    over_four(lambda p: back_copy(p).wait_send())
    over_four(lambda p: tx_copy(p).wait_send())


def on_device(cond, chg, rlx, start, mem, src_cells, dip, counts, obs):
    vmem = pl.BlockSpec(memory_space=pltpu.VMEM)
    smem = pl.BlockSpec(memory_space=pltpu.SMEM)
    field = pltpu.VMEM((2, BX, BY, LANES), F32)
    dma = pltpu.SemaphoreType.DMA
    scratch = [
        pltpu.VMEM((6, 2, GX, 2, 2, BY, LANES), F32),
        pltpu.VMEM((3, GX, 2, 2, BY, LANES), F32),
        pltpu.VMEM((6, 2, BX, BY, LANES), F32),
        pltpu.VMEM((3, 2, BX, BY, LANES), F32),
        pltpu.VMEM((2, 2, BX + 2, BY + 2 * TOP, LANES), F32),
        pltpu.VMEM((2, 2, 2, BX, LANES), F32),
        pltpu.VMEM((2, 2, 2, BX, LANES), F32),
        field, field, field, field, field, field, field, field,
        pltpu.VMEM((NSTEPS, 2, BX, BY, LANES), F32),
        pltpu.VMEM((NSTEPS, 2, BX, BY, LANES), F32),
        field,
        pltpu.VMEM((4 * LANES, ROWS), BF16),
        pltpu.VMEM((ROWS, 4 * LANES), F32),
        pltpu.VMEM((NSTEPS, 1, NDIP), F32),
        pltpu.VMEM((GX, NSTEPS, 1, NDIP), F32),
        pltpu.VMEM((GY, NSTEPS, 1, NDIP), F32),
        pltpu.VMEM((NSTEPS, 1, NDIP), F32),
        pltpu.VMEM((NSTEPS, 1, NDIP), F32),
        pltpu.VMEM((1, NDIP), F32),
        pltpu.VMEM((9, 1, LANES), F32),
        pltpu.VMEM((1, LANES), F32),
        pltpu.VMEM((1, LANES), F32),
        pltpu.VMEM((4, 1, LANES), F32),
        pltpu.VMEM((2, GX, 2, 2, 2, BY, LANES), F32),
        pltpu.VMEM((2, GX, 2, 2, BY, LANES), F32),
        pltpu.VMEM((2, GX, 2, 2, BY, LANES), F32),
        pltpu.VMEM((2, GX, 2, 2, BY, LANES), F32),
        pltpu.VMEM((2, 4, 2, 2, BY, LANES), F32),
        dma((6, SLOTS)), dma((6, SLOTS)), dma((3, SLOTS)), dma((3, SLOTS)),
        dma((2, 4)), dma((2, 4)),
        dma((SLOTS,)), dma((SLOTS,)),
        dma((2, 4)), dma((2, 4)),
        dma((6,)), dma((6,)),
        dma((4, 4)), dma((4, 4)),
    ]
    volts, misfit, grad_c, grad_t = pl.pallas_call(
        kernel,
        out_shape=(
            jax.ShapeDtypeStruct((NSTEPS, 2, LANES), F32),
            jax.ShapeDtypeStruct((1, 1), F32),
            jax.ShapeDtypeStruct((2, BY, 2 * LANES), F32),
            jax.ShapeDtypeStruct((2, BY, 2 * LANES), F32),
        ),
        in_specs=[vmem, vmem, vmem, vmem, vmem, smem, vmem, smem, vmem],
        out_specs=(vmem, vmem, vmem, vmem),
        scratch_shapes=scratch,
        compiler_params=pltpu.CompilerParams(has_side_effects=True, vmem_limit_bytes=56 << 20),
    )(cond, chg, rlx, start, mem, src_cells, dip, counts, obs)
    return (volts, misfit.reshape(()), grad_c, grad_t)


def solution(mesh):
    placed = (
        P("space", None, None),
        P("space", None, None),
        P("space", None, None),
        P("tx", "space", None, None),
        P(None, "tx", "space", None, None),
        P(None, "tx"),
        P(),
        P(),
        P(None, "tx", "space"),
    )
    return jax.shard_map(
        on_device,
        mesh=mesh,
        in_specs=placed,
        out_specs=(P(None, "tx", "space"), P(), P("space", "tx", None), P("space", "tx", None)),
        check_vma=False,
    )
```

```python
import functools

import jax
import jax.numpy as jnp
from jax import lax
from jax.experimental import pallas as pl
from jax.experimental.pallas import tpu as pltpu
from jax.sharding import PartitionSpec as P

MESH = pl.DeviceIdType.MESH
F32 = jnp.float32
BF16 = jnp.bfloat16
NSTEPS = 3
JACOBI = 8
WEIGHTS = (0.4, 0.3, 0.2, 0.1)
RATIOS = (0.25, 1.0, 4.0, 16.0)
STRENGTH = 4.0

NB, NXB = 4, 4
SLOTS = 8
BX, BY, LANES = 16, 32, 128
HALO = 8
EX, EY = BX + 2 * HALO, BY + 2 * HALO
PAD = 8
VTOP = PAD + HALO
NDIP = 4096
CHUNK = 512
ROWS = BX * BY
UNROLL = 4
R1, R2, T1, T2 = range(4)
COND, CHG, RLX = range(3)
U0, R0 = 4, 5
SIDES = tuple((i, j) for i in (-1, 0, 1) for j in (-1, 0, 1) if (i, j) != (0, 0))


def remote(src, dst, send, recv, device):
    return pltpu.make_async_remote_copy(
        src_ref=src, dst_ref=dst, send_sem=send, recv_sem=recv, device_id=device, device_id_type=MESH
    )


def kernel(
    cond, chg, rlx, start, mem, src_cells, dip, counts, obs,
    volts_out, misfit_out, gc_out, gt_out,
    stage, sstage, blk, sblk, entry, va, vb,
    inv, rhs, f1, f2, ka0, ka1, kb0, kb1, ulast, adj, back,
    ut, acc, part, prx, pry, res, obs_all, live, vswap, sq, sqc, sqz,
    grad, rx, rsum, rz,
    fsend, frecv, ssend, srecv, hsend, hrecv, osend, orecv, psend, precv, qsend, qrecv, gsend, grecv, tsend, trecv,
):
    space = lax.axis_index("space")
    tx = lax.axis_index("tx")
    yp = space // SLOTS
    slot = lax.rem(space, SLOTS)
    gx = slot // 2
    mine = lax.rem(yp, 2)
    bx = 2 * (yp // 2) + lax.rem(slot, 2)
    partner = (yp + 1 - 2 * mine) * SLOTS + slot

    def device(b, x, t):
        return (2 * (b // 2) + t) * SLOTS + 2 * x + lax.rem(b, 2)

    def over(count, body, first=0):
        def at(p, carry):
            body(p)
            return carry

        lax.fori_loop(first, count, at, 0)

    def pieces(body):
        def at(i, carry):
            row, layer = i // 2, lax.rem(i, 2)
            for half in range(2):
                body(row, layer, half, (layer, pl.ds(pl.multiple_of(row * BY, BY), BY), pl.ds(half * LANES, LANES)))
            return carry

        lax.fori_loop(0, 2 * NXB, at, 0)

    def first_fields(row, layer, half, where):
        c = cond[where]
        sstage[COND, row, half, layer] = c
        ids = (2 * space + layer) * (128 * 256) + row * (BY * 256) + half * LANES
        ids = ids + lax.broadcasted_iota(jnp.int32, (BY, LANES), 0) * 256
        ids = ids + lax.broadcasted_iota(jnp.int32, (BY, LANES), 1)
        for t in range(2):
            stage[U0, t, row, half, layer] = start[(t,) + where]
            total = mem[(0, t) + where] + mem[(1, t) + where] + mem[(2, t) + where] + mem[(3, t) + where]
            source = jnp.where(ids == src_cells[0, t], STRENGTH, 0.0) - jnp.where(ids == src_cells[1, t], STRENGTH, 0.0)
            stage[R0, t, row, half, layer] = source + c * total

    def later_fields(row, layer, half, where):
        c = cond[where]
        relax = rlx[where]
        sstage[CHG, row, half, layer] = chg[where]
        sstage[RLX, row, half, layer] = relax
        rate = 1.0 / relax
        decays = [jnp.exp(-rate / ratio) for ratio in RATIOS]
        for t in range(2):
            first, second, slope, slope_d = (jnp.zeros((BY, LANES), F32) for _ in range(4))
            for k in range(4):
                scaled = decays[k] * mem[(k, t) + where]
                first = first + scaled
                second = second + decays[k] * scaled
                tilt = scaled * (1.0 / RATIOS[k])
                slope = slope + tilt
                slope_d = slope_d + decays[k] * tilt
            stage[R1, t, row, half, layer] = c * first
            stage[R2, t, row, half, layer] = c * second
            stage[T1, t, row, half, layer] = c * rate * rate * slope
            stage[T2, t, row, half, layer] = 2.0 * c * rate * rate * slope_d

    def landing(f, j):
        layers = pl.ds(HALO + 2 * j, 2)
        if f == U0:
            return entry.at[0, :, layers, pl.ds(VTOP, BY)]
        if f == R0:
            return rhs.at[0, :, layers, pl.ds(HALO, BY)]
        return blk.at[f, :, pl.ds(2 * j, 2)]

    def target(p):
        q = lax.rem(p + slot, SLOTS)
        return q // 2, lax.rem(q, 2), q, device(yp, q // 2, lax.rem(q, 2))

    def field_copy(f, p):
        x, t, q, to = target(p)
        return to, remote(stage.at[f, t, x], landing(f, slot), fsend.at[f, q], frecv.at[f, slot], {"space": to})

    def static_copy(f, p):
        x, t, q, to = target(p)
        return to, remote(sstage.at[f, x], sblk.at[f, :, pl.ds(2 * slot, 2)], ssend.at[f, q], srecv.at[f, slot], {"space": to})

    def begin(f, copy_of):
        def one(p):
            to, copy = copy_of(f, p)
            pl.when(to != space)(copy.start)

        over(SLOTS, one)

    def finish(f, copy_of):
        def one(p):
            to, copy = copy_of(f, p)
            pl.when(to != space)(copy.wait_send)

        over(SLOTS, one)

    def send_field(f):
        begin(f, field_copy)

        def keep():
            if f == U0:
                entry[0, :, pl.ds(HALO + 2 * slot, 2), VTOP : VTOP + BY] = stage[f, mine, gx]
            elif f == R0:
                rhs[0, :, pl.ds(HALO + 2 * slot, 2), HALO : HALO + BY] = stage[f, mine, gx]
            else:
                blk[f, :, pl.ds(2 * slot, 2)] = stage[f, mine, gx]

        pl.when(bx == yp)(keep)

    def send_static(f):
        begin(f, static_copy)

        def keep():
            sblk[f, :, pl.ds(2 * slot, 2)] = sstage[f, gx]

        pl.when(bx == yp)(keep)

    def take_field(f):
        def one(j):
            here = landing(f, j)
            of = bx * SLOTS + j
            copy = remote(here, here, fsend.at[f, j], frecv.at[f, j], {"space": of})
            pl.when(of != space)(copy.wait_recv)

        over(SLOTS, one)

    def take_static(f):
        def one(j):
            here = sblk.at[f, :, pl.ds(2 * j, 2)]
            of = bx * SLOTS + j
            copy = remote(here, here, ssend.at[f, j], srecv.at[f, j], {"space": of})
            pl.when(of != space)(copy.wait_recv)

        over(SLOTS, one)

    pieces(first_fields)
    send_field(U0)
    send_field(R0)
    send_static(COND)

    def clear(ref, index):
        shape = ref.at[index].shape
        ref[index] = jnp.zeros(shape, F32)

    def clear_pads(x):
        for ref in (va, vb):
            for half in range(2):
                clear(ref, (half, x, pl.ds(0, PAD)))
                clear(ref, (half, x, pl.ds(PAD + EY, PAD)))
        for k in range(5):
            for half in range(2):
                clear(entry, (k, half, x, pl.ds(0, PAD)))
                clear(entry, (k, half, x, pl.ds(PAD + EY, PAD)))

    over(EX, clear_pads)

    def clear_rows(low):
        def one(x):
            for half in range(2):
                at = 0 if low else HALO + BY
                for k in range(5):
                    clear(entry, (k, half, x, pl.ds(PAD + at, HALO)))
                for n in range(NSTEPS):
                    clear(rhs, (n, half, x, pl.ds(at, HALO)))
                clear(inv, (half, x, pl.ds(at, HALO)))

        over(EX, one)

    def clear_layers(low):
        def one(i):
            x = i if low else i + HALO + BX
            for half in range(2):
                for k in range(5):
                    clear(entry, (k, half, x, pl.ds(PAD, EY)))
                for n in range(NSTEPS):
                    clear(rhs, (n, half, x))
                clear(inv, (half, x))

        over(HALO, one)

    pl.when(gx == 0)(lambda: clear_rows(True))
    pl.when(gx == NXB - 1)(lambda: clear_rows(False))
    pl.when(bx == 0)(lambda: clear_layers(True))
    pl.when(bx == NB - 1)(lambda: clear_layers(False))

    def slab_lanes(s, count=1):
        return pl.ds(pl.multiple_of(s * LANES, LANES), count * LANES)

    for t in range(2):
        for n in range(NSTEPS):
            vswap[3 * t + n] = obs[n, t : t + 1, :]
    obs_pair = remote(
        vswap.at[pl.ds(3 * (1 - mine), 3)], obs_all.at[:, :, slab_lanes(space)], qsend.at[0], qrecv.at[0], {"space": partner}
    )
    obs_pair_in = remote(
        vswap.at[pl.ds(3 * (1 - mine), 3)], obs_all.at[:, :, slab_lanes(partner)], qsend.at[0], qrecv.at[0], {"space": partner}
    )
    obs_pair.start()
    obs_all[:, :, slab_lanes(space)] = vswap[pl.ds(3 * mine, 3)]

    def obs_copy(p, which):
        to = lax.rem(slot + p, SLOTS)
        here = obs_all.at[:, :, slab_lanes(space if which == 0 else partner)]
        return remote(here, here, osend.at[which, to], orecv.at[which, slot], {"space": yp * SLOTS + to})

    def obs_wait(p, which):
        of = lax.rem(slot + p, SLOTS)
        row = yp if which == 0 else yp + 1 - 2 * mine
        here = obs_all.at[:, :, slab_lanes(row * SLOTS + of)]
        remote(here, here, osend.at[which, of], orecv.at[which, of], {"space": yp * SLOTS + of}).wait_recv()

    def obs_rows(own):
        half = yp // 2 if own else 1 - yp // 2
        here = obs_all.at[:, :, slab_lanes(2 * half * SLOTS, 2 * SLOTS)]
        return remote(here, here, qsend.at[1], qrecv.at[1], {"space": lax.rem(space + 2 * SLOTS, NB * SLOTS)})

    lane_ids = lax.broadcasted_iota(jnp.int32, (1, LANES), 1)

    def live_at(j, carry):
        live[:, pl.ds(pl.multiple_of(j * LANES, LANES), LANES)] = jnp.where(lane_ids < counts[j], 1.0, 0.0)
        return carry

    lax.fori_loop(0, NB * SLOTS, live_at, 0)

    def halo(ref, top, which):
        copies = []
        for side, (i, j) in enumerate(SIDES):
            layers = {-1: (HALO, HALO, HALO + BX), 1: (BX, HALO, 0), 0: (HALO, BX, HALO)}[i]
            rows = {-1: (top, HALO, top + BY), 1: (top + BY - HALO, HALO, top - HALO), 0: (top, BY, top)}[j]
            sends = (bx + i >= 0) & (bx + i < NB) & (gx + j >= 0) & (gx + j < NXB)
            takes = (bx - i >= 0) & (bx - i < NB) & (gx - j >= 0) & (gx - j < NXB)
            to = device(lax.rem(bx + i + NB, NB), lax.rem(gx + j + NXB, NXB), mine)
            copies.append((sends, takes, remote(
                ref.at[:, pl.ds(layers[0], layers[1]), pl.ds(rows[0], rows[1])],
                ref.at[:, pl.ds(layers[2], layers[1]), pl.ds(rows[2], rows[1])],
                hsend.at[which, side], hrecv.at[which, side], {"space": to},
            )))
        return copies

    def halo_start(ref, top, which):
        for sends, _, copy in halo(ref, top, which):
            pl.when(sends)(copy.start)

    def halo_wait(ref, top, which):
        for sends, takes, copy in halo(ref, top, which):
            pl.when(takes)(copy.wait_recv)
            pl.when(sends)(copy.wait_send)

    def over_x(body, unroll=1):
        def at(x, carry):
            body(x)
            return carry

        lax.fori_loop(0, BX, at, 0, unroll=unroll)

    def neighbour_sums(ref, x, top, rows):
        c0 = ref[0, x, top : top + rows]
        c1 = ref[1, x, top : top + rows]
        lane = lax.broadcasted_iota(jnp.int32, (rows, LANES), 1)
        next0, next1 = pltpu.roll(c0, LANES - 1, 1), pltpu.roll(c1, LANES - 1, 1)
        last0, last1 = pltpu.roll(c0, 1, 1), pltpu.roll(c1, 1, 1)
        z0 = jnp.where(lane == LANES - 1, next1, next0) + jnp.where(lane == 0, 0.0, last0)
        z1 = jnp.where(lane == LANES - 1, 0.0, next1) + jnp.where(lane == 0, last0, last1)
        sums = []
        for half, z in ((0, z0), (1, z1)):
            total = ref[half, x + 1, top : top + rows] + ref[half, x - 1, top : top + rows]
            total = total + ref[half, x, top + 1 : top + rows + 1] + ref[half, x, top - 1 : top + rows - 1]
            sums.append(total + z)
        return sums

    def sweeps(first, last, body, closing):
        source = first
        for s in range(1, last + 1):
            goal = va if s % 2 else vb
            if s == HALO:
                def one(x, carry, source=source):
                    closing(x, neighbour_sums(source, x, VTOP, BY))
                    return carry
            else:
                def one(x, carry, source=source, goal=goal):
                    sums = neighbour_sums(source, x, PAD, EY)
                    for half in range(2):
                        goal[half, x, PAD : PAD + EY] = body(half, x, sums[half])
                    return carry
            lax.fori_loop(s, EX - s, one, 0, unroll=UNROLL)
            source = goal

    def locate(sign, k):
        cells = dip[sign : sign + 1, pl.ds(pl.multiple_of(k * CHUNK, CHUNK), CHUNK)]
        x, y, z = cells >> 15, (cells >> 8) & 127, cells & 255
        own = ((x >> 4) == bx) & ((y >> 5) == gx)
        row = jnp.where(own, (x & 15) * BY + (y & 31), -1)
        hot = lax.broadcasted_iota(jnp.int32, (ROWS, CHUNK), 0) == row
        return jnp.where(hot, 1.0, 0.0).astype(BF16), lax.broadcasted_iota(jnp.int32, (2 * LANES, CHUNK), 0) == z

    def potential(n, half):
        if n == NSTEPS - 1:
            return ulast[half]
        return entry[n + 1, half, HALO : HALO + BX, VTOP : VTOP + BY]

    def gather(n):
        for half in range(2):
            rows = potential(n, half).reshape(ROWS, LANES).T
            high = rows.astype(BF16)
            ut[half * LANES : (half + 1) * LANES, :] = high
            ut[(2 + half) * LANES : (3 + half) * LANES, :] = (rows - high.astype(F32)).astype(BF16)

        def at(k, carry):
            found = []
            for sign in range(2):
                hot, depth = locate(sign, k)
                both = jnp.dot(ut[...], hot, preferred_element_type=F32)
                value = both[: 2 * LANES] + both[2 * LANES :]
                found.append(jnp.sum(jnp.where(depth, value, 0.0), axis=0, keepdims=True))
            part[n, :, pl.ds(pl.multiple_of(k * CHUNK, CHUNK), CHUNK)] = found[0] - found[1]
            return carry

        lax.fori_loop(0, NDIP // CHUNK, at, 0)

    def scatter(n):
        acc[n - 1] = jnp.zeros((ROWS, 4 * LANES), F32)

        def at(k, carry):
            value = res[n, :, pl.ds(pl.multiple_of(k * CHUNK, CHUNK), CHUNK)]
            for sign in range(2):
                hot, depth = locate(sign, k)
                placed = jnp.where(depth, value if sign == 0 else -value, 0.0)
                high = placed.astype(BF16)
                low = (placed - high.astype(F32)).astype(BF16)
                acc[n - 1] += lax.dot_general(
                    hot, jnp.concatenate([high, low], axis=0), (((1,), (1,)), ((), ())), preferred_element_type=F32
                )
            return carry

        lax.fori_loop(0, NDIP // CHUNK, at, 0)

    def injected(n, half, x):
        rows = pl.ds(pl.multiple_of(x * BY, BY), BY)
        return (
            acc[n - 1, rows, half * LANES : (half + 1) * LANES]
            + acc[n - 1, rows, (2 + half) * LANES : (3 + half) * LANES]
        )

    take_field(U0)
    halo_start(entry.at[0], VTOP, 0)
    take_field(R0)
    halo_start(rhs.at[0], HALO, 5)
    take_static(COND)

    def inverse(x):
        for half in range(2):
            inv[half, HALO + x, HALO : HALO + BY] = 1.0 / (6.0 + sblk[COND, half, x])

    over_x(inverse)
    halo_start(inv, HALO, 8)
    pieces(later_fields)
    send_static(CHG)
    send_static(RLX)
    send_field(R1)
    halo_wait(entry.at[0], VTOP, 0)
    halo_wait(rhs.at[0], HALO, 5)
    halo_wait(inv, HALO, 8)

    def statics(x):
        for half in range(2):
            c, g = sblk[COND, half, x], sblk[CHG, half, x]
            rate = 1.0 / sblk[RLX, half, x]
            a0, a1, b0, b1 = (jnp.zeros((BY, LANES), F32) for _ in range(4))
            for k in range(4):
                decay = jnp.exp(-rate / RATIOS[k])
                fresh = WEIGHTS[k] * (1.0 - decay)
                a0 = a0 + fresh
                a1 = a1 + fresh * decay
                tilt = decay * (WEIGHTS[k] / RATIOS[k])
                b0 = b0 + tilt
                b1 = b1 + tilt * (1.0 - 2.0 * decay)
            f1[half, x] = c * g * a0
            f2[half, x] = c * g * a1
            ka0[half, x] = c * a0
            ka1[half, x] = c * a1
            kb0[half, x] = c * g * rate * rate * b0
            kb1[half, x] = c * g * rate * rate * b1

    def block_of(k, half, x):
        return entry[k, half, HALO + x, VTOP : VTOP + BY]

    def forward(n):
        def body(half, x, total):
            return (rhs[n, half, x] + total) * inv[half, x]

        def closing(x, sums):
            for half in range(2):
                made = (rhs[n, half, x, HALO : HALO + BY] + sums[half]) * inv[half, x, HALO : HALO + BY]
                if n == NSTEPS - 1:
                    ulast[half, x - HALO] = made
                else:
                    entry[n + 1, half, x, VTOP : VTOP + BY] = made

        sweeps(entry.at[n], JACOBI, body, closing)

    forward(0)
    halo_start(entry.at[1], VTOP, 1)
    take_static(CHG)
    take_static(RLX)
    over_x(statics)
    take_field(R1)

    def step_one(x):
        for half in range(2):
            rhs[1, half, HALO + x, HALO : HALO + BY] = blk[R1, half, x] + f1[half, x] * block_of(1, half, x)

    over_x(step_one)
    halo_start(rhs.at[1], HALO, 6)
    send_field(R2)
    obs_pair_in.wait_recv()
    over(SLOTS, lambda p: obs_copy(p, 0).start(), 1)
    over(SLOTS, lambda p: obs_copy(p, 1).start(), 1)
    gather(0)
    halo_wait(entry.at[1], VTOP, 1)
    halo_wait(rhs.at[1], HALO, 6)
    forward(1)
    halo_start(entry.at[2], VTOP, 2)
    take_field(R2)

    def step_two(x):
        for half in range(2):
            rhs[2, half, HALO + x, HALO : HALO + BY] = (
                blk[R2, half, x] + f2[half, x] * block_of(1, half, x) + f1[half, x] * block_of(2, half, x)
            )

    over_x(step_two)
    halo_start(rhs.at[2], HALO, 7)
    send_field(T1)
    send_field(T2)
    over(SLOTS, lambda p: obs_wait(p, 0), 1)
    over(SLOTS, lambda p: obs_wait(p, 1), 1)
    obs_rows(True).start()
    gather(1)
    halo_wait(entry.at[2], VTOP, 2)
    halo_wait(rhs.at[2], HALO, 7)
    forward(2)
    gather(2)
    obs_rows(False).wait_recv()

    def row_copy(p):
        to = lax.rem(gx + p, NXB)
        return remote(part, prx.at[gx], psend.at[0, to], precv.at[0, gx], {"space": device(bx, to, mine)})

    def row_wait(p):
        of = lax.rem(gx + p, NXB)
        remote(part, prx.at[of], psend.at[0, of], precv.at[0, of], {"space": device(bx, of, mine)}).wait_recv()

    over(4, lambda p: row_copy(p).start(), 1)
    prx[gx] = part[...]
    over(4, row_wait, 1)
    res[...] = (prx[0] + prx[1]) + (prx[2] + prx[3])

    def col_copy(p):
        to = lax.rem(bx + p, NB)
        return remote(res, pry.at[bx], psend.at[1, to], precv.at[1, bx], {"space": device(to, gx, mine)})

    def col_wait(p):
        of = lax.rem(bx + p, NB)
        remote(res, pry.at[of], psend.at[1, of], precv.at[1, of], {"space": device(of, gx, mine)}).wait_recv()

    over(4, lambda p: col_copy(p).start(), 1)
    pry[bx] = res[...]
    over(4, col_wait, 1)
    over(4, lambda p: col_copy(p).wait_send(), 1)
    squares = jnp.zeros((1, NDIP), F32)
    for n in range(NSTEPS):
        volts = live[...] * ((pry[0, n] + pry[1, n]) + (pry[2, n] + pry[3, n]))
        part_resid = live[...] * (volts - obs_all[n])
        pry[0, n] = volts
        res[n] = part_resid
        squares = squares + part_resid * part_resid

    own = pl.ds(pl.multiple_of(space * LANES, LANES), LANES)
    other = pl.ds(pl.multiple_of(partner * LANES, LANES), LANES)
    swap = remote(pry.at[0, :, :, other], vswap.at[pl.ds(6, 3)], qsend.at[2], qrecv.at[2], {"space": partner})
    swap.start()
    lanes = squares[:, 0:LANES]
    for j in range(1, NDIP // LANES):
        lanes = lanes + squares[:, j * LANES : (j + 1) * LANES]
    sq[...] = lanes
    pair = remote(sq, sqc, qsend.at[3], qrecv.at[3], {"space": partner})
    pair.start()
    for n in range(NSTEPS):
        volts_out[n, pl.ds(mine, 1), :] = pry[0, n, :, own]
    swap.wait()
    for n in range(NSTEPS):
        volts_out[n, pl.ds(1 - mine, 1), :] = vswap[6 + n]
    pair.wait()
    sqz[tx] = sq[...] + sqc[...]

    def sq_copy(p):
        to = lax.rem(tx + p, 4)
        return remote(sqz.at[tx], sqz.at[tx], tsend.at[2, to], trecv.at[2, tx], {"tx": to})

    def sq_wait(p):
        of = lax.rem(tx + p, 4)
        remote(sqz.at[of], sqz.at[of], tsend.at[2, of], trecv.at[2, of], {"tx": of}).wait_recv()

    over(4, lambda p: sq_copy(p).start(), 1)

    def begin_adjoint(n):
        def body(x):
            for half in range(2):
                field = injected(n, half, x)
                if n == 1:
                    field = field + back[half, x] + f1[half, x] * adj[1, half, HALO + x, HALO : HALO + BY]
                scaled = field * inv[half, HALO + x, HALO : HALO + BY]
                adj[n - 1, half, HALO + x, HALO : HALO + BY] = scaled
                entry[5 - n, half, HALO + x, VTOP : VTOP + BY] = scaled

        over_x(body)

    def adjoint(n):
        def body(half, x, total):
            scaled = total * inv[half, x]
            adj[n - 1, half, x] += scaled
            return scaled

        def closing(x, sums):
            for half in range(2):
                back[half, x - HALO] = sums[half]

        sweeps(entry.at[5 - n], JACOBI if n == 2 else JACOBI - 1, body, closing)

    scatter(2)
    begin_adjoint(2)
    halo_start(entry.at[3], VTOP, 3)
    scatter(1)
    halo_wait(entry.at[3], VTOP, 3)
    adjoint(2)
    begin_adjoint(1)
    halo_start(entry.at[4], VTOP, 4)
    halo_wait(entry.at[4], VTOP, 4)
    adjoint(1)

    take_field(T1)
    take_field(T2)

    def gradients(x):
        for half in range(2):
            s1, s2 = (adj[k, half, HALO + x, HALO : HALO + BY] for k in range(2))
            u0, u1 = block_of(1, half, x), block_of(2, half, x)
            same = s2 * u1 + s1 * u0
            cross = s2 * u0
            grad[0, x // 2, half, lax.rem(x, 2)] = ka0[half, x] * same + ka1[half, x] * cross
            grad[1, x // 2, half, lax.rem(x, 2)] = (
                s1 * blk[T1, half, x] + s2 * blk[T2, half, x] - kb0[half, x] * same + kb1[half, x] * cross
            )

    over_x(gradients)

    def back_copy(f, p):
        j = lax.rem(p + slot, SLOTS)
        to = bx * SLOTS + j
        return to, remote(grad.at[f, j], rx.at[f, gx, mine], gsend.at[f, j], grecv.at[f, 2 * gx + mine], {"space": to})

    def back_wait(f, q):
        of = device(yp, q // 2, lax.rem(q, 2))
        here = rx.at[f, q // 2, lax.rem(q, 2)]
        copy = remote(here, here, gsend.at[f, q], grecv.at[f, q], {"space": of})
        pl.when(of != space)(copy.wait_recv)

    def tx_copy(f, p):
        to = lax.rem(tx + p, 4)
        return remote(rsum.at[f, to], rz.at[f, tx], tsend.at[f, to], trecv.at[f, tx], {"tx": to})

    def tx_wait(f, p):
        of = lax.rem(tx + p, 4)
        remote(rsum.at[f, of], rz.at[f, of], tsend.at[f, of], trecv.at[f, of], {"tx": of}).wait_recv()

    for f in range(2):
        begin(f, back_copy)

        def keep(f=f):
            rx[f, gx, mine] = grad[f, slot]

        pl.when(bx == yp)(keep)
    over(4, sq_wait, 1)
    total = (sqz[0] + sqz[1]) + (sqz[2] + sqz[3])
    misfit = jnp.sqrt(1.0 + jnp.sum(total, axis=1, keepdims=True))
    misfit_out[...] = misfit
    scale = 1.0 / misfit
    for f in range(2):
        over(SLOTS, functools.partial(back_wait, f))
        for row in range(4):
            rsum[f, row] = rx[f, row, 0] + rx[f, row, 1]
        over(4, lambda p: tx_copy(f, p).start(), 1)
        rz[f, tx] = rsum[f, tx]
    for f, out in ((0, gc_out), (1, gt_out)):
        over(4, functools.partial(tx_wait, f), 1)
        for half in range(2):
            value = (rz[f, 0, half] + rz[f, 1, half]) + (rz[f, 2, half] + rz[f, 3, half])
            out[:, :, half * LANES : (half + 1) * LANES] = value * scale.reshape(1, 1, 1)

    for f in range(6):
        finish(f, field_copy)
    for f in range(3):
        finish(f, static_copy)
    obs_pair.wait_send()
    for which in range(2):
        over(SLOTS, lambda p: obs_copy(p, which).wait_send(), 1)
    obs_rows(True).wait_send()
    over(4, lambda p: row_copy(p).wait_send(), 1)
    over(4, lambda p: sq_copy(p).wait_send(), 1)
    for f in range(2):
        finish(f, back_copy)
        over(4, lambda p: tx_copy(f, p).wait_send(), 1)


def on_device(cond, chg, rlx, start, mem, src_cells, dip, counts, obs):
    vmem = pl.BlockSpec(memory_space=pltpu.VMEM)
    smem = pl.BlockSpec(memory_space=pltpu.SMEM)
    field = pltpu.VMEM((2, BX, BY, LANES), F32)
    dma = pltpu.SemaphoreType.DMA
    wide = pltpu.VMEM((2, EX, EY + 2 * PAD, LANES), F32)
    scratch = [
        pltpu.VMEM((6, 2, NXB, 2, 2, BY, LANES), F32),
        pltpu.VMEM((3, NXB, 2, 2, BY, LANES), F32),
        pltpu.VMEM((4, 2, BX, BY, LANES), F32),
        pltpu.VMEM((3, 2, BX, BY, LANES), F32),
        pltpu.VMEM((5, 2, EX, EY + 2 * PAD, LANES), F32),
        wide, wide,
        pltpu.VMEM((2, EX, EY, LANES), F32),
        pltpu.VMEM((NSTEPS, 2, EX, EY, LANES), F32),
        field, field, field, field, field, field,
        field,
        pltpu.VMEM((2, 2, EX, EY, LANES), F32),
        field,
        pltpu.VMEM((4 * LANES, ROWS), BF16),
        pltpu.VMEM((2, ROWS, 4 * LANES), F32),
        pltpu.VMEM((NSTEPS, 1, NDIP), F32),
        pltpu.VMEM((NXB, NSTEPS, 1, NDIP), F32),
        pltpu.VMEM((NB, NSTEPS, 1, NDIP), F32),
        pltpu.VMEM((NSTEPS, 1, NDIP), F32),
        pltpu.VMEM((NSTEPS, 1, NDIP), F32),
        pltpu.VMEM((1, NDIP), F32),
        pltpu.VMEM((9, 1, LANES), F32),
        pltpu.VMEM((1, LANES), F32),
        pltpu.VMEM((1, LANES), F32),
        pltpu.VMEM((4, 1, LANES), F32),
        pltpu.VMEM((2, SLOTS, 2, 2, BY, LANES), F32),
        pltpu.VMEM((2, NXB, 2, 2, 2, BY, LANES), F32),
        pltpu.VMEM((2, NXB, 2, 2, BY, LANES), F32),
        pltpu.VMEM((2, 4, 2, 2, BY, LANES), F32),
        dma((6, SLOTS)), dma((6, SLOTS)), dma((3, SLOTS)), dma((3, SLOTS)),
        dma((9, 8)), dma((9, 8)),
        dma((2, SLOTS)), dma((2, SLOTS)),
        dma((2, 4)), dma((2, 4)),
        dma((4,)), dma((4,)),
        dma((2, SLOTS)), dma((2, SLOTS)),
        dma((3, 4)), dma((3, 4)),
    ]
    volts, misfit, grad_c, grad_t = pl.pallas_call(
        kernel,
        out_shape=(
            jax.ShapeDtypeStruct((NSTEPS, 2, LANES), F32),
            jax.ShapeDtypeStruct((1, 1), F32),
            jax.ShapeDtypeStruct((2, BY, 2 * LANES), F32),
            jax.ShapeDtypeStruct((2, BY, 2 * LANES), F32),
        ),
        in_specs=[vmem, vmem, vmem, vmem, vmem, smem, vmem, smem, vmem],
        out_specs=(vmem, vmem, vmem, vmem),
        scratch_shapes=scratch,
        compiler_params=pltpu.CompilerParams(has_side_effects=True, vmem_limit_bytes=60 << 20),
    )(cond, chg, rlx, start, mem, src_cells, dip, counts, obs)
    return (volts, misfit.reshape(()), grad_c, grad_t)


def solution(mesh):
    placed = (
        P("space", None, None),
        P("space", None, None),
        P("space", None, None),
        P("tx", "space", None, None),
        P(None, "tx", "space", None, None),
        P(None, "tx"),
        P(),
        P(),
        P(None, "tx", "space"),
    )
    return jax.shard_map(
        on_device,
        mesh=mesh,
        in_specs=placed,
        out_specs=(P(None, "tx", "space"), P(), P("space", "tx", None), P("space", "tx", None)),
        check_vma=False,
    )
```

```python
import functools

import jax
import jax.numpy as jnp
from jax import lax
from jax.experimental import pallas as pl
from jax.experimental.pallas import tpu as pltpu
from jax.sharding import PartitionSpec as P

MESH = pl.DeviceIdType.MESH
F32 = jnp.float32
BF16 = jnp.bfloat16
NSTEPS = 3
JACOBI = 8
WEIGHTS = (0.4, 0.3, 0.2, 0.1)
RATIOS = (0.25, 1.0, 4.0, 16.0)
STRENGTH = 4.0

NB, NXB = 4, 4
SLOTS = 8
BX, BY, LANES = 16, 32, 128
HALO = 8
EX, EY = BX + 2 * HALO, BY + 2 * HALO
PAD = 8
VTOP = PAD + HALO
NDIP = 4096
CHUNK = 512
ROWS = BX * BY
UNROLL = 4
U0, R0, R1, R2 = range(4)
COND, F1, F2 = range(3)
KA0, KA1, KB0, KB1 = range(4)
POT0, POT1, DUAL2, DUAL1 = range(4)
SPACES = 32
SIDES = tuple((i, j) for i in (-1, 0, 1) for j in (-1, 0, 1) if (i, j) != (0, 0))


def remote(src, dst, send, recv, device):
    return pltpu.make_async_remote_copy(
        src_ref=src, dst_ref=dst, send_sem=send, recv_sem=recv, device_id=device, device_id_type=MESH
    )


def kernel(
    cond_hbm, chg_hbm, rlx_hbm, start_hbm, mem_hbm, src_cells, dip, counts, obs,
    volts_out, misfit_out, gc_out, gt_out,
    cond, chg, rlx, start, mem,
    stage, sstage, tilts, factors, blk, sblk, entry, va, vb,
    inv, rhs, ulast, adj, back,
    ut, acc, part, prx, pry, res, obs_all, live, vswap, sq, sqc, sqz,
    rx, rsum, rz,
    lsem, fsend, frecv, ssend, srecv, zsend, zrecv, hsend, hrecv, osend, orecv, psend, precv, qsend, qrecv,
    gsend, grecv, tsend, trecv,
):
    space = lax.axis_index("space")
    tx = lax.axis_index("tx")
    yp = space // SLOTS
    slot = lax.rem(space, SLOTS)
    gx = slot // 2
    mine = lax.rem(yp, 2)
    bx = 2 * (yp // 2) + lax.rem(slot, 2)
    partner = (yp + 1 - 2 * mine) * SLOTS + slot

    def device(b, x, t):
        return (2 * (b // 2) + t) * SLOTS + 2 * x + lax.rem(b, 2)

    def over(count, body, first=0):
        def at(p, carry):
            body(p)
            return carry

        lax.fori_loop(first, count, at, 0)

    barrier = pltpu.get_barrier_semaphore()
    loads = [
        pltpu.make_async_copy(a, b, lsem.at[i])
        for i, (a, b) in enumerate(
            ((cond_hbm, cond), (start_hbm, start), (mem_hbm, mem), (chg_hbm, chg), (rlx_hbm, rlx))
        )
    ]
    for load in loads:
        load.start()

    def greet_space(q):
        pl.semaphore_signal(barrier, 1, device_id={"space": lax.rem(space + q, SPACES)}, device_id_type=MESH)

    def greet_tx(q):
        pl.semaphore_signal(barrier, 1, device_id={"tx": lax.rem(tx + q, 4)}, device_id_type=MESH)

    over(SPACES, greet_space, 1)
    over(4, greet_tx, 1)

    def pieces(body):
        def at(i, carry):
            row, layer = i // 2, lax.rem(i, 2)
            for half in range(2):
                body(row, layer, half, (layer, pl.ds(pl.multiple_of(row * BY, BY), BY), pl.ds(half * LANES, LANES)))
            return carry

        lax.fori_loop(0, 2 * NXB, at, 0)

    def first_fields(row, layer, half, where):
        c = cond[where]
        sstage[COND, row, half, layer] = c
        ids = (2 * space + layer) * (128 * 256) + row * (BY * 256) + half * LANES
        ids = ids + lax.broadcasted_iota(jnp.int32, (BY, LANES), 0) * 256
        ids = ids + lax.broadcasted_iota(jnp.int32, (BY, LANES), 1)
        for t in range(2):
            stage[U0, t, row, half, layer] = start[(t,) + where]
            total = mem[(0, t) + where] + mem[(1, t) + where] + mem[(2, t) + where] + mem[(3, t) + where]
            source = jnp.where(ids == src_cells[0, t], STRENGTH, 0.0) - jnp.where(ids == src_cells[1, t], STRENGTH, 0.0)
            stage[R0, t, row, half, layer] = source + c * total

    def later_fields(row, layer, half, where):
        c, g = cond[where], chg[where]
        rate = 1.0 / rlx[where]
        decays = [jnp.exp(-rate / ratio) for ratio in RATIOS]
        a0, a1, b0, b1 = (jnp.zeros((BY, LANES), F32) for _ in range(4))
        for k in range(4):
            fresh = WEIGHTS[k] * (1.0 - decays[k])
            a0 = a0 + fresh
            a1 = a1 + fresh * decays[k]
            tilt = decays[k] * (WEIGHTS[k] / RATIOS[k])
            b0 = b0 + tilt
            b1 = b1 + tilt * (1.0 - 2.0 * decays[k])
        sstage[F1, row, half, layer] = c * g * a0
        sstage[F2, row, half, layer] = c * g * a1
        factors[KA0, row, half, layer] = c * a0
        factors[KA1, row, half, layer] = c * a1
        factors[KB0, row, half, layer] = c * g * rate * rate * b0
        factors[KB1, row, half, layer] = c * g * rate * rate * b1
        for t in range(2):
            first, second, slope, slope_d = (jnp.zeros((BY, LANES), F32) for _ in range(4))
            for k in range(4):
                scaled = decays[k] * mem[(k, t) + where]
                first = first + scaled
                second = second + decays[k] * scaled
                tilt = scaled * (1.0 / RATIOS[k])
                slope = slope + tilt
                slope_d = slope_d + decays[k] * tilt
            stage[R1, t, row, half, layer] = c * first
            stage[R2, t, row, half, layer] = c * second
            tilts[0, t, row, half, layer] = c * rate * rate * slope
            tilts[1, t, row, half, layer] = 2.0 * c * rate * rate * slope_d

    def landing(f, j):
        layers = pl.ds(HALO + 2 * j, 2)
        if f == U0:
            return entry.at[0, :, layers, pl.ds(VTOP, BY)]
        if f == R0:
            return rhs.at[0, :, layers, pl.ds(HALO, BY)]
        return blk.at[f - R1, :, pl.ds(2 * j, 2)]

    def target(p):
        q = lax.rem(p + slot, SLOTS)
        return q // 2, lax.rem(q, 2), q, device(yp, q // 2, lax.rem(q, 2))

    def field_copy(f, p):
        x, t, q, to = target(p)
        return to, remote(stage.at[f, t, x], landing(f, slot), fsend.at[f, q], frecv.at[f, slot], {"space": to})

    def static_copy(f, p):
        x, t, q, to = target(p)
        quarter = (tx // 2, lax.rem(tx, 2))
        return to, remote(
            sstage.at[(f, x) + quarter], sblk.at[(f,) + quarter + (slot,)], ssend.at[f, q], srecv.at[f, slot], {"space": to}
        )

    def begin(f, copy_of):
        def one(p):
            to, copy = copy_of(f, p)
            pl.when(to != space)(copy.start)

        over(SLOTS, one)

    def finish(f, copy_of):
        def one(p):
            to, copy = copy_of(f, p)
            pl.when(to != space)(copy.wait_send)

        over(SLOTS, one)

    def send_field(f):
        begin(f, field_copy)

        def keep():
            if f == U0:
                entry[0, :, pl.ds(HALO + 2 * slot, 2), VTOP : VTOP + BY] = stage[f, mine, gx]
            elif f == R0:
                rhs[0, :, pl.ds(HALO + 2 * slot, 2), HALO : HALO + BY] = stage[f, mine, gx]
            else:
                blk[f - R1, :, pl.ds(2 * slot, 2)] = stage[f, mine, gx]

        pl.when(bx == yp)(keep)

    def send_static(f):
        begin(f, static_copy)

        def keep():
            sblk[f, tx // 2, lax.rem(tx, 2), slot] = sstage[f, gx, tx // 2, lax.rem(tx, 2)]

        pl.when(bx == yp)(keep)

    def take_field(f):
        def one(j):
            here = landing(f, j)
            of = bx * SLOTS + j
            copy = remote(here, here, fsend.at[f, j], frecv.at[f, j], {"space": of})
            pl.when(of != space)(copy.wait_recv)

        over(SLOTS, one)

    def spread_copy(f, p):
        to = lax.rem(tx + p, 4)
        quarter = sblk.at[f, tx // 2, lax.rem(tx, 2)]
        return remote(quarter, quarter, zsend.at[f, to], zrecv.at[f, tx], {"tx": to})

    def spread_static(f):
        def one(j):
            here = sblk.at[f, tx // 2, lax.rem(tx, 2), j]
            of = bx * SLOTS + j
            copy = remote(here, here, ssend.at[f, j], srecv.at[f, j], {"space": of})
            pl.when(of != space)(copy.wait_recv)

        over(SLOTS, one)
        over(4, lambda p: spread_copy(f, p).start(), 1)

    def take_static(f):
        def one(p):
            of = lax.rem(tx + p, 4)
            quarter = sblk.at[f, of // 2, lax.rem(of, 2)]
            remote(quarter, quarter, zsend.at[f, of], zrecv.at[f, of], {"tx": of}).wait_recv()

        over(4, one, 1)

    def static(f, half, x):
        return sblk[f, half, lax.rem(x, 2), x // 2]

    for load in loads[:3]:
        load.wait()
    pieces(first_fields)

    def clear(ref, index):
        shape = ref.at[index].shape
        ref[index] = jnp.zeros(shape, F32)

    def clear_pads(x):
        for ref in (va, vb):
            for half in range(2):
                clear(ref, (half, x, pl.ds(0, PAD)))
                clear(ref, (half, x, pl.ds(PAD + EY, PAD)))
        for k in range(5):
            for half in range(2):
                clear(entry, (k, half, x, pl.ds(0, PAD)))
                clear(entry, (k, half, x, pl.ds(PAD + EY, PAD)))

    over(EX, clear_pads)

    def clear_rows(low):
        def one(x):
            for half in range(2):
                at = 0 if low else HALO + BY
                for k in range(5):
                    clear(entry, (k, half, x, pl.ds(PAD + at, HALO)))
                for n in range(NSTEPS):
                    clear(rhs, (n, half, x, pl.ds(at, HALO)))
                clear(inv, (half, x, pl.ds(at, HALO)))

        over(EX, one)

    def clear_layers(low):
        def one(i):
            x = i if low else i + HALO + BX
            for half in range(2):
                for k in range(5):
                    clear(entry, (k, half, x, pl.ds(PAD, EY)))
                for n in range(NSTEPS):
                    clear(rhs, (n, half, x))
                clear(inv, (half, x))

        over(HALO, one)

    pl.when(gx == 0)(lambda: clear_rows(True))
    pl.when(gx == NXB - 1)(lambda: clear_rows(False))
    pl.when(bx == 0)(lambda: clear_layers(True))
    pl.when(bx == NB - 1)(lambda: clear_layers(False))

    pl.semaphore_wait(barrier, SPACES + 2)
    send_static(COND)
    send_field(U0)
    send_field(R0)

    def slab_lanes(s, count=1):
        return pl.ds(pl.multiple_of(s * LANES, LANES), count * LANES)

    for t in range(2):
        for n in range(NSTEPS):
            vswap[3 * t + n] = obs[n, t : t + 1, :]
    obs_pair = remote(
        vswap.at[pl.ds(3 * (1 - mine), 3)], obs_all.at[:, :, slab_lanes(space)], qsend.at[0], qrecv.at[0], {"space": partner}
    )
    obs_pair_in = remote(
        vswap.at[pl.ds(3 * (1 - mine), 3)], obs_all.at[:, :, slab_lanes(partner)], qsend.at[0], qrecv.at[0], {"space": partner}
    )
    obs_pair.start()
    obs_all[:, :, slab_lanes(space)] = vswap[pl.ds(3 * mine, 3)]

    def obs_copy(p, which):
        to = lax.rem(slot + p, SLOTS)
        here = obs_all.at[:, :, slab_lanes(space if which == 0 else partner)]
        return remote(here, here, osend.at[which, to], orecv.at[which, slot], {"space": yp * SLOTS + to})

    def obs_wait(p, which):
        of = lax.rem(slot + p, SLOTS)
        row = yp if which == 0 else yp + 1 - 2 * mine
        here = obs_all.at[:, :, slab_lanes(row * SLOTS + of)]
        remote(here, here, osend.at[which, of], orecv.at[which, of], {"space": yp * SLOTS + of}).wait_recv()

    def obs_rows(own):
        half = yp // 2 if own else 1 - yp // 2
        here = obs_all.at[:, :, slab_lanes(2 * half * SLOTS, 2 * SLOTS)]
        return remote(here, here, qsend.at[1], qrecv.at[1], {"space": lax.rem(space + 2 * SLOTS, NB * SLOTS)})

    lane_ids = lax.broadcasted_iota(jnp.int32, (1, LANES), 1)

    def live_at(j, carry):
        live[:, pl.ds(pl.multiple_of(j * LANES, LANES), LANES)] = jnp.where(lane_ids < counts[j], 1.0, 0.0)
        return carry

    lax.fori_loop(0, NB * SLOTS, live_at, 0)

    def halo(ref, top, which):
        width = HALO if top == VTOP else HALO - 1
        copies = []
        for side, (i, j) in enumerate(SIDES):
            deep = width if j == 0 else width - 1
            layers = {-1: (HALO, deep, HALO + BX), 1: (HALO + BX - deep, deep, HALO - deep), 0: (HALO, BX, HALO)}[i]
            rows = {-1: (top, HALO, top + BY), 1: (top + BY - HALO, HALO, top - HALO), 0: (top, BY, top)}[j]
            sends = (bx + i >= 0) & (bx + i < NB) & (gx + j >= 0) & (gx + j < NXB)
            takes = (bx - i >= 0) & (bx - i < NB) & (gx - j >= 0) & (gx - j < NXB)
            to = device(lax.rem(bx + i + NB, NB), lax.rem(gx + j + NXB, NXB), mine)
            copies.append((sends, takes, remote(
                ref.at[:, pl.ds(layers[0], layers[1]), pl.ds(rows[0], rows[1])],
                ref.at[:, pl.ds(layers[2], layers[1]), pl.ds(rows[2], rows[1])],
                hsend.at[which, side], hrecv.at[which, side], {"space": to},
            )))
        return copies

    def halo_start(ref, top, which):
        for sends, _, copy in halo(ref, top, which):
            pl.when(sends)(copy.start)

    def halo_wait(ref, top, which):
        for sends, takes, copy in halo(ref, top, which):
            pl.when(takes)(copy.wait_recv)
            pl.when(sends)(copy.wait_send)

    def over_x(body, unroll=1):
        def at(x, carry):
            body(x)
            return carry

        lax.fori_loop(0, BX, at, 0, unroll=unroll)

    def neighbour_sums(ref, x, top, rows):
        c0 = ref[0, x, top : top + rows]
        c1 = ref[1, x, top : top + rows]
        lane = lax.broadcasted_iota(jnp.int32, (rows, LANES), 1)
        next0, next1 = pltpu.roll(c0, LANES - 1, 1), pltpu.roll(c1, LANES - 1, 1)
        last0, last1 = pltpu.roll(c0, 1, 1), pltpu.roll(c1, 1, 1)
        z0 = jnp.where(lane == LANES - 1, next1, next0) + jnp.where(lane == 0, 0.0, last0)
        z1 = jnp.where(lane == LANES - 1, 0.0, next1) + jnp.where(lane == 0, last0, last1)
        sums = []
        for half, z in ((0, z0), (1, z1)):
            total = ref[half, x + 1, top : top + rows] + ref[half, x - 1, top : top + rows]
            total = total + ref[half, x, top + 1 : top + rows + 1] + ref[half, x, top - 1 : top + rows - 1]
            sums.append(total + z)
        return sums

    def sweeps(first, last, body, closing):
        source = first
        for s in range(1, last + 1):
            goal = va if s % 2 else vb
            if s == HALO:
                def one(x, carry, source=source):
                    closing(x, neighbour_sums(source, x, VTOP, BY))
                    return carry
            else:
                def one(x, carry, source=source, goal=goal):
                    sums = neighbour_sums(source, x, PAD, EY)
                    for half in range(2):
                        goal[half, x, PAD : PAD + EY] = body(half, x, sums[half])
                    return carry
            lax.fori_loop(s, EX - s, one, 0, unroll=UNROLL)
            source = goal

    def locate(sign, k):
        cells = dip[sign : sign + 1, pl.ds(pl.multiple_of(k * CHUNK, CHUNK), CHUNK)]
        x, y, z = cells >> 15, (cells >> 8) & 127, cells & 255
        own = ((x >> 4) == bx) & ((y >> 5) == gx)
        row = jnp.where(own, (x & 15) * BY + (y & 31), -1)
        hot = lax.broadcasted_iota(jnp.int32, (ROWS, CHUNK), 0) == row
        return jnp.where(hot, 1.0, 0.0).astype(BF16), lax.broadcasted_iota(jnp.int32, (2 * LANES, CHUNK), 0) == z

    def potential(n, half):
        if n == NSTEPS - 1:
            return ulast[half]
        return entry[n + 1, half, HALO : HALO + BX, VTOP : VTOP + BY]

    def gather(n):
        for half in range(2):
            rows = potential(n, half).reshape(ROWS, LANES).T
            high = rows.astype(BF16)
            ut[half * LANES : (half + 1) * LANES, :] = high
            ut[(2 + half) * LANES : (3 + half) * LANES, :] = (rows - high.astype(F32)).astype(BF16)

        def at(k, carry):
            found = []
            for sign in range(2):
                hot, depth = locate(sign, k)
                both = jnp.dot(ut[...], hot, preferred_element_type=F32)
                value = both[: 2 * LANES] + both[2 * LANES :]
                found.append(jnp.sum(jnp.where(depth, value, 0.0), axis=0, keepdims=True))
            part[n, :, pl.ds(pl.multiple_of(k * CHUNK, CHUNK), CHUNK)] = found[0] - found[1]
            return carry

        lax.fori_loop(0, NDIP // CHUNK, at, 0)

    def scatter(n):
        acc[n - 1] = jnp.zeros((ROWS, 4 * LANES), F32)

        def at(k, carry):
            value = res[n, :, pl.ds(pl.multiple_of(k * CHUNK, CHUNK), CHUNK)]
            for sign in range(2):
                hot, depth = locate(sign, k)
                placed = jnp.where(depth, value if sign == 0 else -value, 0.0)
                high = placed.astype(BF16)
                low = (placed - high.astype(F32)).astype(BF16)
                acc[n - 1] += lax.dot_general(
                    hot, jnp.concatenate([high, low], axis=0), (((1,), (1,)), ((), ())), preferred_element_type=F32
                )
            return carry

        lax.fori_loop(0, NDIP // CHUNK, at, 0)

    def injected(n, half, x):
        rows = pl.ds(pl.multiple_of(x * BY, BY), BY)
        return (
            acc[n - 1, rows, half * LANES : (half + 1) * LANES]
            + acc[n - 1, rows, (2 + half) * LANES : (3 + half) * LANES]
        )

    spread_static(COND)
    for load in loads[3:]:
        load.wait()
    pieces(later_fields)
    take_field(U0)
    halo_start(entry.at[0], VTOP, 0)
    take_static(COND)

    def inverse(x):
        for half in range(2):
            inv[half, HALO + x, HALO : HALO + BY] = 1.0 / (6.0 + static(COND, half, x))

    over_x(inverse)
    halo_start(inv, HALO, 8)
    take_field(R0)
    halo_start(rhs.at[0], HALO, 5)
    send_static(F1)
    send_static(F2)
    halo_wait(entry.at[0], VTOP, 0)
    halo_wait(inv, HALO, 8)
    halo_wait(rhs.at[0], HALO, 5)
    send_field(R1)
    spread_static(F1)
    spread_static(F2)

    def block_of(k, half, x):
        return entry[k, half, HALO + x, VTOP : VTOP + BY]

    def forward(n):
        def body(half, x, total):
            return (rhs[n, half, x] + total) * inv[half, x]

        def closing(x, sums):
            for half in range(2):
                made = (rhs[n, half, x, HALO : HALO + BY] + sums[half]) * inv[half, x, HALO : HALO + BY]
                if n == NSTEPS - 1:
                    ulast[half, x - HALO] = made
                else:
                    entry[n + 1, half, x, VTOP : VTOP + BY] = made

        sweeps(entry.at[n], JACOBI, body, closing)

    forward(0)
    halo_start(entry.at[1], VTOP, 1)
    take_static(F1)
    take_field(R1)

    def step_one(x):
        for half in range(2):
            rhs[1, half, HALO + x, HALO : HALO + BY] = (
                blk[0, half, x] + static(F1, half, x) * block_of(1, half, x)
            )

    over_x(step_one)
    halo_start(rhs.at[1], HALO, 6)
    obs_pair_in.wait_recv()
    over(SLOTS, lambda p: obs_copy(p, 0).start(), 1)
    over(SLOTS, lambda p: obs_copy(p, 1).start(), 1)
    gather(0)
    halo_wait(entry.at[1], VTOP, 1)
    halo_wait(rhs.at[1], HALO, 6)
    send_field(R2)
    forward(1)
    halo_start(entry.at[2], VTOP, 2)
    take_static(F2)
    take_field(R2)

    def step_two(x):
        for half in range(2):
            rhs[2, half, HALO + x, HALO : HALO + BY] = (
                blk[1, half, x]
                + static(F2, half, x) * block_of(1, half, x)
                + static(F1, half, x) * block_of(2, half, x)
            )

    over_x(step_two)
    halo_start(rhs.at[2], HALO, 7)
    over(SLOTS, lambda p: obs_wait(p, 0), 1)
    over(SLOTS, lambda p: obs_wait(p, 1), 1)
    obs_rows(True).start()
    gather(1)
    halo_wait(entry.at[2], VTOP, 2)
    halo_wait(rhs.at[2], HALO, 7)
    forward(2)

    def back_copy(f, p):
        j = lax.rem(p + slot, SLOTS)
        layers = pl.ds(HALO + 2 * j, 2)
        if f in (POT0, POT1):
            here = entry.at[f + 1, :, layers, pl.ds(VTOP, BY)]
        else:
            here = adj.at[DUAL1 - f, :, layers, pl.ds(HALO, BY)]
        to = bx * SLOTS + j
        return to, remote(here, rx.at[f, gx, mine], gsend.at[f, j], grecv.at[f, 2 * gx + mine], {"space": to})

    def send_back(f):
        begin(f, back_copy)

        def keep():
            layers = pl.ds(HALO + 2 * slot, 2)
            if f in (POT0, POT1):
                rx[f, gx, mine] = entry[f + 1, :, layers, VTOP : VTOP + BY]
            else:
                rx[f, gx, mine] = adj[DUAL1 - f, :, layers, HALO : HALO + BY]

        pl.when(bx == yp)(keep)

    def back_wait(f, q):
        x, t = q // 2, lax.rem(q, 2)
        of = device(yp, x, t)
        here = rx.at[f, x, t]
        copy = remote(here, here, gsend.at[f, q], grecv.at[f, q], {"space": of})
        pl.when(of != space)(copy.wait_recv)

    send_back(POT0)
    send_back(POT1)
    gather(2)
    obs_rows(False).wait_recv()

    def row_copy(p):
        to = lax.rem(gx + p, NXB)
        return remote(part, prx.at[gx], psend.at[0, to], precv.at[0, gx], {"space": device(bx, to, mine)})

    def row_wait(p):
        of = lax.rem(gx + p, NXB)
        remote(part, prx.at[of], psend.at[0, of], precv.at[0, of], {"space": device(bx, of, mine)}).wait_recv()

    over(4, lambda p: row_copy(p).start(), 1)
    prx[gx] = part[...]
    over(4, row_wait, 1)
    res[...] = (prx[0] + prx[1]) + (prx[2] + prx[3])

    def col_copy(p):
        to = lax.rem(bx + p, NB)
        return remote(res, pry.at[bx], psend.at[1, to], precv.at[1, bx], {"space": device(to, gx, mine)})

    def col_wait(p):
        of = lax.rem(bx + p, NB)
        remote(res, pry.at[of], psend.at[1, of], precv.at[1, of], {"space": device(of, gx, mine)}).wait_recv()

    over(4, lambda p: col_copy(p).start(), 1)
    pry[bx] = res[...]
    over(4, col_wait, 1)
    over(4, lambda p: col_copy(p).wait_send(), 1)
    squares = jnp.zeros((1, NDIP), F32)
    for n in range(NSTEPS):
        volts = live[...] * ((pry[0, n] + pry[1, n]) + (pry[2, n] + pry[3, n]))
        part_resid = live[...] * (volts - obs_all[n])
        pry[0, n] = volts
        res[n] = part_resid
        squares = squares + part_resid * part_resid

    own = pl.ds(pl.multiple_of(space * LANES, LANES), LANES)
    other = pl.ds(pl.multiple_of(partner * LANES, LANES), LANES)
    swap = remote(pry.at[0, :, :, other], vswap.at[pl.ds(6, 3)], qsend.at[2], qrecv.at[2], {"space": partner})
    swap.start()
    lanes = squares[:, 0:LANES]
    for j in range(1, NDIP // LANES):
        lanes = lanes + squares[:, j * LANES : (j + 1) * LANES]
    sq[...] = lanes
    pair = remote(sq, sqc, qsend.at[3], qrecv.at[3], {"space": partner})
    pair.start()
    for n in range(NSTEPS):
        volts_out[n, pl.ds(mine, 1), :] = pry[0, n, :, own]
    swap.wait()
    for n in range(NSTEPS):
        volts_out[n, pl.ds(1 - mine, 1), :] = vswap[6 + n]
    pair.wait()
    sqz[tx] = sq[...] + sqc[...]

    def sq_copy(p):
        to = lax.rem(tx + p, 4)
        return remote(sqz.at[tx], sqz.at[tx], tsend.at[2, to], trecv.at[2, tx], {"tx": to})

    def sq_wait(p):
        of = lax.rem(tx + p, 4)
        remote(sqz.at[of], sqz.at[of], tsend.at[2, of], trecv.at[2, of], {"tx": of}).wait_recv()

    over(4, lambda p: sq_copy(p).start(), 1)

    def begin_adjoint(n):
        def body(x):
            for half in range(2):
                field = injected(n, half, x)
                if n == 1:
                    field = field + back[half, x] + static(F1, half, x) * adj[1, half, HALO + x, HALO : HALO + BY]
                scaled = field * inv[half, HALO + x, HALO : HALO + BY]
                adj[n - 1, half, HALO + x, HALO : HALO + BY] = scaled
                entry[5 - n, half, HALO + x, VTOP : VTOP + BY] = scaled

        over_x(body)

    def adjoint(n):
        def body(half, x, total):
            scaled = total * inv[half, x]
            adj[n - 1, half, x] += scaled
            return scaled

        def closing(x, sums):
            for half in range(2):
                back[half, x - HALO] = sums[half]

        sweeps(entry.at[5 - n], JACOBI if n == 2 else JACOBI - 1, body, closing)

    scatter(2)
    begin_adjoint(2)
    halo_start(entry.at[3], VTOP, 3)
    scatter(1)
    halo_wait(entry.at[3], VTOP, 3)
    adjoint(2)
    begin_adjoint(1)
    halo_start(entry.at[4], VTOP, 4)
    halo_wait(entry.at[4], VTOP, 4)
    send_back(DUAL2)
    adjoint(1)
    send_back(DUAL1)

    over(4, sq_wait, 1)
    total = (sqz[0] + sqz[1]) + (sqz[2] + sqz[3])
    misfit = jnp.sqrt(1.0 + jnp.sum(total, axis=1, keepdims=True))
    misfit_out[...] = misfit
    scale = 1.0 / misfit
    for f in (POT0, POT1, DUAL2):
        over(SLOTS, functools.partial(back_wait, f))

    def tx_copy(f, to):
        return remote(rsum.at[f, to], rz.at[f, tx], tsend.at[f, to], trecv.at[f, tx], {"tx": to})

    def tx_wait(f, p):
        of = lax.rem(tx + p, 4)
        remote(rsum.at[f, of], rz.at[f, of], tsend.at[f, of], trecv.at[f, of], {"tx": of}).wait_recv()

    def gradients(i):
        x = lax.rem(gx + i, NXB)
        for t in range(2):
            back_wait(DUAL1, 2 * x + t)
        for half in range(2):
            for layer in range(2):
                at = (half, layer)
                same, cross, tilt = (jnp.zeros((BY, LANES), F32) for _ in range(3))
                for t in range(2):
                    u0, u1, s2, s1 = (rx[(f, x, t) + at] for f in range(4))
                    same = same + (s2 * u1 + s1 * u0)
                    cross = cross + s2 * u0
                    tilt = tilt + (s1 * tilts[(0, t, x) + at] + s2 * tilts[(1, t, x) + at])
                ka0, ka1, kb0, kb1 = (factors[(f, x) + at] for f in range(4))
                rsum[(0, x) + at] = ka0 * same + ka1 * cross
                rsum[(1, x) + at] = tilt - kb0 * same + kb1 * cross

        def give():
            for f in range(2):
                tx_copy(f, x).start()

        def keep():
            for f in range(2):
                rz[f, tx] = rsum[f, x]

        pl.when(x != tx)(give)
        pl.when(x == tx)(keep)

    over(NXB, gradients)
    for f, out in ((0, gc_out), (1, gt_out)):
        over(4, functools.partial(tx_wait, f), 1)
        for half in range(2):
            value = (rz[f, 0, half] + rz[f, 1, half]) + (rz[f, 2, half] + rz[f, 3, half])
            out[:, :, half * LANES : (half + 1) * LANES] = value * scale.reshape(1, 1, 1)

    for f in range(4):
        finish(f, field_copy)
    for f in range(3):
        finish(f, static_copy)
        over(4, lambda p: spread_copy(f, p).wait_send(), 1)
    obs_pair.wait_send()
    for which in range(2):
        over(SLOTS, lambda p: obs_copy(p, which).wait_send(), 1)
    obs_rows(True).wait_send()
    over(4, lambda p: row_copy(p).wait_send(), 1)
    over(4, lambda p: sq_copy(p).wait_send(), 1)
    for f in range(4):
        finish(f, back_copy)
    for f in range(2):
        over(4, lambda p: tx_copy(f, lax.rem(tx + p, 4)).wait_send(), 1)


def on_device(cond, chg, rlx, start, mem, src_cells, dip, counts, obs):
    vmem = pl.BlockSpec(memory_space=pltpu.VMEM)
    whole = pl.BlockSpec(memory_space=pl.ANY)
    smem = pl.BlockSpec(memory_space=pltpu.SMEM)
    field = pltpu.VMEM((2, BX, BY, LANES), F32)
    dma = pltpu.SemaphoreType.DMA
    wide = pltpu.VMEM((2, EX, EY + 2 * PAD, LANES), F32)
    slab = pltpu.VMEM((2, 128, 2 * LANES), F32)
    scratch = [
        slab, slab, slab,
        pltpu.VMEM((2, 2, 128, 2 * LANES), F32),
        pltpu.VMEM((4, 2, 2, 128, 2 * LANES), F32),
        pltpu.VMEM((4, 2, NXB, 2, 2, BY, LANES), F32),
        pltpu.VMEM((3, NXB, 2, 2, BY, LANES), F32),
        pltpu.VMEM((2, 2, NXB, 2, 2, BY, LANES), F32),
        pltpu.VMEM((4, NXB, 2, 2, BY, LANES), F32),
        pltpu.VMEM((2, 2, BX, BY, LANES), F32),
        pltpu.VMEM((3, 2, 2, BX // 2, BY, LANES), F32),
        pltpu.VMEM((5, 2, EX, EY + 2 * PAD, LANES), F32),
        wide, wide,
        pltpu.VMEM((2, EX, EY, LANES), F32),
        pltpu.VMEM((NSTEPS, 2, EX, EY, LANES), F32),
        field,
        pltpu.VMEM((2, 2, EX, EY, LANES), F32),
        field,
        pltpu.VMEM((4 * LANES, ROWS), BF16),
        pltpu.VMEM((2, ROWS, 4 * LANES), F32),
        pltpu.VMEM((NSTEPS, 1, NDIP), F32),
        pltpu.VMEM((NXB, NSTEPS, 1, NDIP), F32),
        pltpu.VMEM((NB, NSTEPS, 1, NDIP), F32),
        pltpu.VMEM((NSTEPS, 1, NDIP), F32),
        pltpu.VMEM((NSTEPS, 1, NDIP), F32),
        pltpu.VMEM((1, NDIP), F32),
        pltpu.VMEM((9, 1, LANES), F32),
        pltpu.VMEM((1, LANES), F32),
        pltpu.VMEM((1, LANES), F32),
        pltpu.VMEM((4, 1, LANES), F32),
        pltpu.VMEM((4, NXB, 2, 2, 2, BY, LANES), F32),
        pltpu.VMEM((2, NXB, 2, 2, BY, LANES), F32),
        pltpu.VMEM((2, 4, 2, 2, BY, LANES), F32),
        dma((5,)),
        dma((4, SLOTS)), dma((4, SLOTS)), dma((3, SLOTS)), dma((3, SLOTS)),
        dma((3, 4)), dma((3, 4)),
        dma((9, 8)), dma((9, 8)),
        dma((2, SLOTS)), dma((2, SLOTS)),
        dma((2, 4)), dma((2, 4)),
        dma((4,)), dma((4,)),
        dma((4, SLOTS)), dma((4, SLOTS)),
        dma((3, 4)), dma((3, 4)),
    ]
    volts, misfit, grad_c, grad_t = pl.pallas_call(
        kernel,
        out_shape=(
            jax.ShapeDtypeStruct((NSTEPS, 2, LANES), F32),
            jax.ShapeDtypeStruct((1, 1), F32),
            jax.ShapeDtypeStruct((2, BY, 2 * LANES), F32),
            jax.ShapeDtypeStruct((2, BY, 2 * LANES), F32),
        ),
        in_specs=[whole, whole, whole, whole, whole, smem, vmem, smem, vmem],
        out_specs=(vmem, vmem, vmem, vmem),
        scratch_shapes=scratch,
        compiler_params=pltpu.CompilerParams(has_side_effects=True, collective_id=0, vmem_limit_bytes=60 << 20),
    )(cond, chg, rlx, start, mem, src_cells, dip, counts, obs)
    return (volts, misfit.reshape(()), grad_c, grad_t)


def solution(mesh):
    placed = (
        P("space", None, None),
        P("space", None, None),
        P("space", None, None),
        P("tx", "space", None, None),
        P(None, "tx", "space", None, None),
        P(None, "tx"),
        P(),
        P(),
        P(None, "tx", "space"),
    )
    return jax.shard_map(
        on_device,
        mesh=mesh,
        in_specs=placed,
        out_specs=(P(None, "tx", "space"), P(), P("space", "tx", None), P("space", "tx", None)),
        check_vma=False,
    )
```

```python
import functools

import jax
import jax.numpy as jnp
from jax import lax
from jax.experimental import pallas as pl
from jax.experimental.pallas import tpu as pltpu
from jax.sharding import PartitionSpec as P

MESH = pl.DeviceIdType.MESH
F32 = jnp.float32
BF16 = jnp.bfloat16
NSTEPS = 3
JACOBI = 8
WEIGHTS = (0.4, 0.3, 0.2, 0.1)
RATIOS = (0.25, 1.0, 4.0, 16.0)
STRENGTH = 4.0

NB, NXB = 4, 4
SLOTS = 8
BX, BY, LANES = 16, 32, 128
HALO = 8
EX, EY = BX + 2 * HALO, BY + 2 * HALO
PAD = 8
VTOP = PAD + HALO
NDIP = 4096
CHUNK = 512
ROWS = BX * BY
UNROLL = 8
U0, R0, R1, R2 = range(4)
COND, F1, F2 = range(3)
KA0, KA1, KB0, KB1 = range(4)
POT0, POT1, DUAL2, DUAL1 = range(4)
SPACES = 32
SIDES = tuple((i, j) for i in (-1, 0, 1) for j in (-1, 0, 1) if (i, j) != (0, 0))


def remote(src, dst, send, recv, device):
    return pltpu.make_async_remote_copy(
        src_ref=src, dst_ref=dst, send_sem=send, recv_sem=recv, device_id=device, device_id_type=MESH
    )


def kernel(
    cond_hbm, chg_hbm, rlx_hbm, start_hbm, mem_hbm, src_cells, dip, counts, obs,
    volts_out, misfit_out, gc_out, gt_out,
    cond, chg, rlx, start, mem,
    perm, hots, stage, sstage, tilts, factors, blk, sblk, entry, va, vb,
    inv, rhs, ulast, adj, back,
    ut, acc, part, prx, pry, res, obs_all, live, vswap, sq, sqc, sqz,
    rx, rsum, rz,
    lsem, fsend, frecv, ssend, srecv, zsend, zrecv, hsend, hrecv, osend, orecv, psend, precv, qsend, qrecv,
    gsend, grecv, tsend, trecv,
):
    space = lax.axis_index("space")
    tx = lax.axis_index("tx")
    yp = space // SLOTS
    slot = lax.rem(space, SLOTS)
    gx = slot // 2
    mine = lax.rem(yp, 2)
    bx = 2 * (yp // 2) + lax.rem(slot, 2)
    partner = (yp + 1 - 2 * mine) * SLOTS + slot

    def device(b, x, t):
        return (2 * (b // 2) + t) * SLOTS + 2 * x + lax.rem(b, 2)

    def over(count, body, first=0):
        def at(p, carry):
            body(p)
            return carry

        lax.fori_loop(first, count, at, 0)

    barrier = pltpu.get_barrier_semaphore()
    loads = [
        pltpu.make_async_copy(a, b, lsem.at[i])
        for i, (a, b) in enumerate(
            ((cond_hbm, cond), (start_hbm, start), (mem_hbm, mem), (chg_hbm, chg), (rlx_hbm, rlx))
        )
    ]
    for load in loads:
        load.start()

    def greet_space(q):
        pl.semaphore_signal(barrier, 1, device_id={"space": lax.rem(space + q, SPACES)}, device_id_type=MESH)

    def greet_tx(q):
        pl.semaphore_signal(barrier, 1, device_id={"tx": lax.rem(tx + q, 4)}, device_id_type=MESH)

    over(SPACES, greet_space, 1)
    over(4, greet_tx, 1)

    def three(value):
        high = value.astype(BF16)
        rest = value - high.astype(F32)
        middle = rest.astype(BF16)
        return high, middle, (rest - middle.astype(F32)).astype(BF16)

    def reorder(value, axis):
        parts = jnp.concatenate(three(value), axis=0)
        moved = lax.dot_general(parts, perm[...], (((1,), (axis,)), ((), ())), preferred_element_type=F32)
        rows = value.shape[0]
        return (moved[:rows] + moved[rows : 2 * rows]) + moved[2 * rows :]

    cell = lax.broadcasted_iota(jnp.int32, (2 * LANES, 2 * LANES), 0)
    goal = lax.broadcasted_iota(jnp.int32, (2 * LANES, 2 * LANES), 1)
    perm[...] = jnp.where(goal == (cell & 1) * LANES + (cell >> 1), 1.0, 0.0).astype(BF16)

    def pieces(body):
        def at(i, carry):
            row, layer = i // 2, lax.rem(i, 2)
            body(row, layer, (layer, pl.ds(pl.multiple_of(row * BY, BY), BY), slice(None)))
            return carry

        lax.fori_loop(0, 2 * NXB, at, 0)

    def first_fields(row, layer, where):
        sources = [cond[where]]
        for t in range(2):
            sources.append(start[(t,) + where])
            sources.append(mem[(0, t) + where] + mem[(1, t) + where] + mem[(2, t) + where] + mem[(3, t) + where])
        moved = reorder(jnp.concatenate(sources, axis=0), 0)
        for half in range(2):
            c, u_a, q_a, u_b, q_b = (
                moved[i * BY : (i + 1) * BY, half * LANES : (half + 1) * LANES] for i in range(5)
            )
            sstage[COND, row, half, layer] = c
            ids = (2 * space + layer) * (128 * 256) + row * (BY * 256) + half
            ids = ids + lax.broadcasted_iota(jnp.int32, (BY, LANES), 0) * 256
            ids = ids + lax.broadcasted_iota(jnp.int32, (BY, LANES), 1) * 2
            for t, (u, q) in enumerate(((u_a, q_a), (u_b, q_b))):
                stage[U0, t, row, half, layer] = u
                source = jnp.where(ids == src_cells[0, t], STRENGTH, 0.0)
                source = source - jnp.where(ids == src_cells[1, t], STRENGTH, 0.0)
                stage[R0, t, row, half, layer] = source + c * q

    def later_fields(row, layer, where):
        sources = [chg[where], rlx[where]] + [mem[(k, t) + where] for t in range(2) for k in range(4)]
        moved = reorder(jnp.concatenate(sources, axis=0), 0)
        for half in range(2):
            later_half(
                row, layer, half,
                [moved[i * BY : (i + 1) * BY, half * LANES : (half + 1) * LANES] for i in range(10)],
            )

    def later_half(row, layer, half, values):
        c, g = sstage[COND, row, half, layer], values[0]
        rate = 1.0 / values[1]
        decays = [jnp.exp(-rate / ratio) for ratio in RATIOS]
        a0, a1, b0, b1 = (jnp.zeros((BY, LANES), F32) for _ in range(4))
        for k in range(4):
            fresh = WEIGHTS[k] * (1.0 - decays[k])
            a0 = a0 + fresh
            a1 = a1 + fresh * decays[k]
            tilt = decays[k] * (WEIGHTS[k] / RATIOS[k])
            b0 = b0 + tilt
            b1 = b1 + tilt * (1.0 - 2.0 * decays[k])
        sstage[F1, row, half, layer] = c * g * a0
        sstage[F2, row, half, layer] = c * g * a1
        factors[KA0, row, half, layer] = c * a0
        factors[KA1, row, half, layer] = c * a1
        factors[KB0, row, half, layer] = c * g * rate * rate * b0
        factors[KB1, row, half, layer] = c * g * rate * rate * b1
        for t in range(2):
            first, second, slope, slope_d = (jnp.zeros((BY, LANES), F32) for _ in range(4))
            for k in range(4):
                scaled = decays[k] * values[2 + 4 * t + k]
                first = first + scaled
                second = second + decays[k] * scaled
                tilt = scaled * (1.0 / RATIOS[k])
                slope = slope + tilt
                slope_d = slope_d + decays[k] * tilt
            stage[R1, t, row, half, layer] = c * first
            stage[R2, t, row, half, layer] = c * second
            tilts[0, t, row, half, layer] = c * rate * rate * slope
            tilts[1, t, row, half, layer] = 2.0 * c * rate * rate * slope_d

    def landing(f, j):
        layers = pl.ds(HALO + 2 * j, 2)
        if f == U0:
            return entry.at[0, :, layers, pl.ds(VTOP, BY)]
        if f == R0:
            return rhs.at[0, :, layers, pl.ds(HALO, BY)]
        return blk.at[f - R1, :, pl.ds(2 * j, 2)]

    def target(p):
        q = lax.rem(p + slot, SLOTS)
        return q // 2, lax.rem(q, 2), q, device(yp, q // 2, lax.rem(q, 2))

    def field_copy(f, p):
        x, t, q, to = target(p)
        return to, remote(stage.at[f, t, x], landing(f, slot), fsend.at[f, q], frecv.at[f, slot], {"space": to})

    def static_copy(f, p):
        x, t, q, to = target(p)
        quarter = (tx // 2, lax.rem(tx, 2))
        return to, remote(
            sstage.at[(f, x) + quarter], sblk.at[(f,) + quarter + (slot,)], ssend.at[f, q], srecv.at[f, slot], {"space": to}
        )

    def begin(f, copy_of):
        def one(p):
            to, copy = copy_of(f, p)
            pl.when(to != space)(copy.start)

        over(SLOTS, one)

    def finish(f, copy_of):
        def one(p):
            to, copy = copy_of(f, p)
            pl.when(to != space)(copy.wait_send)

        over(SLOTS, one)

    def send_field(f):
        begin(f, field_copy)

        def keep():
            if f == U0:
                entry[0, :, pl.ds(HALO + 2 * slot, 2), VTOP : VTOP + BY] = stage[f, mine, gx]
            elif f == R0:
                rhs[0, :, pl.ds(HALO + 2 * slot, 2), HALO : HALO + BY] = stage[f, mine, gx]
            else:
                blk[f - R1, :, pl.ds(2 * slot, 2)] = stage[f, mine, gx]

        pl.when(bx == yp)(keep)

    def send_static(f):
        begin(f, static_copy)

        def keep():
            sblk[f, tx // 2, lax.rem(tx, 2), slot] = sstage[f, gx, tx // 2, lax.rem(tx, 2)]

        pl.when(bx == yp)(keep)

    def take_field(f):
        def one(j):
            here = landing(f, j)
            of = bx * SLOTS + j
            copy = remote(here, here, fsend.at[f, j], frecv.at[f, j], {"space": of})
            pl.when(of != space)(copy.wait_recv)

        over(SLOTS, one)

    def spread_copy(f, p):
        to = lax.rem(tx + p, 4)
        quarter = sblk.at[f, tx // 2, lax.rem(tx, 2)]
        return remote(quarter, quarter, zsend.at[f, to], zrecv.at[f, tx], {"tx": to})

    def spread_static(f):
        def one(j):
            here = sblk.at[f, tx // 2, lax.rem(tx, 2), j]
            of = bx * SLOTS + j
            copy = remote(here, here, ssend.at[f, j], srecv.at[f, j], {"space": of})
            pl.when(of != space)(copy.wait_recv)

        over(SLOTS, one)
        over(4, lambda p: spread_copy(f, p).start(), 1)

    def take_static(f):
        def one(p):
            of = lax.rem(tx + p, 4)
            quarter = sblk.at[f, of // 2, lax.rem(of, 2)]
            remote(quarter, quarter, zsend.at[f, of], zrecv.at[f, of], {"tx": of}).wait_recv()

        over(4, one, 1)

    def static(f, half, x):
        return sblk[f, half, lax.rem(x, 2), x // 2]

    for load in loads[:3]:
        load.wait()
    pieces(first_fields)

    def clear(ref, index):
        shape = ref.at[index].shape
        ref[index] = jnp.zeros(shape, F32)

    def clear_pads(x):
        for ref in (va, vb):
            for half in range(2):
                clear(ref, (half, x, pl.ds(0, PAD)))
                clear(ref, (half, x, pl.ds(PAD + EY, PAD)))
        for k in range(5):
            for half in range(2):
                clear(entry, (k, half, x, pl.ds(0, PAD)))
                clear(entry, (k, half, x, pl.ds(PAD + EY, PAD)))

    over(EX, clear_pads)

    def clear_rows(low):
        def one(x):
            for half in range(2):
                at = 0 if low else HALO + BY
                for k in range(5):
                    clear(entry, (k, half, x, pl.ds(PAD + at, HALO)))
                for n in range(NSTEPS):
                    clear(rhs, (n, half, x, pl.ds(at, HALO)))
                clear(inv, (half, x, pl.ds(at, HALO)))

        over(EX, one)

    def clear_layers(low):
        def one(i):
            x = i if low else i + HALO + BX
            for half in range(2):
                for k in range(5):
                    clear(entry, (k, half, x, pl.ds(PAD, EY)))
                for n in range(NSTEPS):
                    clear(rhs, (n, half, x))
                clear(inv, (half, x))

        over(HALO, one)

    pl.when(gx == 0)(lambda: clear_rows(True))
    pl.when(gx == NXB - 1)(lambda: clear_rows(False))
    pl.when(bx == 0)(lambda: clear_layers(True))
    pl.when(bx == NB - 1)(lambda: clear_layers(False))

    pl.semaphore_wait(barrier, SPACES + 2)
    send_static(COND)
    send_field(U0)
    send_field(R0)

    def slab_lanes(s, count=1):
        return pl.ds(pl.multiple_of(s * LANES, LANES), count * LANES)

    for t in range(2):
        for n in range(NSTEPS):
            vswap[3 * t + n] = obs[n, t : t + 1, :]
    obs_pair = remote(
        vswap.at[pl.ds(3 * (1 - mine), 3)], obs_all.at[:, :, slab_lanes(space)], qsend.at[0], qrecv.at[0], {"space": partner}
    )
    obs_pair_in = remote(
        vswap.at[pl.ds(3 * (1 - mine), 3)], obs_all.at[:, :, slab_lanes(partner)], qsend.at[0], qrecv.at[0], {"space": partner}
    )
    obs_pair.start()
    obs_all[:, :, slab_lanes(space)] = vswap[pl.ds(3 * mine, 3)]

    def obs_copy(p, which):
        to = lax.rem(slot + p, SLOTS)
        here = obs_all.at[:, :, slab_lanes(space if which == 0 else partner)]
        return remote(here, here, osend.at[which, to], orecv.at[which, slot], {"space": yp * SLOTS + to})

    def obs_wait(p, which):
        of = lax.rem(slot + p, SLOTS)
        row = yp if which == 0 else yp + 1 - 2 * mine
        here = obs_all.at[:, :, slab_lanes(row * SLOTS + of)]
        remote(here, here, osend.at[which, of], orecv.at[which, of], {"space": yp * SLOTS + of}).wait_recv()

    def obs_rows(own):
        half = yp // 2 if own else 1 - yp // 2
        here = obs_all.at[:, :, slab_lanes(2 * half * SLOTS, 2 * SLOTS)]
        return remote(here, here, qsend.at[1], qrecv.at[1], {"space": lax.rem(space + 2 * SLOTS, NB * SLOTS)})

    lane_ids = lax.broadcasted_iota(jnp.int32, (1, LANES), 1)

    def live_at(j, carry):
        live[:, pl.ds(pl.multiple_of(j * LANES, LANES), LANES)] = jnp.where(lane_ids < counts[j], 1.0, 0.0)
        return carry

    lax.fori_loop(0, NB * SLOTS, live_at, 0)

    def halo(ref, top, which):
        width = HALO if top == VTOP else HALO - 1
        copies = []
        for side, (i, j) in enumerate(SIDES):
            deep = width if j == 0 else width - 1
            layers = {-1: (HALO, deep, HALO + BX), 1: (HALO + BX - deep, deep, HALO - deep), 0: (HALO, BX, HALO)}[i]
            rows = {-1: (top, HALO, top + BY), 1: (top + BY - HALO, HALO, top - HALO), 0: (top, BY, top)}[j]
            sends = (bx + i >= 0) & (bx + i < NB) & (gx + j >= 0) & (gx + j < NXB)
            takes = (bx - i >= 0) & (bx - i < NB) & (gx - j >= 0) & (gx - j < NXB)
            to = device(lax.rem(bx + i + NB, NB), lax.rem(gx + j + NXB, NXB), mine)
            copies.append((sends, takes, remote(
                ref.at[:, pl.ds(layers[0], layers[1]), pl.ds(rows[0], rows[1])],
                ref.at[:, pl.ds(layers[2], layers[1]), pl.ds(rows[2], rows[1])],
                hsend.at[which, side], hrecv.at[which, side], {"space": to},
            )))
        return copies

    def halo_start(ref, top, which):
        for sends, _, copy in halo(ref, top, which):
            pl.when(sends)(copy.start)

    def halo_wait(ref, top, which):
        for sends, takes, copy in halo(ref, top, which):
            pl.when(takes)(copy.wait_recv)
            pl.when(sends)(copy.wait_send)

    def over_x(body, unroll=1):
        def at(x, carry):
            body(x)
            return carry

        lax.fori_loop(0, BX, at, 0, unroll=unroll)

    def neighbour_sums(ref, x, top, rows):
        c0 = ref[0, x, top : top + rows]
        c1 = ref[1, x, top : top + rows]
        lane = lax.broadcasted_iota(jnp.int32, (rows, LANES), 1)
        z0 = c1 + jnp.where(lane == 0, 0.0, pltpu.roll(c1, 1, 1))
        z1 = c0 + jnp.where(lane == LANES - 1, 0.0, pltpu.roll(c0, LANES - 1, 1))
        sums = []
        for half, z in ((0, z0), (1, z1)):
            total = ref[half, x + 1, top : top + rows] + ref[half, x - 1, top : top + rows]
            total = total + ref[half, x, top + 1 : top + rows + 1] + ref[half, x, top - 1 : top + rows - 1]
            sums.append(total + z)
        return sums

    def sweeps(first, last, body, closing):
        source = first
        for s in range(1, last + 1):
            goal = va if s % 2 else vb
            if s == HALO:
                def one(x, carry, source=source):
                    closing(x, neighbour_sums(source, x, VTOP, BY))
                    return carry
            else:
                def one(x, carry, source=source, goal=goal):
                    sums = neighbour_sums(source, x, PAD, EY)
                    for half in range(2):
                        goal[half, x, PAD : PAD + EY] = body(half, x, sums[half])
                    return carry
            lax.fori_loop(s, EX - s, one, 0, unroll=UNROLL)
            source = goal

    def depth_of(sign, k):
        z = dip[sign : sign + 1, pl.ds(pl.multiple_of(k * CHUNK, CHUNK), CHUNK)] & 255
        return lax.broadcasted_iota(jnp.int32, (2 * LANES, CHUNK), 0) == (z & 1) * LANES + (z >> 1)

    def mark_rows(k):
        for sign in range(2):
            cells = dip[sign : sign + 1, pl.ds(pl.multiple_of(k * CHUNK, CHUNK), CHUNK)]
            x, y = cells >> 15, (cells >> 8) & 127
            own = ((x >> 4) == bx) & ((y >> 5) == gx)
            row = jnp.where(own, (x & 15) * BY + (y & 31), -1)
            hot = lax.broadcasted_iota(jnp.int32, (ROWS, CHUNK), 0) == row
            hots[sign, k] = jnp.where(hot, 1.0, 0.0).astype(BF16)

    def potential(n, half):
        if n == NSTEPS - 1:
            return ulast[half]
        return entry[n + 1, half, HALO : HALO + BX, VTOP : VTOP + BY]

    def gather(n):
        for half in range(2):
            rows = potential(n, half).reshape(ROWS, LANES).T
            high = rows.astype(BF16)
            ut[half * LANES : (half + 1) * LANES, :] = high
            ut[(2 + half) * LANES : (3 + half) * LANES, :] = (rows - high.astype(F32)).astype(BF16)

        def at(k, carry):
            found = []
            for sign in range(2):
                both = jnp.dot(ut[...], hots[sign, k], preferred_element_type=F32)
                value = both[: 2 * LANES] + both[2 * LANES :]
                found.append(jnp.sum(jnp.where(depth_of(sign, k), value, 0.0), axis=0, keepdims=True))
            part[n, :, pl.ds(pl.multiple_of(k * CHUNK, CHUNK), CHUNK)] = found[0] - found[1]
            return carry

        lax.fori_loop(0, NDIP // CHUNK, at, 0)

    def scatter(n):
        acc[n - 1] = jnp.zeros((ROWS, 4 * LANES), F32)

        def at(k, carry):
            value = res[n, :, pl.ds(pl.multiple_of(k * CHUNK, CHUNK), CHUNK)]
            for sign in range(2):
                placed = jnp.where(depth_of(sign, k), value if sign == 0 else -value, 0.0)
                high = placed.astype(BF16)
                low = (placed - high.astype(F32)).astype(BF16)
                acc[n - 1] += lax.dot_general(
                    hots[sign, k], jnp.concatenate([high, low], axis=0), (((1,), (1,)), ((), ())), preferred_element_type=F32
                )
            return carry

        lax.fori_loop(0, NDIP // CHUNK, at, 0)

    def injected(n, half, x):
        rows = pl.ds(pl.multiple_of(x * BY, BY), BY)
        return (
            acc[n - 1, rows, half * LANES : (half + 1) * LANES]
            + acc[n - 1, rows, (2 + half) * LANES : (3 + half) * LANES]
        )

    def row_copy(n, p):
        to = lax.rem(gx + p, NXB)
        return remote(
            part.at[n], prx.at[gx, n], psend.at[0, n, to], precv.at[0, n, gx], {"space": device(bx, to, mine)}
        )

    def row_wait(n, p):
        of = lax.rem(gx + p, NXB)
        here = prx.at[of, n]
        remote(here, here, psend.at[0, n, of], precv.at[0, n, of], {"space": device(bx, of, mine)}).wait_recv()

    def row_copies(n):
        over(4, lambda p: row_copy(n, p).start(), 1)
        prx[gx, n] = part[n]

    def row_sums(n):
        over(4, functools.partial(row_wait, n), 1)
        res[n] = (prx[0, n] + prx[1, n]) + (prx[2, n] + prx[3, n])

    def col_copy(n, p):
        to = lax.rem(bx + p, NB)
        return remote(
            res.at[n], pry.at[bx, n], psend.at[1, n, to], precv.at[1, n, bx], {"space": device(to, gx, mine)}
        )

    def col_wait(n, p):
        of = lax.rem(bx + p, NB)
        here = pry.at[of, n]
        remote(here, here, psend.at[1, n, of], precv.at[1, n, of], {"space": device(of, gx, mine)}).wait_recv()

    def col_copies(n):
        over(4, lambda p: col_copy(n, p).start(), 1)
        pry[bx, n] = res[n]

    spread_static(COND)
    for load in loads[3:]:
        load.wait()
    pieces(later_fields)
    over(NDIP // CHUNK, mark_rows)
    take_field(U0)
    halo_start(entry.at[0], VTOP, 0)
    take_static(COND)

    def inverse(x):
        for half in range(2):
            inv[half, HALO + x, HALO : HALO + BY] = 1.0 / (6.0 + static(COND, half, x))

    over_x(inverse)
    halo_start(inv, HALO, 8)
    take_field(R0)
    halo_start(rhs.at[0], HALO, 5)
    send_static(F1)
    halo_wait(entry.at[0], VTOP, 0)
    halo_wait(inv, HALO, 8)
    halo_wait(rhs.at[0], HALO, 5)
    send_field(R1)
    send_static(F2)
    spread_static(F1)

    def block_of(k, half, x):
        return entry[k, half, HALO + x, VTOP : VTOP + BY]

    def forward(n):
        def body(half, x, total):
            return (rhs[n, half, x] + total) * inv[half, x]

        def closing(x, sums):
            for half in range(2):
                made = (rhs[n, half, x, HALO : HALO + BY] + sums[half]) * inv[half, x, HALO : HALO + BY]
                if n == NSTEPS - 1:
                    ulast[half, x - HALO] = made
                else:
                    entry[n + 1, half, x, VTOP : VTOP + BY] = made

        sweeps(entry.at[n], JACOBI, body, closing)

    forward(0)
    halo_start(entry.at[1], VTOP, 1)
    take_static(F1)
    take_field(R1)

    def step_one(x):
        for half in range(2):
            rhs[1, half, HALO + x, HALO : HALO + BY] = (
                blk[0, half, x] + static(F1, half, x) * block_of(1, half, x)
            )

    over_x(step_one)
    halo_start(rhs.at[1], HALO, 6)
    spread_static(F2)
    obs_pair_in.wait_recv()
    over(SLOTS, lambda p: obs_copy(p, 0).start(), 1)
    over(SLOTS, lambda p: obs_copy(p, 1).start(), 1)
    gather(0)
    row_copies(0)
    halo_wait(entry.at[1], VTOP, 1)
    halo_wait(rhs.at[1], HALO, 6)
    send_field(R2)
    forward(1)
    halo_start(entry.at[2], VTOP, 2)
    take_static(F2)
    take_field(R2)

    def step_two(x):
        for half in range(2):
            rhs[2, half, HALO + x, HALO : HALO + BY] = (
                blk[1, half, x]
                + static(F2, half, x) * block_of(1, half, x)
                + static(F1, half, x) * block_of(2, half, x)
            )

    over_x(step_two)
    halo_start(rhs.at[2], HALO, 7)
    over(SLOTS, lambda p: obs_wait(p, 0), 1)
    over(SLOTS, lambda p: obs_wait(p, 1), 1)
    obs_rows(True).start()
    gather(1)
    row_copies(1)
    row_sums(0)
    col_copies(0)
    halo_wait(entry.at[2], VTOP, 2)
    halo_wait(rhs.at[2], HALO, 7)
    forward(2)

    def back_copy(f, p):
        j = lax.rem(p + slot, SLOTS)
        layers = pl.ds(HALO + 2 * j, 2)
        if f in (POT0, POT1):
            here = entry.at[f + 1, :, layers, pl.ds(VTOP, BY)]
        else:
            here = adj.at[DUAL1 - f, :, layers, pl.ds(HALO, BY)]
        to = bx * SLOTS + j
        return to, remote(here, rx.at[f, gx, mine], gsend.at[f, j], grecv.at[f, 2 * gx + mine], {"space": to})

    def send_back(f):
        begin(f, back_copy)

        def keep():
            layers = pl.ds(HALO + 2 * slot, 2)
            if f in (POT0, POT1):
                rx[f, gx, mine] = entry[f + 1, :, layers, VTOP : VTOP + BY]
            else:
                rx[f, gx, mine] = adj[DUAL1 - f, :, layers, HALO : HALO + BY]

        pl.when(bx == yp)(keep)

    def back_wait(f, q):
        x, t = q // 2, lax.rem(q, 2)
        of = device(yp, x, t)
        here = rx.at[f, x, t]
        copy = remote(here, here, gsend.at[f, q], grecv.at[f, q], {"space": of})
        pl.when(of != space)(copy.wait_recv)

    send_back(POT0)
    send_back(POT1)
    gather(2)
    obs_rows(False).wait_recv()

    row_copies(2)
    row_sums(1)
    col_copies(1)
    row_sums(2)
    col_copies(2)
    for n in range(NSTEPS):
        over(4, functools.partial(col_wait, n), 1)
        over(4, lambda p: col_copy(n, p).wait_send(), 1)
    squares = jnp.zeros((1, NDIP), F32)
    for n in range(NSTEPS):
        volts = live[...] * ((pry[0, n] + pry[1, n]) + (pry[2, n] + pry[3, n]))
        part_resid = live[...] * (volts - obs_all[n])
        pry[0, n] = volts
        res[n] = part_resid
        squares = squares + part_resid * part_resid

    own = pl.ds(pl.multiple_of(space * LANES, LANES), LANES)
    other = pl.ds(pl.multiple_of(partner * LANES, LANES), LANES)
    swap = remote(pry.at[0, :, :, other], vswap.at[pl.ds(6, 3)], qsend.at[2], qrecv.at[2], {"space": partner})
    swap.start()
    lanes = squares[:, 0:LANES]
    for j in range(1, NDIP // LANES):
        lanes = lanes + squares[:, j * LANES : (j + 1) * LANES]
    sq[...] = lanes
    pair = remote(sq, sqc, qsend.at[3], qrecv.at[3], {"space": partner})
    pair.start()
    for n in range(NSTEPS):
        volts_out[n, pl.ds(mine, 1), :] = pry[0, n, :, own]
    swap.wait()
    for n in range(NSTEPS):
        volts_out[n, pl.ds(1 - mine, 1), :] = vswap[6 + n]
    pair.wait()
    sqz[tx] = sq[...] + sqc[...]

    def sq_copy(p):
        to = lax.rem(tx + p, 4)
        return remote(sqz.at[tx], sqz.at[tx], tsend.at[2, to], trecv.at[2, tx], {"tx": to})

    def sq_wait(p):
        of = lax.rem(tx + p, 4)
        remote(sqz.at[of], sqz.at[of], tsend.at[2, of], trecv.at[2, of], {"tx": of}).wait_recv()

    over(4, lambda p: sq_copy(p).start(), 1)

    def begin_adjoint(n):
        def body(x):
            for half in range(2):
                field = injected(n, half, x)
                if n == 1:
                    field = field + back[half, x] + static(F1, half, x) * adj[1, half, HALO + x, HALO : HALO + BY]
                scaled = field * inv[half, HALO + x, HALO : HALO + BY]
                adj[n - 1, half, HALO + x, HALO : HALO + BY] = scaled
                entry[5 - n, half, HALO + x, VTOP : VTOP + BY] = scaled

        over_x(body)

    def adjoint(n):
        def body(half, x, total):
            scaled = total * inv[half, x]
            adj[n - 1, half, x] += scaled
            return scaled

        def closing(x, sums):
            for half in range(2):
                back[half, x - HALO] = sums[half]

        sweeps(entry.at[5 - n], JACOBI if n == 2 else JACOBI - 1, body, closing)

    scatter(2)
    begin_adjoint(2)
    halo_start(entry.at[3], VTOP, 3)
    scatter(1)
    halo_wait(entry.at[3], VTOP, 3)
    adjoint(2)
    begin_adjoint(1)
    halo_start(entry.at[4], VTOP, 4)
    halo_wait(entry.at[4], VTOP, 4)
    send_back(DUAL2)
    adjoint(1)
    send_back(DUAL1)

    over(4, sq_wait, 1)
    total = (sqz[0] + sqz[1]) + (sqz[2] + sqz[3])
    misfit = jnp.sqrt(1.0 + jnp.sum(total, axis=1, keepdims=True))
    misfit_out[...] = misfit
    scale = 1.0 / misfit
    for f in (POT0, POT1, DUAL2):
        over(SLOTS, functools.partial(back_wait, f))

    def tx_copy(f, to):
        return remote(rsum.at[f, to], rz.at[f, tx], tsend.at[f, to], trecv.at[f, tx], {"tx": to})

    def tx_wait(f, p):
        of = lax.rem(tx + p, 4)
        remote(rsum.at[f, of], rz.at[f, of], tsend.at[f, of], trecv.at[f, of], {"tx": of}).wait_recv()

    def gradients(i):
        x = lax.rem(gx + i, NXB)
        for t in range(2):
            back_wait(DUAL1, 2 * x + t)
        for half in range(2):
            for layer in range(2):
                at = (half, layer)
                same, cross, tilt = (jnp.zeros((BY, LANES), F32) for _ in range(3))
                for t in range(2):
                    u0, u1, s2, s1 = (rx[(f, x, t) + at] for f in range(4))
                    same = same + (s2 * u1 + s1 * u0)
                    cross = cross + s2 * u0
                    tilt = tilt + (s1 * tilts[(0, t, x) + at] + s2 * tilts[(1, t, x) + at])
                ka0, ka1, kb0, kb1 = (factors[(f, x) + at] for f in range(4))
                rsum[(0, x) + at] = ka0 * same + ka1 * cross
                rsum[(1, x) + at] = tilt - kb0 * same + kb1 * cross

        def give():
            for f in range(2):
                tx_copy(f, x).start()

        def keep():
            for f in range(2):
                rz[f, tx] = rsum[f, x]

        pl.when(x != tx)(give)
        pl.when(x == tx)(keep)

    over(NXB, gradients)
    for f, out in ((0, gc_out), (1, gt_out)):
        over(4, functools.partial(tx_wait, f), 1)
        halves = [(rz[f, 0, half] + rz[f, 1, half]) + (rz[f, 2, half] + rz[f, 3, half]) for half in range(2)]
        value = reorder(jnp.concatenate([half.reshape(2 * BY, LANES) for half in halves], axis=1), 1)
        out[...] = value.reshape(2, BY, 2 * LANES) * scale.reshape(1, 1, 1)

    for f in range(4):
        finish(f, field_copy)
    for f in range(3):
        finish(f, static_copy)
        over(4, lambda p: spread_copy(f, p).wait_send(), 1)
    obs_pair.wait_send()
    for which in range(2):
        over(SLOTS, lambda p: obs_copy(p, which).wait_send(), 1)
    obs_rows(True).wait_send()
    for n in range(NSTEPS):
        over(4, lambda p: row_copy(n, p).wait_send(), 1)
    over(4, lambda p: sq_copy(p).wait_send(), 1)
    for f in range(4):
        finish(f, back_copy)
    for f in range(2):
        over(4, lambda p: tx_copy(f, lax.rem(tx + p, 4)).wait_send(), 1)


def on_device(cond, chg, rlx, start, mem, src_cells, dip, counts, obs):
    vmem = pl.BlockSpec(memory_space=pltpu.VMEM)
    whole = pl.BlockSpec(memory_space=pl.ANY)
    smem = pl.BlockSpec(memory_space=pltpu.SMEM)
    field = pltpu.VMEM((2, BX, BY, LANES), F32)
    dma = pltpu.SemaphoreType.DMA
    wide = pltpu.VMEM((2, EX, EY + 2 * PAD, LANES), F32)
    slab = pltpu.VMEM((2, 128, 2 * LANES), F32)
    scratch = [
        slab, slab, slab,
        pltpu.VMEM((2, 2, 128, 2 * LANES), F32),
        pltpu.VMEM((4, 2, 2, 128, 2 * LANES), F32),
        pltpu.VMEM((2 * LANES, 2 * LANES), BF16),
        pltpu.VMEM((2, NDIP // CHUNK, ROWS, CHUNK), BF16),
        pltpu.VMEM((4, 2, NXB, 2, 2, BY, LANES), F32),
        pltpu.VMEM((3, NXB, 2, 2, BY, LANES), F32),
        pltpu.VMEM((2, 2, NXB, 2, 2, BY, LANES), F32),
        pltpu.VMEM((4, NXB, 2, 2, BY, LANES), F32),
        pltpu.VMEM((2, 2, BX, BY, LANES), F32),
        pltpu.VMEM((3, 2, 2, BX // 2, BY, LANES), F32),
        pltpu.VMEM((5, 2, EX, EY + 2 * PAD, LANES), F32),
        wide, wide,
        pltpu.VMEM((2, EX, EY, LANES), F32),
        pltpu.VMEM((NSTEPS, 2, EX, EY, LANES), F32),
        field,
        pltpu.VMEM((2, 2, EX, EY, LANES), F32),
        field,
        pltpu.VMEM((4 * LANES, ROWS), BF16),
        pltpu.VMEM((2, ROWS, 4 * LANES), F32),
        pltpu.VMEM((NSTEPS, 1, NDIP), F32),
        pltpu.VMEM((NXB, NSTEPS, 1, NDIP), F32),
        pltpu.VMEM((NB, NSTEPS, 1, NDIP), F32),
        pltpu.VMEM((NSTEPS, 1, NDIP), F32),
        pltpu.VMEM((NSTEPS, 1, NDIP), F32),
        pltpu.VMEM((1, NDIP), F32),
        pltpu.VMEM((9, 1, LANES), F32),
        pltpu.VMEM((1, LANES), F32),
        pltpu.VMEM((1, LANES), F32),
        pltpu.VMEM((4, 1, LANES), F32),
        pltpu.VMEM((4, NXB, 2, 2, 2, BY, LANES), F32),
        pltpu.VMEM((2, NXB, 2, 2, BY, LANES), F32),
        pltpu.VMEM((2, 4, 2, 2, BY, LANES), F32),
        dma((5,)),
        dma((4, SLOTS)), dma((4, SLOTS)), dma((3, SLOTS)), dma((3, SLOTS)),
        dma((3, 4)), dma((3, 4)),
        dma((9, 8)), dma((9, 8)),
        dma((2, SLOTS)), dma((2, SLOTS)),
        dma((2, NSTEPS, 4)), dma((2, NSTEPS, 4)),
        dma((4,)), dma((4,)),
        dma((4, SLOTS)), dma((4, SLOTS)),
        dma((3, 4)), dma((3, 4)),
    ]
    volts, misfit, grad_c, grad_t = pl.pallas_call(
        kernel,
        out_shape=(
            jax.ShapeDtypeStruct((NSTEPS, 2, LANES), F32),
            jax.ShapeDtypeStruct((1, 1), F32),
            jax.ShapeDtypeStruct((2, BY, 2 * LANES), F32),
            jax.ShapeDtypeStruct((2, BY, 2 * LANES), F32),
        ),
        in_specs=[whole, whole, whole, whole, whole, smem, vmem, smem, vmem],
        out_specs=(vmem, vmem, vmem, vmem),
        scratch_shapes=scratch,
        compiler_params=pltpu.CompilerParams(has_side_effects=True, collective_id=0, vmem_limit_bytes=60 << 20),
    )(cond, chg, rlx, start, mem, src_cells, dip, counts, obs)
    return (volts, misfit.reshape(()), grad_c, grad_t)


def solution(mesh):
    placed = (
        P("space", None, None),
        P("space", None, None),
        P("space", None, None),
        P("tx", "space", None, None),
        P(None, "tx", "space", None, None),
        P(None, "tx"),
        P(),
        P(),
        P(None, "tx", "space"),
    )
    return jax.shard_map(
        on_device,
        mesh=mesh,
        in_specs=placed,
        out_specs=(P(None, "tx", "space"), P(), P("space", "tx", None), P("space", "tx", None)),
        check_vma=False,
    )
```

```python
import functools

import jax
import jax.numpy as jnp
from jax import lax
from jax.experimental import pallas as pl
from jax.experimental.pallas import tpu as pltpu
from jax.sharding import PartitionSpec as P

MESH = pl.DeviceIdType.MESH
F32 = jnp.float32
BF16 = jnp.bfloat16
NSTEPS = 3
JACOBI = 8
WEIGHTS = (0.4, 0.3, 0.2, 0.1)
RATIOS = (0.25, 1.0, 4.0, 16.0)
STRENGTH = 4.0

NB, NXB = 4, 4
SLOTS = 8
BX, BY, LANES = 16, 32, 128
HALO = 8
EX, EY = BX + 2 * HALO, BY + 2 * HALO
PAD = 8
VTOP = PAD + HALO
NDIP = 4096
CHUNK = 512
HALF = NDIP // 2
HALF_CHUNKS = HALF // CHUNK
ROWS = BX * BY
UNROLL = 8
U0, R0, R1, R2 = range(4)
COND, F1, F2 = range(3)
KA0, KA1, KB0, KB1 = range(4)
POT0, POT1, DUAL2, DUAL1 = range(4)
SPACES = 32
SIDES = tuple((i, j) for i in (-1, 0, 1) for j in (-1, 0, 1) if (i, j) != (0, 0))


def remote(src, dst, send, recv, device):
    return pltpu.make_async_remote_copy(
        src_ref=src, dst_ref=dst, send_sem=send, recv_sem=recv, device_id=device, device_id_type=MESH
    )


def kernel(
    cond_hbm, chg_hbm, rlx_hbm, start_hbm, mem_hbm, src_cells, dip, counts, obs,
    volts_out, misfit_out, gc_out, gt_out,
    cond, chg, rlx, start, mem,
    perm, hots, stage, sstage, tilts, factors, blk, sblk, entry, va, vb,
    inv, rhs, ulast, adj, back,
    ut, acc, part, prx, pry, rows, volts, res, obs_all, live, vswap, sq, sqc, sqz,
    rx, rsum, rz,
    lsem, fsend, frecv, ssend, srecv, zsend, zrecv, hsend, hrecv, osend, orecv, psend, precv, qsend, qrecv,
    gsend, grecv, tsend, trecv,
):
    space = lax.axis_index("space")
    tx = lax.axis_index("tx")
    yp = space // SLOTS
    slot = lax.rem(space, SLOTS)
    gx = slot // 2
    mine = lax.rem(yp, 2)
    bx = 2 * (yp // 2) + lax.rem(slot, 2)
    partner = (yp + 1 - 2 * mine) * SLOTS + slot

    def device(b, x, t):
        return (2 * (b // 2) + t) * SLOTS + 2 * x + lax.rem(b, 2)

    def over(count, body, first=0):
        def at(p, carry):
            body(p)
            return carry

        lax.fori_loop(first, count, at, 0)

    barrier = pltpu.get_barrier_semaphore()
    loads = [
        pltpu.make_async_copy(a, b, lsem.at[i])
        for i, (a, b) in enumerate(
            ((cond_hbm, cond), (start_hbm, start), (mem_hbm, mem), (chg_hbm, chg), (rlx_hbm, rlx))
        )
    ]
    for load in loads:
        load.start()

    def greet_space(q):
        pl.semaphore_signal(barrier, 1, device_id={"space": lax.rem(space + q, SPACES)}, device_id_type=MESH)

    def greet_tx(q):
        pl.semaphore_signal(barrier, 1, device_id={"tx": lax.rem(tx + q, 4)}, device_id_type=MESH)

    over(SPACES, greet_space, 1)
    over(4, greet_tx, 1)

    def three(value):
        high = value.astype(BF16)
        rest = value - high.astype(F32)
        middle = rest.astype(BF16)
        return high, middle, (rest - middle.astype(F32)).astype(BF16)

    def reorder(value, axis):
        parts = jnp.concatenate(three(value), axis=0)
        moved = lax.dot_general(parts, perm[...], (((1,), (axis,)), ((), ())), preferred_element_type=F32)
        rows = value.shape[0]
        return (moved[:rows] + moved[rows : 2 * rows]) + moved[2 * rows :]

    cell = lax.broadcasted_iota(jnp.int32, (2 * LANES, 2 * LANES), 0)
    goal = lax.broadcasted_iota(jnp.int32, (2 * LANES, 2 * LANES), 1)
    perm[...] = jnp.where(goal == (cell & 1) * LANES + (cell >> 1), 1.0, 0.0).astype(BF16)

    def pieces(body):
        def at(i, carry):
            row, layer = i // 2, lax.rem(i, 2)
            body(row, layer, (layer, pl.ds(pl.multiple_of(row * BY, BY), BY), slice(None)))
            return carry

        lax.fori_loop(0, 2 * NXB, at, 0)

    def first_fields(row, layer, where):
        sources = [cond[where]]
        for t in range(2):
            sources.append(start[(t,) + where])
            sources.append(mem[(0, t) + where] + mem[(1, t) + where] + mem[(2, t) + where] + mem[(3, t) + where])
        moved = reorder(jnp.concatenate(sources, axis=0), 0)
        for half in range(2):
            c, u_a, q_a, u_b, q_b = (
                moved[i * BY : (i + 1) * BY, half * LANES : (half + 1) * LANES] for i in range(5)
            )
            sstage[COND, row, half, layer] = c
            ids = (2 * space + layer) * (128 * 256) + row * (BY * 256) + half
            ids = ids + lax.broadcasted_iota(jnp.int32, (BY, LANES), 0) * 256
            ids = ids + lax.broadcasted_iota(jnp.int32, (BY, LANES), 1) * 2
            for t, (u, q) in enumerate(((u_a, q_a), (u_b, q_b))):
                stage[U0, t, row, half, layer] = u
                source = jnp.where(ids == src_cells[0, t], STRENGTH, 0.0)
                source = source - jnp.where(ids == src_cells[1, t], STRENGTH, 0.0)
                stage[R0, t, row, half, layer] = source + c * q

    def later_fields(row, layer, where):
        sources = [chg[where], rlx[where]] + [mem[(k, t) + where] for t in range(2) for k in range(4)]
        moved = reorder(jnp.concatenate(sources, axis=0), 0)
        for half in range(2):
            later_half(
                row, layer, half,
                [moved[i * BY : (i + 1) * BY, half * LANES : (half + 1) * LANES] for i in range(10)],
            )

    def later_half(row, layer, half, values):
        c, g = sstage[COND, row, half, layer], values[0]
        rate = 1.0 / values[1]
        decays = [jnp.exp(-rate / ratio) for ratio in RATIOS]
        a0, a1, b0, b1 = (jnp.zeros((BY, LANES), F32) for _ in range(4))
        for k in range(4):
            fresh = WEIGHTS[k] * (1.0 - decays[k])
            a0 = a0 + fresh
            a1 = a1 + fresh * decays[k]
            tilt = decays[k] * (WEIGHTS[k] / RATIOS[k])
            b0 = b0 + tilt
            b1 = b1 + tilt * (1.0 - 2.0 * decays[k])
        sstage[F1, row, half, layer] = c * g * a0
        sstage[F2, row, half, layer] = c * g * a1
        factors[KA0, row, half, layer] = c * a0
        factors[KA1, row, half, layer] = c * a1
        factors[KB0, row, half, layer] = c * g * rate * rate * b0
        factors[KB1, row, half, layer] = c * g * rate * rate * b1
        for t in range(2):
            first, second, slope, slope_d = (jnp.zeros((BY, LANES), F32) for _ in range(4))
            for k in range(4):
                scaled = decays[k] * values[2 + 4 * t + k]
                first = first + scaled
                second = second + decays[k] * scaled
                tilt = scaled * (1.0 / RATIOS[k])
                slope = slope + tilt
                slope_d = slope_d + decays[k] * tilt
            stage[R1, t, row, half, layer] = c * first
            stage[R2, t, row, half, layer] = c * second
            tilts[0, t, row, half, layer] = c * rate * rate * slope
            tilts[1, t, row, half, layer] = 2.0 * c * rate * rate * slope_d

    def landing(f, j):
        layers = pl.ds(HALO + 2 * j, 2)
        if f == U0:
            return entry.at[0, :, layers, pl.ds(VTOP, BY)]
        if f == R0:
            return rhs.at[0, :, layers, pl.ds(HALO, BY)]
        return blk.at[f - R1, :, pl.ds(2 * j, 2)]

    def target(p):
        q = lax.rem(p + slot, SLOTS)
        return q // 2, lax.rem(q, 2), q, device(yp, q // 2, lax.rem(q, 2))

    def field_copy(f, p):
        x, t, q, to = target(p)
        return to, remote(stage.at[f, t, x], landing(f, slot), fsend.at[f, q], frecv.at[f, slot], {"space": to})

    def static_copy(f, p):
        x, t, q, to = target(p)
        quarter = (tx // 2, lax.rem(tx, 2))
        return to, remote(
            sstage.at[(f, x) + quarter], sblk.at[(f,) + quarter + (slot,)], ssend.at[f, q], srecv.at[f, slot], {"space": to}
        )

    def begin(f, copy_of):
        def one(p):
            to, copy = copy_of(f, p)
            pl.when(to != space)(copy.start)

        over(SLOTS, one)

    def finish(f, copy_of):
        def one(p):
            to, copy = copy_of(f, p)
            pl.when(to != space)(copy.wait_send)

        over(SLOTS, one)

    def send_field(f):
        begin(f, field_copy)

        def keep():
            if f == U0:
                entry[0, :, pl.ds(HALO + 2 * slot, 2), VTOP : VTOP + BY] = stage[f, mine, gx]
            elif f == R0:
                rhs[0, :, pl.ds(HALO + 2 * slot, 2), HALO : HALO + BY] = stage[f, mine, gx]
            else:
                blk[f - R1, :, pl.ds(2 * slot, 2)] = stage[f, mine, gx]

        pl.when(bx == yp)(keep)

    def send_static(f):
        begin(f, static_copy)

        def keep():
            sblk[f, tx // 2, lax.rem(tx, 2), slot] = sstage[f, gx, tx // 2, lax.rem(tx, 2)]

        pl.when(bx == yp)(keep)

    def take_field(f):
        def one(j):
            here = landing(f, j)
            of = bx * SLOTS + j
            copy = remote(here, here, fsend.at[f, j], frecv.at[f, j], {"space": of})
            pl.when(of != space)(copy.wait_recv)

        over(SLOTS, one)

    def spread_copy(f, p):
        to = lax.rem(tx + p, 4)
        quarter = sblk.at[f, tx // 2, lax.rem(tx, 2)]
        return remote(quarter, quarter, zsend.at[f, to], zrecv.at[f, tx], {"tx": to})

    def spread_static(f):
        def one(j):
            here = sblk.at[f, tx // 2, lax.rem(tx, 2), j]
            of = bx * SLOTS + j
            copy = remote(here, here, ssend.at[f, j], srecv.at[f, j], {"space": of})
            pl.when(of != space)(copy.wait_recv)

        over(SLOTS, one)
        over(4, lambda p: spread_copy(f, p).start(), 1)

    def take_static(f):
        def one(p):
            of = lax.rem(tx + p, 4)
            quarter = sblk.at[f, of // 2, lax.rem(of, 2)]
            remote(quarter, quarter, zsend.at[f, of], zrecv.at[f, of], {"tx": of}).wait_recv()

        over(4, one, 1)

    def static(f, half, x):
        return sblk[f, half, lax.rem(x, 2), x // 2]

    for load in loads[:3]:
        load.wait()
    pieces(first_fields)

    def clear(ref, index):
        shape = ref.at[index].shape
        ref[index] = jnp.zeros(shape, F32)

    def clear_pads(x):
        for ref in (va, vb):
            for half in range(2):
                clear(ref, (half, x, pl.ds(0, PAD)))
                clear(ref, (half, x, pl.ds(PAD + EY, PAD)))
        for k in range(5):
            for half in range(2):
                clear(entry, (k, half, x, pl.ds(0, PAD)))
                clear(entry, (k, half, x, pl.ds(PAD + EY, PAD)))

    over(EX, clear_pads)

    def clear_rows(low):
        def one(x):
            for half in range(2):
                at = 0 if low else HALO + BY
                for k in range(5):
                    clear(entry, (k, half, x, pl.ds(PAD + at, HALO)))
                for n in range(NSTEPS):
                    clear(rhs, (n, half, x, pl.ds(at, HALO)))
                clear(inv, (half, x, pl.ds(at, HALO)))

        over(EX, one)

    def clear_layers(low):
        def one(i):
            x = i if low else i + HALO + BX
            for half in range(2):
                for k in range(5):
                    clear(entry, (k, half, x, pl.ds(PAD, EY)))
                for n in range(NSTEPS):
                    clear(rhs, (n, half, x))
                clear(inv, (half, x))

        over(HALO, one)

    pl.when(gx == 0)(lambda: clear_rows(True))
    pl.when(gx == NXB - 1)(lambda: clear_rows(False))
    pl.when(bx == 0)(lambda: clear_layers(True))
    pl.when(bx == NB - 1)(lambda: clear_layers(False))

    pl.semaphore_wait(barrier, SPACES + 2)
    send_static(COND)
    send_field(U0)
    send_field(R0)

    def slab_lanes(s, count=1):
        return pl.ds(pl.multiple_of(s * LANES, LANES), count * LANES)

    for t in range(2):
        for n in range(NSTEPS):
            vswap[3 * t + n] = obs[n, t : t + 1, :]
    obs_pair = remote(
        vswap.at[pl.ds(3 * (1 - mine), 3)], obs_all.at[:, :, slab_lanes(space)], qsend.at[0], qrecv.at[0], {"space": partner}
    )
    obs_pair_in = remote(
        vswap.at[pl.ds(3 * (1 - mine), 3)], obs_all.at[:, :, slab_lanes(partner)], qsend.at[0], qrecv.at[0], {"space": partner}
    )
    obs_pair.start()
    obs_all[:, :, slab_lanes(space)] = vswap[pl.ds(3 * mine, 3)]

    def obs_copy(p, which):
        to = lax.rem(slot + p, SLOTS)
        here = obs_all.at[:, :, slab_lanes(space if which == 0 else partner)]
        return remote(here, here, osend.at[which, to], orecv.at[which, slot], {"space": yp * SLOTS + to})

    def obs_wait(p, which):
        of = lax.rem(slot + p, SLOTS)
        row = yp if which == 0 else yp + 1 - 2 * mine
        here = obs_all.at[:, :, slab_lanes(row * SLOTS + of)]
        remote(here, here, osend.at[which, of], orecv.at[which, of], {"space": yp * SLOTS + of}).wait_recv()

    def obs_rows(own):
        half = yp // 2 if own else 1 - yp // 2
        here = obs_all.at[:, :, slab_lanes(2 * half * SLOTS, 2 * SLOTS)]
        return remote(here, here, qsend.at[1], qrecv.at[1], {"space": lax.rem(space + 2 * SLOTS, NB * SLOTS)})

    lane_ids = lax.broadcasted_iota(jnp.int32, (1, LANES), 1)

    def live_at(j, carry):
        live[:, pl.ds(pl.multiple_of(j * LANES, LANES), LANES)] = jnp.where(lane_ids < counts[j], 1.0, 0.0)
        return carry

    lax.fori_loop(0, NB * SLOTS, live_at, 0)

    def halo(ref, top, which):
        width = HALO if top == VTOP else HALO - 1
        copies = []
        for side, (i, j) in enumerate(SIDES):
            deep = width if j == 0 else width - 1
            layers = {-1: (HALO, deep, HALO + BX), 1: (HALO + BX - deep, deep, HALO - deep), 0: (HALO, BX, HALO)}[i]
            rows = {-1: (top, HALO, top + BY), 1: (top + BY - HALO, HALO, top - HALO), 0: (top, BY, top)}[j]
            sends = (bx + i >= 0) & (bx + i < NB) & (gx + j >= 0) & (gx + j < NXB)
            takes = (bx - i >= 0) & (bx - i < NB) & (gx - j >= 0) & (gx - j < NXB)
            to = device(lax.rem(bx + i + NB, NB), lax.rem(gx + j + NXB, NXB), mine)
            copies.append((sends, takes, remote(
                ref.at[:, pl.ds(layers[0], layers[1]), pl.ds(rows[0], rows[1])],
                ref.at[:, pl.ds(layers[2], layers[1]), pl.ds(rows[2], rows[1])],
                hsend.at[which, side], hrecv.at[which, side], {"space": to},
            )))
        return copies

    def halo_start(ref, top, which):
        for sends, _, copy in halo(ref, top, which):
            pl.when(sends)(copy.start)

    def halo_wait(ref, top, which):
        for sends, takes, copy in halo(ref, top, which):
            pl.when(takes)(copy.wait_recv)
            pl.when(sends)(copy.wait_send)

    def over_x(body, unroll=1):
        def at(x, carry):
            body(x)
            return carry

        lax.fori_loop(0, BX, at, 0, unroll=unroll)

    def neighbour_sums(ref, x, top, rows):
        c0 = ref[0, x, top : top + rows]
        c1 = ref[1, x, top : top + rows]
        lane = lax.broadcasted_iota(jnp.int32, (rows, LANES), 1)
        z0 = c1 + jnp.where(lane == 0, 0.0, pltpu.roll(c1, 1, 1))
        z1 = c0 + jnp.where(lane == LANES - 1, 0.0, pltpu.roll(c0, LANES - 1, 1))
        sums = []
        for half, z in ((0, z0), (1, z1)):
            total = ref[half, x + 1, top : top + rows] + ref[half, x - 1, top : top + rows]
            total = total + ref[half, x, top + 1 : top + rows + 1] + ref[half, x, top - 1 : top + rows - 1]
            sums.append(total + z)
        return sums

    def sweeps(first, last, body, closing):
        source = first
        for s in range(1, last + 1):
            goal = va if s % 2 else vb
            if s == HALO:
                def one(x, carry, source=source):
                    closing(x, neighbour_sums(source, x, VTOP, BY))
                    return carry
            else:
                def one(x, carry, source=source, goal=goal):
                    sums = neighbour_sums(source, x, PAD, EY)
                    for half in range(2):
                        goal[half, x, PAD : PAD + EY] = body(half, x, sums[half])
                    return carry
            lax.fori_loop(s, EX - s, one, 0, unroll=UNROLL)
            source = goal

    def depth_of(sign, k):
        z = dip[sign : sign + 1, pl.ds(pl.multiple_of(k * CHUNK, CHUNK), CHUNK)] & 255
        return lax.broadcasted_iota(jnp.int32, (2 * LANES, CHUNK), 0) == (z & 1) * LANES + (z >> 1)

    def mark_rows(k):
        for sign in range(2):
            cells = dip[sign : sign + 1, pl.ds(pl.multiple_of(k * CHUNK, CHUNK), CHUNK)]
            x, y = cells >> 15, (cells >> 8) & 127
            own = ((x >> 4) == bx) & ((y >> 5) == gx)
            row = jnp.where(own, (x & 15) * BY + (y & 31), -1)
            hot = lax.broadcasted_iota(jnp.int32, (ROWS, CHUNK), 0) == row
            hots[sign, k] = jnp.where(hot, 1.0, 0.0).astype(BF16)

    def potential(n, half):
        if n == NSTEPS - 1:
            return ulast[half]
        return entry[n + 1, half, HALO : HALO + BX, VTOP : VTOP + BY]

    def gather_table(n):
        for half in range(2):
            rows = potential(n, half).reshape(ROWS, LANES).T
            high = rows.astype(BF16)
            ut[half * LANES : (half + 1) * LANES, :] = high
            ut[(2 + half) * LANES : (3 + half) * LANES, :] = (rows - high.astype(F32)).astype(BF16)

    def gather_part(n, h):
        def at(k, carry):
            found = []
            for sign in range(2):
                both = jnp.dot(ut[...], hots[sign, k], preferred_element_type=F32)
                value = both[: 2 * LANES] + both[2 * LANES :]
                found.append(jnp.sum(jnp.where(depth_of(sign, k), value, 0.0), axis=0, keepdims=True))
            part[n, :, pl.ds(pl.multiple_of(k * CHUNK, CHUNK), CHUNK)] = found[0] - found[1]
            return carry

        lax.fori_loop(h * HALF_CHUNKS, (h + 1) * HALF_CHUNKS, at, 0)

    def gather(n):
        gather_table(n)
        for h in range(2):
            gather_part(n, h)

    def scatter(n, h):
        if h == 0:
            acc[n - 1] = jnp.zeros((ROWS, 4 * LANES), F32)

        def at(k, carry):
            value = res[n, :, pl.ds(pl.multiple_of(k * CHUNK, CHUNK), CHUNK)]
            for sign in range(2):
                placed = jnp.where(depth_of(sign, k), value if sign == 0 else -value, 0.0)
                high = placed.astype(BF16)
                low = (placed - high.astype(F32)).astype(BF16)
                acc[n - 1] += lax.dot_general(
                    hots[sign, k], jnp.concatenate([high, low], axis=0), (((1,), (1,)), ((), ())), preferred_element_type=F32
                )
            return carry

        lax.fori_loop(h * HALF_CHUNKS, (h + 1) * HALF_CHUNKS, at, 0)

    def injected(n, half, x):
        rows = pl.ds(pl.multiple_of(x * BY, BY), BY)
        return (
            acc[n - 1, rows, half * LANES : (half + 1) * LANES]
            + acc[n - 1, rows, (2 + half) * LANES : (3 + half) * LANES]
        )

    def span(h):
        return pl.ds(h * HALF, HALF)

    def row_copy(n, h, p):
        to = lax.rem(gx + p, NXB)
        return remote(
            part.at[n, :, span(h)], prx.at[gx, n, :, span(h)], psend.at[0, n, h, to], precv.at[0, n, h, gx],
            {"space": device(bx, to, mine)},
        )

    def row_wait(n, h, p):
        of = lax.rem(gx + p, NXB)
        here = prx.at[of, n, :, span(h)]
        remote(
            here, here, psend.at[0, n, h, of], precv.at[0, n, h, of], {"space": device(bx, of, mine)}
        ).wait_recv()

    def row_copies(n, h):
        over(4, lambda p: row_copy(n, h, p).start(), 1)
        prx[gx, n, :, span(h)] = part[n, :, span(h)]

    def col_copy(n, h, p):
        to = lax.rem(bx + p, NB)
        return remote(
            rows.at[n, :, span(h)], pry.at[bx, n, :, span(h)], psend.at[1, n, h, to], precv.at[1, n, h, bx],
            {"space": device(to, gx, mine)},
        )

    def col_wait(n, h, p):
        of = lax.rem(bx + p, NB)
        here = pry.at[of, n, :, span(h)]
        remote(
            here, here, psend.at[1, n, h, of], precv.at[1, n, h, of], {"space": device(of, gx, mine)}
        ).wait_recv()

    def row_sums(n, h):
        over(4, functools.partial(row_wait, n, h), 1)
        at = (n, slice(None), span(h))
        rows[at] = (prx[(0,) + at] + prx[(1,) + at]) + (prx[(2,) + at] + prx[(3,) + at])
        over(4, lambda p: col_copy(n, h, p).start(), 1)
        pry[(bx,) + at] = rows[at]

    def residual(n, h):
        over(4, functools.partial(col_wait, n, h), 1)
        at = (n, slice(None), span(h))
        alive = live[:, span(h)]
        value = alive * ((pry[(0,) + at] + pry[(1,) + at]) + (pry[(2,) + at] + pry[(3,) + at]))
        volts[at] = value
        res[at] = alive * (value - obs_all[at])

    def back_copy(f, p):
        j = lax.rem(p + slot, SLOTS)
        layers = pl.ds(HALO + 2 * j, 2)
        if f in (POT0, POT1):
            here = entry.at[f + 1, :, layers, pl.ds(VTOP, BY)]
        else:
            here = adj.at[DUAL1 - f, :, layers, pl.ds(HALO, BY)]
        to = bx * SLOTS + j
        return to, remote(here, rx.at[f, gx, mine], gsend.at[f, j], grecv.at[f, 2 * gx + mine], {"space": to})

    def send_back(f):
        begin(f, back_copy)

        def keep():
            layers = pl.ds(HALO + 2 * slot, 2)
            if f in (POT0, POT1):
                rx[f, gx, mine] = entry[f + 1, :, layers, VTOP : VTOP + BY]
            else:
                rx[f, gx, mine] = adj[DUAL1 - f, :, layers, HALO : HALO + BY]

        pl.when(bx == yp)(keep)

    def back_wait(f, q):
        x, t = q // 2, lax.rem(q, 2)
        of = device(yp, x, t)
        here = rx.at[f, x, t]
        copy = remote(here, here, gsend.at[f, q], grecv.at[f, q], {"space": of})
        pl.when(of != space)(copy.wait_recv)

    spread_static(COND)
    for load in loads[3:]:
        load.wait()
    pieces(later_fields)
    over(NDIP // CHUNK, mark_rows)
    take_field(U0)
    halo_start(entry.at[0], VTOP, 0)
    take_static(COND)

    def inverse(x):
        for half in range(2):
            inv[half, HALO + x, HALO : HALO + BY] = 1.0 / (6.0 + static(COND, half, x))

    over_x(inverse)
    halo_start(inv, HALO, 8)
    take_field(R0)
    halo_start(rhs.at[0], HALO, 5)
    send_static(F1)
    halo_wait(entry.at[0], VTOP, 0)
    halo_wait(inv, HALO, 8)
    halo_wait(rhs.at[0], HALO, 5)
    send_field(R1)
    send_static(F2)
    spread_static(F1)

    def block_of(k, half, x):
        return entry[k, half, HALO + x, VTOP : VTOP + BY]

    def forward(n):
        def body(half, x, total):
            return (rhs[n, half, x] + total) * inv[half, x]

        def closing(x, sums):
            for half in range(2):
                made = (rhs[n, half, x, HALO : HALO + BY] + sums[half]) * inv[half, x, HALO : HALO + BY]
                if n == NSTEPS - 1:
                    ulast[half, x - HALO] = made
                else:
                    entry[n + 1, half, x, VTOP : VTOP + BY] = made

        sweeps(entry.at[n], JACOBI, body, closing)

    forward(0)
    halo_start(entry.at[1], VTOP, 1)
    take_static(F1)
    take_field(R1)

    def step_one(x):
        for half in range(2):
            rhs[1, half, HALO + x, HALO : HALO + BY] = (
                blk[0, half, x] + static(F1, half, x) * block_of(1, half, x)
            )

    over_x(step_one)
    halo_start(rhs.at[1], HALO, 6)
    spread_static(F2)
    obs_pair_in.wait_recv()
    over(SLOTS, lambda p: obs_copy(p, 0).start(), 1)
    over(SLOTS, lambda p: obs_copy(p, 1).start(), 1)
    gather(0)
    for h in range(2):
        row_copies(0, h)
    halo_wait(entry.at[1], VTOP, 1)
    halo_wait(rhs.at[1], HALO, 6)
    send_field(R2)
    forward(1)
    halo_start(entry.at[2], VTOP, 2)
    take_static(F2)
    take_field(R2)

    def step_two(x):
        for half in range(2):
            rhs[2, half, HALO + x, HALO : HALO + BY] = (
                blk[1, half, x]
                + static(F2, half, x) * block_of(1, half, x)
                + static(F1, half, x) * block_of(2, half, x)
            )

    over_x(step_two)
    halo_start(rhs.at[2], HALO, 7)
    over(SLOTS, lambda p: obs_wait(p, 0), 1)
    over(SLOTS, lambda p: obs_wait(p, 1), 1)
    obs_rows(True).start()
    gather(1)
    for h in range(2):
        row_copies(1, h)
        row_sums(0, h)
    halo_wait(entry.at[2], VTOP, 2)
    halo_wait(rhs.at[2], HALO, 7)
    send_back(POT0)
    forward(2)

    gather_table(2)
    gather_part(2, 0)
    row_copies(2, 0)
    gather_part(2, 1)
    row_copies(2, 1)
    obs_rows(False).wait_recv()
    row_sums(2, 0)
    row_sums(2, 1)
    for h in range(2):
        row_sums(1, h)

    def begin_adjoint(n):
        def body(x):
            for half in range(2):
                field = injected(n, half, x)
                if n == 1:
                    field = field + back[half, x] + static(F1, half, x) * adj[1, half, HALO + x, HALO : HALO + BY]
                scaled = field * inv[half, HALO + x, HALO : HALO + BY]
                adj[n - 1, half, HALO + x, HALO : HALO + BY] = scaled
                entry[5 - n, half, HALO + x, VTOP : VTOP + BY] = scaled

        over_x(body)

    def adjoint(n):
        def body(half, x, total):
            scaled = total * inv[half, x]
            adj[n - 1, half, x] += scaled
            return scaled

        def closing(x, sums):
            for half in range(2):
                back[half, x - HALO] = sums[half]

        sweeps(entry.at[5 - n], JACOBI if n == 2 else JACOBI - 1, body, closing)

    for h in range(2):
        residual(2, h)
        scatter(2, h)
    begin_adjoint(2)
    halo_start(entry.at[3], VTOP, 3)
    for h in range(2):
        residual(1, h)
        scatter(1, h)
        residual(0, h)

    squares = jnp.zeros((1, NDIP), F32)
    for n in range(NSTEPS):
        squares = squares + res[n] * res[n]

    own = pl.ds(pl.multiple_of(space * LANES, LANES), LANES)
    other = pl.ds(pl.multiple_of(partner * LANES, LANES), LANES)
    swap = remote(volts.at[:, :, other], vswap.at[pl.ds(6, 3)], qsend.at[2], qrecv.at[2], {"space": partner})
    swap.start()
    lanes = squares[:, 0:LANES]
    for j in range(1, NDIP // LANES):
        lanes = lanes + squares[:, j * LANES : (j + 1) * LANES]
    sq[...] = lanes
    pair = remote(sq, sqc, qsend.at[3], qrecv.at[3], {"space": partner})
    pair.start()
    for n in range(NSTEPS):
        volts_out[n, pl.ds(mine, 1), :] = volts[n, :, own]
    swap.wait()
    for n in range(NSTEPS):
        volts_out[n, pl.ds(1 - mine, 1), :] = vswap[6 + n]
    pair.wait()
    sqz[tx] = sq[...] + sqc[...]

    def sq_copy(p):
        to = lax.rem(tx + p, 4)
        return remote(sqz.at[tx], sqz.at[tx], tsend.at[2, to], trecv.at[2, tx], {"tx": to})

    def sq_wait(p):
        of = lax.rem(tx + p, 4)
        remote(sqz.at[of], sqz.at[of], tsend.at[2, of], trecv.at[2, of], {"tx": of}).wait_recv()

    over(4, lambda p: sq_copy(p).start(), 1)

    halo_wait(entry.at[3], VTOP, 3)
    send_back(POT1)
    adjoint(2)
    begin_adjoint(1)
    halo_start(entry.at[4], VTOP, 4)
    halo_wait(entry.at[4], VTOP, 4)
    send_back(DUAL2)
    adjoint(1)
    send_back(DUAL1)

    over(4, sq_wait, 1)
    total = (sqz[0] + sqz[1]) + (sqz[2] + sqz[3])
    misfit = jnp.sqrt(1.0 + jnp.sum(total, axis=1, keepdims=True))
    misfit_out[...] = misfit
    scale = 1.0 / misfit
    for f in (POT0, POT1, DUAL2):
        over(SLOTS, functools.partial(back_wait, f))

    def tx_copy(f, to):
        return remote(rsum.at[f, to], rz.at[f, tx], tsend.at[f, to], trecv.at[f, tx], {"tx": to})

    def tx_wait(f, p):
        of = lax.rem(tx + p, 4)
        remote(rsum.at[f, of], rz.at[f, of], tsend.at[f, of], trecv.at[f, of], {"tx": of}).wait_recv()

    def gradients(i):
        x = lax.rem(gx + i, NXB)
        for t in range(2):
            back_wait(DUAL1, 2 * x + t)
        for half in range(2):
            for layer in range(2):
                at = (half, layer)
                same, cross, tilt = (jnp.zeros((BY, LANES), F32) for _ in range(3))
                for t in range(2):
                    u0, u1, s2, s1 = (rx[(f, x, t) + at] for f in range(4))
                    same = same + (s2 * u1 + s1 * u0)
                    cross = cross + s2 * u0
                    tilt = tilt + (s1 * tilts[(0, t, x) + at] + s2 * tilts[(1, t, x) + at])
                ka0, ka1, kb0, kb1 = (factors[(f, x) + at] for f in range(4))
                rsum[(0, x) + at] = ka0 * same + ka1 * cross
                rsum[(1, x) + at] = tilt - kb0 * same + kb1 * cross

        def give():
            for f in range(2):
                tx_copy(f, x).start()

        def keep():
            for f in range(2):
                rz[f, tx] = rsum[f, x]

        pl.when(x != tx)(give)
        pl.when(x == tx)(keep)

    over(NXB, gradients)
    for f, out in ((0, gc_out), (1, gt_out)):
        over(4, functools.partial(tx_wait, f), 1)
        halves = [(rz[f, 0, half] + rz[f, 1, half]) + (rz[f, 2, half] + rz[f, 3, half]) for half in range(2)]
        value = reorder(jnp.concatenate([half.reshape(2 * BY, LANES) for half in halves], axis=1), 1)
        out[...] = value.reshape(2, BY, 2 * LANES) * scale.reshape(1, 1, 1)

    for f in range(4):
        finish(f, field_copy)
    for f in range(3):
        finish(f, static_copy)
        over(4, lambda p: spread_copy(f, p).wait_send(), 1)
    obs_pair.wait_send()
    for which in range(2):
        over(SLOTS, lambda p: obs_copy(p, which).wait_send(), 1)
    obs_rows(True).wait_send()
    for n in range(NSTEPS):
        for h in range(2):
            over(4, lambda p: row_copy(n, h, p).wait_send(), 1)
            over(4, lambda p: col_copy(n, h, p).wait_send(), 1)
    over(4, lambda p: sq_copy(p).wait_send(), 1)
    for f in range(4):
        finish(f, back_copy)
    for f in range(2):
        over(4, lambda p: tx_copy(f, lax.rem(tx + p, 4)).wait_send(), 1)


def hand_over(*refs):
    given, made, sems = refs[:4], refs[4:8], refs[8]
    copies = [pltpu.make_async_copy(a, b, sems.at[i]) for i, (a, b) in enumerate(zip(given, made))]
    for copy in copies:
        copy.start()
    for copy in copies:
        copy.wait()


def on_device(cond, chg, rlx, start, mem, src_cells, dip, counts, obs):
    vmem = pl.BlockSpec(memory_space=pltpu.VMEM)
    whole = pl.BlockSpec(memory_space=pl.ANY)
    smem = pl.BlockSpec(memory_space=pltpu.SMEM)
    field = pltpu.VMEM((2, BX, BY, LANES), F32)
    dma = pltpu.SemaphoreType.DMA
    wide = pltpu.VMEM((2, EX, EY + 2 * PAD, LANES), F32)
    slab = pltpu.VMEM((2, 128, 2 * LANES), F32)
    scratch = [
        slab, slab, slab,
        pltpu.VMEM((2, 2, 128, 2 * LANES), F32),
        pltpu.VMEM((4, 2, 2, 128, 2 * LANES), F32),
        pltpu.VMEM((2 * LANES, 2 * LANES), BF16),
        pltpu.VMEM((2, NDIP // CHUNK, ROWS, CHUNK), BF16),
        pltpu.VMEM((4, 2, NXB, 2, 2, BY, LANES), F32),
        pltpu.VMEM((3, NXB, 2, 2, BY, LANES), F32),
        pltpu.VMEM((2, 2, NXB, 2, 2, BY, LANES), F32),
        pltpu.VMEM((4, NXB, 2, 2, BY, LANES), F32),
        pltpu.VMEM((2, 2, BX, BY, LANES), F32),
        pltpu.VMEM((3, 2, 2, BX // 2, BY, LANES), F32),
        pltpu.VMEM((5, 2, EX, EY + 2 * PAD, LANES), F32),
        wide, wide,
        pltpu.VMEM((2, EX, EY, LANES), F32),
        pltpu.VMEM((NSTEPS, 2, EX, EY, LANES), F32),
        field,
        pltpu.VMEM((2, 2, EX, EY, LANES), F32),
        field,
        pltpu.VMEM((4 * LANES, ROWS), BF16),
        pltpu.VMEM((2, ROWS, 4 * LANES), F32),
        pltpu.VMEM((NSTEPS, 1, NDIP), F32),
        pltpu.VMEM((NXB, NSTEPS, 1, NDIP), F32),
        pltpu.VMEM((NB, NSTEPS, 1, NDIP), F32),
        pltpu.VMEM((NSTEPS, 1, NDIP), F32),
        pltpu.VMEM((NSTEPS, 1, NDIP), F32),
        pltpu.VMEM((NSTEPS, 1, NDIP), F32),
        pltpu.VMEM((NSTEPS, 1, NDIP), F32),
        pltpu.VMEM((1, NDIP), F32),
        pltpu.VMEM((9, 1, LANES), F32),
        pltpu.VMEM((1, LANES), F32),
        pltpu.VMEM((1, LANES), F32),
        pltpu.VMEM((4, 1, LANES), F32),
        pltpu.VMEM((4, NXB, 2, 2, 2, BY, LANES), F32),
        pltpu.VMEM((2, NXB, 2, 2, BY, LANES), F32),
        pltpu.VMEM((2, 4, 2, 2, BY, LANES), F32),
        dma((5,)),
        dma((4, SLOTS)), dma((4, SLOTS)), dma((3, SLOTS)), dma((3, SLOTS)),
        dma((3, 4)), dma((3, 4)),
        dma((9, 8)), dma((9, 8)),
        dma((2, SLOTS)), dma((2, SLOTS)),
        dma((2, NSTEPS, 2, 4)), dma((2, NSTEPS, 2, 4)),
        dma((4,)), dma((4,)),
        dma((4, SLOTS)), dma((4, SLOTS)),
        dma((3, 4)), dma((3, 4)),
    ]
    volts, misfit, grad_c, grad_t = pl.pallas_call(
        kernel,
        out_shape=(
            jax.ShapeDtypeStruct((NSTEPS, 2, LANES), F32),
            jax.ShapeDtypeStruct((1, 1), F32),
            jax.ShapeDtypeStruct((2, BY, 2 * LANES), F32),
            jax.ShapeDtypeStruct((2, BY, 2 * LANES), F32),
        ),
        in_specs=[whole, whole, whole, whole, whole, smem, vmem, smem, vmem],
        out_specs=(vmem, vmem, vmem, vmem),
        scratch_shapes=scratch,
        compiler_params=pltpu.CompilerParams(has_side_effects=True, collective_id=0, vmem_limit_bytes=60 << 20),
    )(cond, chg, rlx, start, mem, src_cells, dip, counts, obs)
    results = (volts, misfit, grad_c, grad_t)
    volts, misfit, grad_c, grad_t = pl.pallas_call(
        hand_over,
        out_shape=tuple(jax.ShapeDtypeStruct(a.shape, F32) for a in results),
        in_specs=[whole] * 4,
        out_specs=(whole,) * 4,
        scratch_shapes=[dma((4,))],
    )(*results)
    return (volts, misfit.reshape(()), grad_c, grad_t)


def solution(mesh):
    placed = (
        P("space", None, None),
        P("space", None, None),
        P("space", None, None),
        P("tx", "space", None, None),
        P(None, "tx", "space", None, None),
        P(None, "tx"),
        P(),
        P(),
        P(None, "tx", "space"),
    )
    return jax.shard_map(
        on_device,
        mesh=mesh,
        in_specs=placed,
        out_specs=(P(None, "tx", "space"), P(), P("space", "tx", None), P("space", "tx", None)),
        check_vma=False,
    )
```

```python
import functools

import jax
import jax.numpy as jnp
from jax import lax
from jax.experimental import pallas as pl
from jax.experimental.pallas import tpu as pltpu
from jax.sharding import PartitionSpec as P

MESH = pl.DeviceIdType.MESH
F32 = jnp.float32
BF16 = jnp.bfloat16
NSTEPS = 3
JACOBI = 8
WEIGHTS = (0.4, 0.3, 0.2, 0.1)
RATIOS = (0.25, 1.0, 4.0, 16.0)
STRENGTH = 4.0

NB, NXB = 4, 4
SLOTS = 8
BX, BY, LANES = 16, 32, 128
HALO = 8
EX, EY = BX + 2 * HALO, BY + 2 * HALO
PAD = 8
VTOP = PAD + HALO
NDIP = 4096
CHUNK = 512
HALF = NDIP // 2
HALF_CHUNKS = HALF // CHUNK
ROWS = BX * BY
UNROLL = 8
U0, R0, R1, R2 = range(4)
COND, F1, F2 = range(3)
KA0, KA1, KB0, KB1 = range(4)
POT0, POT1, DUAL2, DUAL1 = range(4)
SPACES = 32
SIDES = ((0, -1), (0, 1), (-1, 0), (1, 0), (-1, -1), (-1, 1), (1, -1), (1, 1))


def remote(src, dst, send, recv, device):
    return pltpu.make_async_remote_copy(
        src_ref=src, dst_ref=dst, send_sem=send, recv_sem=recv, device_id=device, device_id_type=MESH
    )


def kernel(
    cond_hbm, chg_hbm, rlx_hbm, start_hbm, mem_hbm, src_cells, dip, counts, obs,
    volts_out, misfit_out, gc_out, gt_out,
    cond, chg, rlx, start, mem,
    perm, hots, stage, sstage, tilts, factors, blk, sblk, entry, va, vb,
    inv, rhs, ulast, adj, back,
    ut, acc, part, prx, pry, rows, volts, res, obs_all, live, vswap, sq, sqc, sqz,
    rx, rsum, rz,
    lsem, fsend, frecv, ssend, srecv, zsend, zrecv, hsend, hrecv, osend, orecv, psend, precv, qsend, qrecv,
    gsend, grecv, tsend, trecv,
):
    space = lax.axis_index("space")
    tx = lax.axis_index("tx")
    yp = space // SLOTS
    slot = lax.rem(space, SLOTS)
    gx = slot // 2
    mine = lax.rem(yp, 2)
    bx = 2 * (yp // 2) + lax.rem(slot, 2)
    partner = (yp + 1 - 2 * mine) * SLOTS + slot

    def device(b, x, t):
        return (2 * (b // 2) + t) * SLOTS + 2 * x + lax.rem(b, 2)

    def over(count, body, first=0):
        def at(p, carry):
            body(p)
            return carry

        lax.fori_loop(first, count, at, 0)

    barrier = pltpu.get_barrier_semaphore()
    loads = [
        pltpu.make_async_copy(a, b, lsem.at[i])
        for i, (a, b) in enumerate(
            ((cond_hbm, cond), (start_hbm, start), (mem_hbm, mem), (chg_hbm, chg), (rlx_hbm, rlx))
        )
    ]
    for load in loads:
        load.start()

    def greet_space(q):
        pl.semaphore_signal(barrier, 1, device_id={"space": lax.rem(space + q, SPACES)}, device_id_type=MESH)

    def greet_tx(q):
        pl.semaphore_signal(barrier, 1, device_id={"tx": lax.rem(tx + q, 4)}, device_id_type=MESH)

    over(SPACES, greet_space, 1)
    over(4, greet_tx, 1)

    def three(value):
        high = value.astype(BF16)
        rest = value - high.astype(F32)
        middle = rest.astype(BF16)
        return high, middle, (rest - middle.astype(F32)).astype(BF16)

    def reorder(value, axis):
        parts = jnp.concatenate(three(value), axis=0)
        moved = lax.dot_general(parts, perm[...], (((1,), (axis,)), ((), ())), preferred_element_type=F32)
        rows = value.shape[0]
        return (moved[:rows] + moved[rows : 2 * rows]) + moved[2 * rows :]

    cell = lax.broadcasted_iota(jnp.int32, (2 * LANES, 2 * LANES), 0)
    goal = lax.broadcasted_iota(jnp.int32, (2 * LANES, 2 * LANES), 1)
    perm[...] = jnp.where(goal == (cell & 1) * LANES + (cell >> 1), 1.0, 0.0).astype(BF16)

    def pieces(body):
        def at(i, carry):
            row, layer = i // 2, lax.rem(i, 2)
            body(row, layer, (layer, pl.ds(pl.multiple_of(row * BY, BY), BY), slice(None)))
            return carry

        lax.fori_loop(0, 2 * NXB, at, 0)

    def first_fields(row, layer, where):
        sources = [cond[where]]
        for t in range(2):
            sources.append(start[(t,) + where])
            sources.append(mem[(0, t) + where] + mem[(1, t) + where] + mem[(2, t) + where] + mem[(3, t) + where])
        moved = reorder(jnp.concatenate(sources, axis=0), 0)
        for half in range(2):
            c, u_a, q_a, u_b, q_b = (
                moved[i * BY : (i + 1) * BY, half * LANES : (half + 1) * LANES] for i in range(5)
            )
            sstage[COND, row, half, layer] = c
            ids = (2 * space + layer) * (128 * 256) + row * (BY * 256) + half
            ids = ids + lax.broadcasted_iota(jnp.int32, (BY, LANES), 0) * 256
            ids = ids + lax.broadcasted_iota(jnp.int32, (BY, LANES), 1) * 2
            for t, (u, q) in enumerate(((u_a, q_a), (u_b, q_b))):
                stage[U0, t, row, half, layer] = u
                source = jnp.where(ids == src_cells[0, t], STRENGTH, 0.0)
                source = source - jnp.where(ids == src_cells[1, t], STRENGTH, 0.0)
                stage[R0, t, row, half, layer] = source + c * q

    def later_fields(row, layer, where):
        sources = [chg[where], rlx[where]] + [mem[(k, t) + where] for t in range(2) for k in range(4)]
        moved = reorder(jnp.concatenate(sources, axis=0), 0)
        for half in range(2):
            later_half(
                row, layer, half,
                [moved[i * BY : (i + 1) * BY, half * LANES : (half + 1) * LANES] for i in range(10)],
            )

    def later_half(row, layer, half, values):
        c, g = sstage[COND, row, half, layer], values[0]
        rate = 1.0 / values[1]
        decays = [jnp.exp(-rate / ratio) for ratio in RATIOS]
        a0, a1, b0, b1 = (jnp.zeros((BY, LANES), F32) for _ in range(4))
        for k in range(4):
            fresh = WEIGHTS[k] * (1.0 - decays[k])
            a0 = a0 + fresh
            a1 = a1 + fresh * decays[k]
            tilt = decays[k] * (WEIGHTS[k] / RATIOS[k])
            b0 = b0 + tilt
            b1 = b1 + tilt * (1.0 - 2.0 * decays[k])
        sstage[F1, row, half, layer] = c * g * a0
        sstage[F2, row, half, layer] = c * g * a1
        factors[KA0, row, half, layer] = c * a0
        factors[KA1, row, half, layer] = c * a1
        factors[KB0, row, half, layer] = c * g * rate * rate * b0
        factors[KB1, row, half, layer] = c * g * rate * rate * b1
        for t in range(2):
            first, second, slope, slope_d = (jnp.zeros((BY, LANES), F32) for _ in range(4))
            for k in range(4):
                scaled = decays[k] * values[2 + 4 * t + k]
                first = first + scaled
                second = second + decays[k] * scaled
                tilt = scaled * (1.0 / RATIOS[k])
                slope = slope + tilt
                slope_d = slope_d + decays[k] * tilt
            stage[R1, t, row, half, layer] = c * first
            stage[R2, t, row, half, layer] = c * second
            tilts[0, t, row, half, layer] = c * rate * rate * slope
            tilts[1, t, row, half, layer] = 2.0 * c * rate * rate * slope_d

    def landing(f, j):
        layers = pl.ds(HALO + 2 * j, 2)
        if f == U0:
            return entry.at[0, :, layers, pl.ds(VTOP, BY)]
        if f == R0:
            return rhs.at[0, :, layers, pl.ds(HALO, BY)]
        return blk.at[f - R1, :, pl.ds(2 * j, 2)]

    def target(p):
        q = lax.rem(p + slot, SLOTS)
        return q // 2, lax.rem(q, 2), q, device(yp, q // 2, lax.rem(q, 2))

    def field_copy(f, p):
        x, t, q, to = target(p)
        return to, remote(stage.at[f, t, x], landing(f, slot), fsend.at[f, q], frecv.at[f, slot], {"space": to})

    def static_copy(f, p):
        x, t, q, to = target(p)
        quarter = (tx // 2, lax.rem(tx, 2))
        return to, remote(
            sstage.at[(f, x) + quarter], sblk.at[(f,) + quarter + (slot,)], ssend.at[f, q], srecv.at[f, slot], {"space": to}
        )

    def begin(f, copy_of):
        def one(p):
            to, copy = copy_of(f, p)
            pl.when(to != space)(copy.start)

        over(SLOTS, one)

    def finish(f, copy_of):
        def one(p):
            to, copy = copy_of(f, p)
            pl.when(to != space)(copy.wait_send)

        over(SLOTS, one)

    def send_field(f):
        begin(f, field_copy)

        def keep():
            if f == U0:
                entry[0, :, pl.ds(HALO + 2 * slot, 2), VTOP : VTOP + BY] = stage[f, mine, gx]
            elif f == R0:
                rhs[0, :, pl.ds(HALO + 2 * slot, 2), HALO : HALO + BY] = stage[f, mine, gx]
            else:
                blk[f - R1, :, pl.ds(2 * slot, 2)] = stage[f, mine, gx]

        pl.when(bx == yp)(keep)

    def send_static(f):
        begin(f, static_copy)

        def keep():
            sblk[f, tx // 2, lax.rem(tx, 2), slot] = sstage[f, gx, tx // 2, lax.rem(tx, 2)]

        pl.when(bx == yp)(keep)

    def take_field(f):
        def one(j):
            here = landing(f, j)
            of = bx * SLOTS + j
            copy = remote(here, here, fsend.at[f, j], frecv.at[f, j], {"space": of})
            pl.when(of != space)(copy.wait_recv)

        over(SLOTS, one)

    def spread_copy(f, p):
        to = lax.rem(tx + p, 4)
        quarter = sblk.at[f, tx // 2, lax.rem(tx, 2)]
        return remote(quarter, quarter, zsend.at[f, to], zrecv.at[f, tx], {"tx": to})

    def spread_static(f):
        def one(j):
            here = sblk.at[f, tx // 2, lax.rem(tx, 2), j]
            of = bx * SLOTS + j
            copy = remote(here, here, ssend.at[f, j], srecv.at[f, j], {"space": of})
            pl.when(of != space)(copy.wait_recv)

        over(SLOTS, one)
        over(4, lambda p: spread_copy(f, p).start(), 1)

    def take_static(f):
        def one(p):
            of = lax.rem(tx + p, 4)
            quarter = sblk.at[f, of // 2, lax.rem(of, 2)]
            remote(quarter, quarter, zsend.at[f, of], zrecv.at[f, of], {"tx": of}).wait_recv()

        over(4, one, 1)

    def static(f, half, x):
        return sblk[f, half, lax.rem(x, 2), x // 2]

    for load in loads[:3]:
        load.wait()
    pieces(first_fields)

    def clear(ref, index):
        shape = ref.at[index].shape
        ref[index] = jnp.zeros(shape, F32)

    def clear_pads(x):
        for ref in (va, vb):
            for half in range(2):
                clear(ref, (half, x, pl.ds(0, PAD)))
                clear(ref, (half, x, pl.ds(PAD + EY, PAD)))
        for k in range(5):
            for half in range(2):
                clear(entry, (k, half, x, pl.ds(0, PAD)))
                clear(entry, (k, half, x, pl.ds(PAD + EY, PAD)))

    over(EX, clear_pads)

    def clear_rows(low):
        def one(x):
            for half in range(2):
                at = 0 if low else HALO + BY
                for k in range(5):
                    clear(entry, (k, half, x, pl.ds(PAD + at, HALO)))
                for n in range(NSTEPS):
                    clear(rhs, (n, half, x, pl.ds(at, HALO)))
                clear(inv, (half, x, pl.ds(at, HALO)))

        over(EX, one)

    def clear_layers(low):
        def one(i):
            x = i if low else i + HALO + BX
            for half in range(2):
                for k in range(5):
                    clear(entry, (k, half, x, pl.ds(PAD, EY)))
                for n in range(NSTEPS):
                    clear(rhs, (n, half, x))
                clear(inv, (half, x))

        over(HALO, one)

    pl.when(gx == 0)(lambda: clear_rows(True))
    pl.when(gx == NXB - 1)(lambda: clear_rows(False))
    pl.when(bx == 0)(lambda: clear_layers(True))
    pl.when(bx == NB - 1)(lambda: clear_layers(False))

    pl.semaphore_wait(barrier, SPACES + 2)
    send_static(COND)
    send_field(U0)
    send_field(R0)

    def slab_lanes(s, count=1):
        return pl.ds(pl.multiple_of(s * LANES, LANES), count * LANES)

    for t in range(2):
        for n in range(NSTEPS):
            vswap[3 * t + n] = obs[n, t : t + 1, :]
    obs_pair = remote(
        vswap.at[pl.ds(3 * (1 - mine), 3)], obs_all.at[:, :, slab_lanes(space)], qsend.at[0], qrecv.at[0], {"space": partner}
    )
    obs_pair_in = remote(
        vswap.at[pl.ds(3 * (1 - mine), 3)], obs_all.at[:, :, slab_lanes(partner)], qsend.at[0], qrecv.at[0], {"space": partner}
    )
    obs_pair.start()
    obs_all[:, :, slab_lanes(space)] = vswap[pl.ds(3 * mine, 3)]

    def obs_copy(p, which):
        to = lax.rem(slot + p, SLOTS)
        here = obs_all.at[:, :, slab_lanes(space if which == 0 else partner)]
        return remote(here, here, osend.at[which, to], orecv.at[which, slot], {"space": yp * SLOTS + to})

    def obs_wait(p, which):
        of = lax.rem(slot + p, SLOTS)
        row = yp if which == 0 else yp + 1 - 2 * mine
        here = obs_all.at[:, :, slab_lanes(row * SLOTS + of)]
        remote(here, here, osend.at[which, of], orecv.at[which, of], {"space": yp * SLOTS + of}).wait_recv()

    def obs_rows(own):
        half = yp // 2 if own else 1 - yp // 2
        here = obs_all.at[:, :, slab_lanes(2 * half * SLOTS, 2 * SLOTS)]
        return remote(here, here, qsend.at[1], qrecv.at[1], {"space": lax.rem(space + 2 * SLOTS, NB * SLOTS)})

    lane_ids = lax.broadcasted_iota(jnp.int32, (1, LANES), 1)

    def live_at(j, carry):
        live[:, pl.ds(pl.multiple_of(j * LANES, LANES), LANES)] = jnp.where(lane_ids < counts[j], 1.0, 0.0)
        return carry

    lax.fori_loop(0, NB * SLOTS, live_at, 0)

    def halo(ref, top, which):
        width = HALO if top == VTOP else HALO - 1
        copies, passed = [], []
        even = lax.rem(bx, 2) == 0
        for side, (i, j) in enumerate(SIDES):
            deep = width if j == 0 else width - 1
            layers = {-1: (HALO, deep, HALO + BX), 1: (HALO + BX - deep, deep, HALO - deep), 0: (HALO, BX, HALO)}[i]
            rows = {-1: (top, HALO, top + BY), 1: (top + BY - HALO, HALO, top - HALO), 0: (top, BY, top)}[j]
            sends = (bx + i >= 0) & (bx + i < NB) & (gx + j >= 0) & (gx + j < NXB)
            takes = (bx - i >= 0) & (bx - i < NB) & (gx - j >= 0) & (gx - j < NXB)
            to = device(lax.rem(bx + i + NB, NB), lax.rem(gx + j + NXB, NXB), mine)
            if i != 0 and j != 0:
                joint = even if i == 1 else jnp.logical_not(even)
                sends = sends & jnp.logical_not(joint)
                gives = joint & (gx - j >= 0) & (gx - j < NXB)
                passed.append((gives, remote(
                    ref.at[:, pl.ds(layers[0], layers[1]), pl.ds(rows[2], rows[1])],
                    ref.at[:, pl.ds(layers[2], layers[1]), pl.ds(rows[2], rows[1])],
                    hsend.at[which, side], hrecv.at[which, side],
                    {"space": device(lax.rem(bx + i + NB, NB), gx, mine)},
                )))
            copies.append((i == 0, sends, takes, remote(
                ref.at[:, pl.ds(layers[0], layers[1]), pl.ds(rows[0], rows[1])],
                ref.at[:, pl.ds(layers[2], layers[1]), pl.ds(rows[2], rows[1])],
                hsend.at[which, side], hrecv.at[which, side], {"space": to},
            )))
        return copies, passed

    def halo_start(ref, top, which):
        for _, sends, _, copy in halo(ref, top, which)[0]:
            pl.when(sends)(copy.start)

    def halo_wait(ref, top, which):
        copies, passed = halo(ref, top, which)
        for along_rows, _, takes, copy in copies:
            if along_rows:
                pl.when(takes)(copy.wait_recv)
        for gives, copy in passed:
            pl.when(gives)(copy.start)
        for along_rows, sends, takes, copy in copies:
            if not along_rows:
                pl.when(takes)(copy.wait_recv)
            pl.when(sends)(copy.wait_send)
        for gives, copy in passed:
            pl.when(gives)(copy.wait_send)

    def over_x(body, unroll=1):
        def at(x, carry):
            body(x)
            return carry

        lax.fori_loop(0, BX, at, 0, unroll=unroll)

    def neighbour_sums(ref, x, top, rows):
        c0 = ref[0, x, top : top + rows]
        c1 = ref[1, x, top : top + rows]
        lane = lax.broadcasted_iota(jnp.int32, (rows, LANES), 1)
        z0 = c1 + jnp.where(lane == 0, 0.0, pltpu.roll(c1, 1, 1))
        z1 = c0 + jnp.where(lane == LANES - 1, 0.0, pltpu.roll(c0, LANES - 1, 1))
        sums = []
        for half, z in ((0, z0), (1, z1)):
            total = ref[half, x + 1, top : top + rows] + ref[half, x - 1, top : top + rows]
            total = total + ref[half, x, top + 1 : top + rows + 1] + ref[half, x, top - 1 : top + rows - 1]
            sums.append(total + z)
        return sums

    def sweeps(first, last, body, closing):
        source = first
        for s in range(1, last + 1):
            goal = va if s % 2 else vb
            if s == HALO:
                def one(x, carry, source=source):
                    closing(x, neighbour_sums(source, x, VTOP, BY))
                    return carry
            else:
                def one(x, carry, source=source, goal=goal):
                    sums = neighbour_sums(source, x, PAD, EY)
                    for half in range(2):
                        goal[half, x, PAD : PAD + EY] = body(half, x, sums[half])
                    return carry
            lax.fori_loop(s, EX - s, one, 0, unroll=UNROLL)
            source = goal

    def depth_of(sign, k):
        z = dip[sign : sign + 1, pl.ds(pl.multiple_of(k * CHUNK, CHUNK), CHUNK)] & 255
        return lax.broadcasted_iota(jnp.int32, (2 * LANES, CHUNK), 0) == (z & 1) * LANES + (z >> 1)

    def mark_rows(k):
        for sign in range(2):
            cells = dip[sign : sign + 1, pl.ds(pl.multiple_of(k * CHUNK, CHUNK), CHUNK)]
            x, y = cells >> 15, (cells >> 8) & 127
            own = ((x >> 4) == bx) & ((y >> 5) == gx)
            row = jnp.where(own, (x & 15) * BY + (y & 31), -1)
            hot = lax.broadcasted_iota(jnp.int32, (ROWS, CHUNK), 0) == row
            hots[sign, k] = jnp.where(hot, 1.0, 0.0).astype(BF16)

    def potential(n, half):
        if n == NSTEPS - 1:
            return ulast[half]
        return entry[n + 1, half, HALO : HALO + BX, VTOP : VTOP + BY]

    def gather_table(n):
        for half in range(2):
            rows = potential(n, half).reshape(ROWS, LANES).T
            high = rows.astype(BF16)
            ut[half * LANES : (half + 1) * LANES, :] = high
            ut[(2 + half) * LANES : (3 + half) * LANES, :] = (rows - high.astype(F32)).astype(BF16)

    def gather_part(n, h):
        def at(k, carry):
            found = []
            for sign in range(2):
                both = jnp.dot(ut[...], hots[sign, k], preferred_element_type=F32)
                value = both[: 2 * LANES] + both[2 * LANES :]
                found.append(jnp.sum(jnp.where(depth_of(sign, k), value, 0.0), axis=0, keepdims=True))
            part[n, :, pl.ds(pl.multiple_of(k * CHUNK, CHUNK), CHUNK)] = found[0] - found[1]
            return carry

        lax.fori_loop(h * HALF_CHUNKS, (h + 1) * HALF_CHUNKS, at, 0)

    def gather(n):
        gather_table(n)
        for h in range(2):
            gather_part(n, h)

    def scatter(n, h):
        if h == 0:
            acc[n - 1] = jnp.zeros((ROWS, 4 * LANES), F32)

        def at(k, carry):
            value = res[n, :, pl.ds(pl.multiple_of(k * CHUNK, CHUNK), CHUNK)]
            for sign in range(2):
                placed = jnp.where(depth_of(sign, k), value if sign == 0 else -value, 0.0)
                high = placed.astype(BF16)
                low = (placed - high.astype(F32)).astype(BF16)
                acc[n - 1] += lax.dot_general(
                    hots[sign, k], jnp.concatenate([high, low], axis=0), (((1,), (1,)), ((), ())), preferred_element_type=F32
                )
            return carry

        lax.fori_loop(h * HALF_CHUNKS, (h + 1) * HALF_CHUNKS, at, 0)

    def injected(n, half, x):
        rows = pl.ds(pl.multiple_of(x * BY, BY), BY)
        return (
            acc[n - 1, rows, half * LANES : (half + 1) * LANES]
            + acc[n - 1, rows, (2 + half) * LANES : (3 + half) * LANES]
        )

    def span(h):
        return pl.ds(h * HALF, HALF)

    def row_copy(n, h, p):
        to = lax.rem(gx + p, NXB)
        return remote(
            part.at[n, :, span(h)], prx.at[gx, n, :, span(h)], psend.at[0, n, h, to], precv.at[0, n, h, gx],
            {"space": device(bx, to, mine)},
        )

    def row_wait(n, h, p):
        of = lax.rem(gx + p, NXB)
        here = prx.at[of, n, :, span(h)]
        remote(
            here, here, psend.at[0, n, h, of], precv.at[0, n, h, of], {"space": device(bx, of, mine)}
        ).wait_recv()

    def row_copies(n, h):
        over(4, lambda p: row_copy(n, h, p).start(), 1)
        prx[gx, n, :, span(h)] = part[n, :, span(h)]

    def col_copy(n, h, p):
        to = lax.rem(bx + p, NB)
        return remote(
            rows.at[n, :, span(h)], pry.at[bx, n, :, span(h)], psend.at[1, n, h, to], precv.at[1, n, h, bx],
            {"space": device(to, gx, mine)},
        )

    def col_wait(n, h, p):
        of = lax.rem(bx + p, NB)
        here = pry.at[of, n, :, span(h)]
        remote(
            here, here, psend.at[1, n, h, of], precv.at[1, n, h, of], {"space": device(of, gx, mine)}
        ).wait_recv()

    def row_sums(n, h):
        over(4, functools.partial(row_wait, n, h), 1)
        at = (n, slice(None), span(h))
        rows[at] = (prx[(0,) + at] + prx[(1,) + at]) + (prx[(2,) + at] + prx[(3,) + at])
        over(4, lambda p: col_copy(n, h, p).start(), 1)
        pry[(bx,) + at] = rows[at]

    def residual(n, h):
        over(4, functools.partial(col_wait, n, h), 1)
        at = (n, slice(None), span(h))
        alive = live[:, span(h)]
        value = alive * ((pry[(0,) + at] + pry[(1,) + at]) + (pry[(2,) + at] + pry[(3,) + at]))
        volts[at] = value
        res[at] = alive * (value - obs_all[at])

    def back_copy(f, p):
        j = lax.rem(p + slot, SLOTS)
        layers = pl.ds(HALO + 2 * j, 2)
        if f in (POT0, POT1):
            here = entry.at[f + 1, :, layers, pl.ds(VTOP, BY)]
        else:
            here = adj.at[DUAL1 - f, :, layers, pl.ds(HALO, BY)]
        to = bx * SLOTS + j
        return to, remote(here, rx.at[f, gx, mine], gsend.at[f, j], grecv.at[f, 2 * gx + mine], {"space": to})

    def send_back(f):
        begin(f, back_copy)

        def keep():
            layers = pl.ds(HALO + 2 * slot, 2)
            if f in (POT0, POT1):
                rx[f, gx, mine] = entry[f + 1, :, layers, VTOP : VTOP + BY]
            else:
                rx[f, gx, mine] = adj[DUAL1 - f, :, layers, HALO : HALO + BY]

        pl.when(bx == yp)(keep)

    def back_wait(f, q):
        x, t = q // 2, lax.rem(q, 2)
        of = device(yp, x, t)
        here = rx.at[f, x, t]
        copy = remote(here, here, gsend.at[f, q], grecv.at[f, q], {"space": of})
        pl.when(of != space)(copy.wait_recv)

    spread_static(COND)
    for load in loads[3:]:
        load.wait()
    pieces(later_fields)
    over(NDIP // CHUNK, mark_rows)
    take_field(U0)
    halo_start(entry.at[0], VTOP, 0)
    take_static(COND)

    def inverse(x):
        for half in range(2):
            inv[half, HALO + x, HALO : HALO + BY] = 1.0 / (6.0 + static(COND, half, x))

    over_x(inverse)
    halo_start(inv, HALO, 8)
    take_field(R0)
    halo_start(rhs.at[0], HALO, 5)
    send_static(F1)
    halo_wait(entry.at[0], VTOP, 0)
    halo_wait(inv, HALO, 8)
    halo_wait(rhs.at[0], HALO, 5)
    send_field(R1)
    send_static(F2)
    spread_static(F1)

    def block_of(k, half, x):
        return entry[k, half, HALO + x, VTOP : VTOP + BY]

    def forward(n):
        def body(half, x, total):
            return (rhs[n, half, x] + total) * inv[half, x]

        def closing(x, sums):
            for half in range(2):
                made = (rhs[n, half, x, HALO : HALO + BY] + sums[half]) * inv[half, x, HALO : HALO + BY]
                if n == NSTEPS - 1:
                    ulast[half, x - HALO] = made
                else:
                    entry[n + 1, half, x, VTOP : VTOP + BY] = made

        sweeps(entry.at[n], JACOBI, body, closing)

    forward(0)
    halo_start(entry.at[1], VTOP, 1)
    take_static(F1)
    take_field(R1)

    def step_one(x):
        for half in range(2):
            rhs[1, half, HALO + x, HALO : HALO + BY] = (
                blk[0, half, x] + static(F1, half, x) * block_of(1, half, x)
            )

    over_x(step_one)
    halo_start(rhs.at[1], HALO, 6)
    spread_static(F2)
    obs_pair_in.wait_recv()
    over(SLOTS, lambda p: obs_copy(p, 0).start(), 1)
    over(SLOTS, lambda p: obs_copy(p, 1).start(), 1)
    gather(0)
    for h in range(2):
        row_copies(0, h)
    halo_wait(entry.at[1], VTOP, 1)
    halo_wait(rhs.at[1], HALO, 6)
    send_field(R2)
    forward(1)
    halo_start(entry.at[2], VTOP, 2)
    take_static(F2)
    take_field(R2)

    def step_two(x):
        for half in range(2):
            rhs[2, half, HALO + x, HALO : HALO + BY] = (
                blk[1, half, x]
                + static(F2, half, x) * block_of(1, half, x)
                + static(F1, half, x) * block_of(2, half, x)
            )

    over_x(step_two)
    halo_start(rhs.at[2], HALO, 7)
    over(SLOTS, lambda p: obs_wait(p, 0), 1)
    over(SLOTS, lambda p: obs_wait(p, 1), 1)
    obs_rows(True).start()
    gather(1)
    for h in range(2):
        row_copies(1, h)
        row_sums(0, h)
    halo_wait(entry.at[2], VTOP, 2)
    halo_wait(rhs.at[2], HALO, 7)
    send_back(POT0)
    forward(2)

    gather_table(2)
    gather_part(2, 0)
    row_copies(2, 0)
    gather_part(2, 1)
    row_copies(2, 1)
    obs_rows(False).wait_recv()
    row_sums(2, 0)
    row_sums(2, 1)
    for h in range(2):
        row_sums(1, h)

    def begin_adjoint(n):
        def body(x):
            for half in range(2):
                field = injected(n, half, x)
                if n == 1:
                    field = field + back[half, x] + static(F1, half, x) * adj[1, half, HALO + x, HALO : HALO + BY]
                scaled = field * inv[half, HALO + x, HALO : HALO + BY]
                adj[n - 1, half, HALO + x, HALO : HALO + BY] = scaled
                entry[5 - n, half, HALO + x, VTOP : VTOP + BY] = scaled

        over_x(body)

    def adjoint(n):
        def body(half, x, total):
            scaled = total * inv[half, x]
            adj[n - 1, half, x] += scaled
            return scaled

        def closing(x, sums):
            for half in range(2):
                back[half, x - HALO] = sums[half]

        sweeps(entry.at[5 - n], JACOBI if n == 2 else JACOBI - 1, body, closing)

    for h in range(2):
        residual(2, h)
        scatter(2, h)
    begin_adjoint(2)
    halo_start(entry.at[3], VTOP, 3)
    for h in range(2):
        residual(1, h)
        scatter(1, h)
        residual(0, h)

    squares = jnp.zeros((1, NDIP), F32)
    for n in range(NSTEPS):
        squares = squares + res[n] * res[n]

    own = pl.ds(pl.multiple_of(space * LANES, LANES), LANES)
    other = pl.ds(pl.multiple_of(partner * LANES, LANES), LANES)
    swap = remote(volts.at[:, :, other], vswap.at[pl.ds(6, 3)], qsend.at[2], qrecv.at[2], {"space": partner})
    swap.start()
    lanes = squares[:, 0:LANES]
    for j in range(1, NDIP // LANES):
        lanes = lanes + squares[:, j * LANES : (j + 1) * LANES]
    sq[...] = lanes
    pair = remote(sq, sqc, qsend.at[3], qrecv.at[3], {"space": partner})
    pair.start()
    for n in range(NSTEPS):
        volts_out[n, pl.ds(mine, 1), :] = volts[n, :, own]
    swap.wait()
    for n in range(NSTEPS):
        volts_out[n, pl.ds(1 - mine, 1), :] = vswap[6 + n]
    pair.wait()
    sqz[tx] = sq[...] + sqc[...]

    def sq_copy(p):
        to = lax.rem(tx + p, 4)
        return remote(sqz.at[tx], sqz.at[tx], tsend.at[2, to], trecv.at[2, tx], {"tx": to})

    def sq_wait(p):
        of = lax.rem(tx + p, 4)
        remote(sqz.at[of], sqz.at[of], tsend.at[2, of], trecv.at[2, of], {"tx": of}).wait_recv()

    over(4, lambda p: sq_copy(p).start(), 1)

    halo_wait(entry.at[3], VTOP, 3)
    send_back(POT1)
    adjoint(2)
    begin_adjoint(1)
    halo_start(entry.at[4], VTOP, 4)
    halo_wait(entry.at[4], VTOP, 4)
    send_back(DUAL2)
    adjoint(1)
    send_back(DUAL1)

    over(4, sq_wait, 1)
    total = (sqz[0] + sqz[1]) + (sqz[2] + sqz[3])
    misfit = jnp.sqrt(1.0 + jnp.sum(total, axis=1, keepdims=True))
    misfit_out[...] = misfit
    scale = 1.0 / misfit
    for f in (POT0, POT1, DUAL2):
        over(SLOTS, functools.partial(back_wait, f))

    def tx_copy(f, to):
        return remote(rsum.at[f, to], rz.at[f, tx], tsend.at[f, to], trecv.at[f, tx], {"tx": to})

    def tx_wait(f, p):
        of = lax.rem(tx + p, 4)
        remote(rsum.at[f, of], rz.at[f, of], tsend.at[f, of], trecv.at[f, of], {"tx": of}).wait_recv()

    def gradients(i):
        x = lax.rem(gx + i, NXB)
        for t in range(2):
            back_wait(DUAL1, 2 * x + t)
        for half in range(2):
            for layer in range(2):
                at = (half, layer)
                same, cross, tilt = (jnp.zeros((BY, LANES), F32) for _ in range(3))
                for t in range(2):
                    u0, u1, s2, s1 = (rx[(f, x, t) + at] for f in range(4))
                    same = same + (s2 * u1 + s1 * u0)
                    cross = cross + s2 * u0
                    tilt = tilt + (s1 * tilts[(0, t, x) + at] + s2 * tilts[(1, t, x) + at])
                ka0, ka1, kb0, kb1 = (factors[(f, x) + at] for f in range(4))
                rsum[(0, x) + at] = ka0 * same + ka1 * cross
                rsum[(1, x) + at] = tilt - kb0 * same + kb1 * cross

        def give():
            for f in range(2):
                tx_copy(f, x).start()

        def keep():
            for f in range(2):
                rz[f, tx] = rsum[f, x]

        pl.when(x != tx)(give)
        pl.when(x == tx)(keep)

    over(NXB, gradients)
    for f, out in ((0, gc_out), (1, gt_out)):
        over(4, functools.partial(tx_wait, f), 1)
        halves = [(rz[f, 0, half] + rz[f, 1, half]) + (rz[f, 2, half] + rz[f, 3, half]) for half in range(2)]
        value = reorder(jnp.concatenate([half.reshape(2 * BY, LANES) for half in halves], axis=1), 1)
        out[...] = value.reshape(2, BY, 2 * LANES) * scale.reshape(1, 1, 1)

    for f in range(4):
        finish(f, field_copy)
    for f in range(3):
        finish(f, static_copy)
        over(4, lambda p: spread_copy(f, p).wait_send(), 1)
    obs_pair.wait_send()
    for which in range(2):
        over(SLOTS, lambda p: obs_copy(p, which).wait_send(), 1)
    obs_rows(True).wait_send()
    for n in range(NSTEPS):
        for h in range(2):
            over(4, lambda p: row_copy(n, h, p).wait_send(), 1)
            over(4, lambda p: col_copy(n, h, p).wait_send(), 1)
    over(4, lambda p: sq_copy(p).wait_send(), 1)
    for f in range(4):
        finish(f, back_copy)
    for f in range(2):
        over(4, lambda p: tx_copy(f, lax.rem(tx + p, 4)).wait_send(), 1)


def hand_over(*refs):
    given, made, sems = refs[:4], refs[4:8], refs[8]
    copies = [pltpu.make_async_copy(a, b, sems.at[i]) for i, (a, b) in enumerate(zip(given, made))]
    for copy in copies:
        copy.start()
    for copy in copies:
        copy.wait()


def on_device(cond, chg, rlx, start, mem, src_cells, dip, counts, obs):
    vmem = pl.BlockSpec(memory_space=pltpu.VMEM)
    whole = pl.BlockSpec(memory_space=pl.ANY)
    smem = pl.BlockSpec(memory_space=pltpu.SMEM)
    field = pltpu.VMEM((2, BX, BY, LANES), F32)
    dma = pltpu.SemaphoreType.DMA
    wide = pltpu.VMEM((2, EX, EY + 2 * PAD, LANES), F32)
    slab = pltpu.VMEM((2, 128, 2 * LANES), F32)
    scratch = [
        slab, slab, slab,
        pltpu.VMEM((2, 2, 128, 2 * LANES), F32),
        pltpu.VMEM((4, 2, 2, 128, 2 * LANES), F32),
        pltpu.VMEM((2 * LANES, 2 * LANES), BF16),
        pltpu.VMEM((2, NDIP // CHUNK, ROWS, CHUNK), BF16),
        pltpu.VMEM((4, 2, NXB, 2, 2, BY, LANES), F32),
        pltpu.VMEM((3, NXB, 2, 2, BY, LANES), F32),
        pltpu.VMEM((2, 2, NXB, 2, 2, BY, LANES), F32),
        pltpu.VMEM((4, NXB, 2, 2, BY, LANES), F32),
        pltpu.VMEM((2, 2, BX, BY, LANES), F32),
        pltpu.VMEM((3, 2, 2, BX // 2, BY, LANES), F32),
        pltpu.VMEM((5, 2, EX, EY + 2 * PAD, LANES), F32),
        wide, wide,
        pltpu.VMEM((2, EX, EY, LANES), F32),
        pltpu.VMEM((NSTEPS, 2, EX, EY, LANES), F32),
        field,
        pltpu.VMEM((2, 2, EX, EY, LANES), F32),
        field,
        pltpu.VMEM((4 * LANES, ROWS), BF16),
        pltpu.VMEM((2, ROWS, 4 * LANES), F32),
        pltpu.VMEM((NSTEPS, 1, NDIP), F32),
        pltpu.VMEM((NXB, NSTEPS, 1, NDIP), F32),
        pltpu.VMEM((NB, NSTEPS, 1, NDIP), F32),
        pltpu.VMEM((NSTEPS, 1, NDIP), F32),
        pltpu.VMEM((NSTEPS, 1, NDIP), F32),
        pltpu.VMEM((NSTEPS, 1, NDIP), F32),
        pltpu.VMEM((NSTEPS, 1, NDIP), F32),
        pltpu.VMEM((1, NDIP), F32),
        pltpu.VMEM((9, 1, LANES), F32),
        pltpu.VMEM((1, LANES), F32),
        pltpu.VMEM((1, LANES), F32),
        pltpu.VMEM((4, 1, LANES), F32),
        pltpu.VMEM((4, NXB, 2, 2, 2, BY, LANES), F32),
        pltpu.VMEM((2, NXB, 2, 2, BY, LANES), F32),
        pltpu.VMEM((2, 4, 2, 2, BY, LANES), F32),
        dma((5,)),
        dma((4, SLOTS)), dma((4, SLOTS)), dma((3, SLOTS)), dma((3, SLOTS)),
        dma((3, 4)), dma((3, 4)),
        dma((9, 8)), dma((9, 8)),
        dma((2, SLOTS)), dma((2, SLOTS)),
        dma((2, NSTEPS, 2, 4)), dma((2, NSTEPS, 2, 4)),
        dma((4,)), dma((4,)),
        dma((4, SLOTS)), dma((4, SLOTS)),
        dma((3, 4)), dma((3, 4)),
    ]
    volts, misfit, grad_c, grad_t = pl.pallas_call(
        kernel,
        out_shape=(
            jax.ShapeDtypeStruct((NSTEPS, 2, LANES), F32),
            jax.ShapeDtypeStruct((1, 1), F32),
            jax.ShapeDtypeStruct((2, BY, 2 * LANES), F32),
            jax.ShapeDtypeStruct((2, BY, 2 * LANES), F32),
        ),
        in_specs=[whole, whole, whole, whole, whole, smem, vmem, smem, vmem],
        out_specs=(vmem, vmem, vmem, vmem),
        scratch_shapes=scratch,
        compiler_params=pltpu.CompilerParams(has_side_effects=True, collective_id=0, vmem_limit_bytes=60 << 20),
    )(cond, chg, rlx, start, mem, src_cells, dip, counts, obs)
    results = (volts, misfit, grad_c, grad_t)
    volts, misfit, grad_c, grad_t = pl.pallas_call(
        hand_over,
        out_shape=tuple(jax.ShapeDtypeStruct(a.shape, F32) for a in results),
        in_specs=[whole] * 4,
        out_specs=(whole,) * 4,
        scratch_shapes=[dma((4,))],
    )(*results)
    return (volts, misfit.reshape(()), grad_c, grad_t)


def solution(mesh):
    placed = (
        P("space", None, None),
        P("space", None, None),
        P("space", None, None),
        P("tx", "space", None, None),
        P(None, "tx", "space", None, None),
        P(None, "tx"),
        P(),
        P(),
        P(None, "tx", "space"),
    )
    return jax.shard_map(
        on_device,
        mesh=mesh,
        in_specs=placed,
        out_specs=(P(None, "tx", "space"), P(), P("space", "tx", None), P("space", "tx", None)),
        check_vma=False,
    )
```
